32 devices in a mesh: dp: 8 (over y, x, core), mp: 4 (over z).
Axes of the slice: x: 2, y: 2, z: 4, core: 2. Of those that a mesh axis runs over, the one named last changes fastest.
Arguments:
- inputs: bfloat16 [8, 1024, 1024], P('dp', 'mp')
- segments: int32 [8, 1024], P('dp'), may hold values from 0 to 5, never falling along the last dimension, each value on 1 to 512 neighbouring positions
- positions: int32 [8, 1024], P('dp'), may hold values from 0 to 1279, as said below
- boxes: int32 [2, 8, 1024], P(None, 'dp'), may hold values from 0 to 255
- pad_mask: int32 [8, 1024], P('dp'), may hold values from 0 to 1, as said below
- w_qkv: bfloat16 [3, 1024, 1024], P(None, 'dp', 'mp'), may hold values from -0.09375 to 0.09375
- w_out: bfloat16 [1024, 1024], P('mp', 'dp'), may hold values from -3 to 3
- w_gate_up: bfloat16 [2, 1024, 2816], P(None, 'dp', 'mp'), may hold values from -0.1875 to 0.1875
- w_down: bfloat16 [2816, 1024], P('mp', 'dp'), may hold values from -0.109375 to 0.109375
- bias_tables: bfloat16 [3, 32, 16], P(None, None, 'mp'), may hold values from -4 to 4
- gains: bfloat16 [2, 1024], replicated, may hold values from 0.25 to 1.75
- out_grad: bfloat16 [8, 1024, 1024], P('dp', 'mp'), may hold values from -6 to 6
Outputs:
- out: bfloat16 [8, 1024, 1024], P('dp', 'mp')
- input_grad: bfloat16 [8, 1024, 1024], P('dp', 'mp')
- w_qkv_grad: float32 [3, 1024, 1024], P(None, 'dp', 'mp')
- w_out_grad: float32 [1024, 1024], P('mp', 'dp')
- w_gate_up_grad: float32 [2, 1024, 2816], P(None, 'dp', 'mp')
- w_down_grad: float32 [2816, 1024], P('mp', 'dp')
- table_grad: float32 [3, 32, 16], P(None, 'dp', 'mp')
- gain_grad: float32 [2, 1024], P(None, ('dp', 'mp'))
The draws below stay inside these ranges and needn't reach their ends.
Inputs may be any that keep to these rules, and one draw needn't show every extreme that they name: Along each row positions start at 0 and rise by 1 or 2 from token to token; the last token of every row is at 1279. `pad_mask`: in each row the 1s form a leading run and the 0s the rest.
All inputs are finite; a program needn't handle non-finite values.
Results may differ from the reference program's by a relative error of at most 0.018.
Values may be sent and summed in bfloat16 or wider, within the bound.
No kernel may reach another device: no remote copies, remote signals or barrier semaphores. Data moves between devices by JAX's collectives and lax.ppermute only.
A program may use at most 320 MiB of HBM per device.

```python
import math
from functools import partial
import jax
import jax.numpy as jnp
import numpy as np
from jax import lax

D = 1024
HEADS = 16
FF = 2816
NB = 32
LEN = 1024
ROWS = 8


def draw_inputs(key, part):
    normal_key, row_key, column_key = jax.random.split(key, 3)
    normal_part = jax.random.normal(normal_key, (ROWS, LEN, D), jnp.float32)
    row_scale = jnp.exp(jax.random.uniform(row_key, (ROWS, LEN, 1), jnp.float32, math.log(0.3), math.log(3.0)))
    column_scale = jnp.exp(jax.random.uniform(column_key, (D,), jnp.float32, math.log(0.5), math.log(2.0)))
    return (normal_part * row_scale * column_scale).astype(jnp.bfloat16)


def draw_positions(key, part):
    row_keys = jax.random.split(key, ROWS)
    gap_order = jax.vmap(lambda one_key: jax.random.permutation(one_key, LEN - 1))(row_keys)
    gap_flags = (gap_order < LEN // 4).astype(jnp.int32)
    skipped = jnp.concatenate([jnp.zeros((ROWS, 1), jnp.int32), jnp.cumsum(gap_flags, axis=1)], axis=1)
    return jnp.arange(LEN, dtype=jnp.int32)[None, :] + skipped


def draw_pad_mask(key, part):
    tail_lengths = jax.random.randint(key, (ROWS, 1), 0, LEN // 8 + 1)
    return (jnp.arange(LEN, dtype=jnp.int32)[None, :] < LEN - tail_lengths).astype(jnp.int32)


def touch_ends(entries, own_key, low, largest):
    longest = entries.shape.index(max(entries.shape))
    spots = []
    for shift in (0, 1):
        where = [jax.random.randint(jax.random.fold_in(own_key, axis), (), 0, length) for axis, length in enumerate(entries.shape)]
        where[longest] = (where[longest] + shift) % entries.shape[longest]
        spots.append(tuple(where))
    return entries.at[spots[0]].set(low).at[spots[1]].set(largest)


def block_scale(stream_key, dims, cuts, smallest, high):
    loudness, own = 1.0, jax.random.fold_in(stream_key, 6)
    for axis_at, parts in cuts:
        draws = jnp.exp(jax.random.uniform(jax.random.fold_in(own, axis_at), (parts,), jnp.float32, smallest / len(cuts), high / len(cuts)))
        loudness = loudness * jnp.repeat(draws, dims[axis_at] // parts).reshape([-1 if axis == axis_at else 1 for axis in range(len(dims))])
    return loudness


def split_up(number_of, total, bound, skew):
    weights = [(1 << 20) // math.isqrt(standing ** skew) + 1 for standing in range(2, number_of + 1)]
    spare, given = total - bound - (number_of - 1), [1] * (number_of - 1)
    while spare > 0:
        free = [i for i in range(number_of - 1) if given[i] < bound]
        pool, remaining = sum([weights[i] for i in free]), spare
        for i in free:
            extra = min(bound - given[i], max(1, remaining * weights[i] // pool), spare)
            given[i] = given[i] + extra
            spare = spare - extra
    return np.array([bound] + given)


def ragged(rng, count, total, reach, lean):
    if count == 2:
        one = jax.random.randint(rng, (), max(1, total - reach), min(reach, total - 1) + 1)
        return jnp.stack([one, total - one])
    tallies = jnp.asarray(split_up(count, total, reach, lean), jnp.int32)
    pairs = (count - 1) // 2
    giver, receiver = tallies[1:1 + 2 * pairs:2], tallies[2:2 + 2 * pairs:2]
    slack = jnp.minimum(giver - 1, reach - receiver)
    moved = jax.random.randint(jax.random.fold_in(rng, 1), (pairs,), 0, 1 << 20) % (slack + 1)
    tallies = tallies.at[1:1 + 2 * pairs:2].set(giver - moved).at[2:2 + 2 * pairs:2].set(receiver + moved)
    return tallies[jax.random.permutation(jax.random.fold_in(rng, 2), count)]


def gaussian(own_key, extent, width, bound, shards=(), kind=jnp.bfloat16):
    gain = block_scale(own_key, extent, shards, -0.22, 0.18) if shards else 1.0
    entries = jax.random.normal(own_key, extent, jnp.float32) * width * gain
    return jnp.minimum(jnp.maximum(entries, -bound), bound).astype(kind)


def setup_inputs(seed: int = 0) -> dict:
    keys = jax.random.split(jax.random.key(seed), 13)
    inputs = draw_inputs(jax.random.fold_in(keys[12], 71), 0)
    segments = jax.vmap(lambda own: jnp.searchsorted(jnp.cumsum(ragged(own, 6, LEN, LEN // 2, 0)), jnp.arange(LEN), side="right"))(jax.random.split(keys[1], ROWS)).reshape((ROWS, LEN)).astype(jnp.int32)
    positions = draw_positions(jax.random.fold_in(keys[12], 71), 0)
    boxes = touch_ends(jax.random.randint(keys[3], (2, ROWS, LEN), 0, 256), jax.random.fold_in(keys[3], 1), 0, 255).astype(jnp.int32)
    pad_mask = draw_pad_mask(jax.random.fold_in(keys[12], 71), 0)
    w_qkv = gaussian(keys[5], (3, D, D), (4 * D) ** -0.5, 0.09375, ((1, 8), (2, 4)))
    w_out = gaussian(keys[6], (D, D), (max(4, D // 256)) ** -0.5, 3.0, ((0, 4), (1, 8)))
    w_gate_up = gaussian(keys[7], (2, D, FF), D ** -0.5, 0.1875, ((1, 8), (2, 4)))
    w_down = gaussian(keys[8], (FF, D), FF ** -0.5, 0.109375, ((0, 4), (1, 8)))
    bias_tables = gaussian(keys[9], (3, NB, HEADS), 0.7, 4.0, ((2, 4),))
    gains = jnp.clip(1.0 + 0.15 * jax.random.normal(keys[10], (2, D), jnp.float32), 0.25, 1.75).astype(jnp.bfloat16)
    out_grad = gaussian(keys[11], (ROWS, LEN, D), 1.0, 6.0, ((0, 8), (1, 4)))
    return dict(inputs=inputs, segments=segments, positions=positions, boxes=boxes, pad_mask=pad_mask, w_qkv=w_qkv, w_out=w_out, w_gate_up=w_gate_up, w_down=w_down, bias_tables=bias_tables, gains=gains, out_grad=out_grad)


epsilon = 1e-06
gelu_coefficient = 0.7978845608028654
thresholds = (12, 16, 23, 32, 46, 64, 91)
highest = lax.Precision.HIGHEST

@jax.custom_vjp
def low(v):
    return lax.optimization_barrier(v.astype(jnp.bfloat16)).astype(jnp.float32)

@jax.custom_vjp
def low_back(v):
    return v

def low_keep(v):
    return (low(v), None)

def low_pass(kept, grad):
    return (grad,)

def back_keep(v):
    return (v, None)

def back_low(kept, grad):
    return (low(grad),)
low.defvjp(low_keep, low_pass)
low_back.defvjp(back_keep, back_low)

def bucket_of(distance):
    magnitude = jnp.abs(distance)
    stepped = 8 + sum(((magnitude >= boundary).astype(jnp.int32) for boundary in thresholds))
    return jnp.where(magnitude < 8, magnitude, stepped) + 16 * (distance > 0).astype(jnp.int32)

def rms_scale(row_values, gain_row):
    return row_values * lax.rsqrt(lax.optimization_barrier(jnp.mean(row_values * row_values, axis=-1, keepdims=True)) + epsilon) * gain_row

def gelu_tanh(values):
    return 0.5 * values * (1.0 + jnp.tanh(gelu_coefficient * (values + 0.044715 * values * values * values)))

def row_attention(tables, row_items):
    queries, key_rows, values, segment, position, across, downward, padding = row_items
    length = queries.shape[0]
    head_count = tables.shape[2]
    head_dim = queries.shape[1] // head_count
    rel_kind = bucket_of(position[None, :] - position[:, None])
    hor_kind = bucket_of(across[None, :] - across[:, None])
    ver_kind = bucket_of(downward[None, :] - downward[:, None])
    table_terms = tables[0][rel_kind] + tables[1][hor_kind] + tables[2][ver_kind]
    bias_terms = jnp.moveaxis(table_terms, 2, 0)
    index_rows = lax.broadcasted_iota(jnp.int32, (length, length), 0)
    index_cols = lax.broadcasted_iota(jnp.int32, (length, length), 1)
    allowed = (segment[:, None] == segment[None, :]) & ((padding[None, :] == 1) | (index_rows == index_cols))
    raw_scores = jnp.einsum('qhe,khe->hqk', queries.reshape(length, head_count, head_dim), key_rows.reshape(length, head_count, head_dim), precision=highest)
    scores = low_back(raw_scores + bias_terms)
    probabilities = jax.nn.softmax(jnp.where(allowed[None], scores, -1e+30), axis=-1)
    mixed_rows = jnp.einsum('hqk,khe->qhe', low(probabilities), values.reshape(length, head_count, head_dim), precision=highest)
    return mixed_rows.reshape(length, -1)

def reference(inputs, segments, positions, boxes, pad_mask, w_qkv, w_out, w_gate_up, w_down, bias_tables, gains, out_grad):
    labels = (segments, positions, boxes[0], boxes[1], pad_mask)

    def forward(input_rows, qkv_weight, out_weight, gate_up_weight, down_weight, tables, gain_rows):
        normed_one = low(rms_scale(input_rows, gain_rows[0]))
        projected = low_back(low(jnp.einsum('rld,cdm->crlm', normed_one, qkv_weight, precision=highest)))
        attend = jax.checkpoint(partial(row_attention, tables))
        mixed_output = lax.map(attend, (projected[0], projected[1], projected[2]) + labels)
        mixed_output = low_back(low(mixed_output))
        attn = low_back(jnp.einsum('rlm,md->rld', mixed_output, out_weight, precision=highest))
        middle = input_rows + attn
        normed_two = low(rms_scale(middle, gain_rows[1]))
        gate_up = low_back(jnp.einsum('rld,cdf->crlf', normed_two, gate_up_weight, precision=highest))
        hidden_state = low(gelu_tanh(gate_up[0]) * gate_up[1])
        return middle + low_back(jnp.einsum('rlf,fd->rld', hidden_state, down_weight, precision=highest))
    primals = (inputs.astype(jnp.float32), w_qkv.astype(jnp.float32), w_out.astype(jnp.float32), w_gate_up.astype(jnp.float32), w_down.astype(jnp.float32), bias_tables.astype(jnp.float32), gains.astype(jnp.float32))
    result, pullback = jax.vjp(forward, *primals)
    gradients = pullback(out_grad.astype(jnp.float32))
    return (result.astype(jnp.bfloat16), gradients[0].astype(jnp.bfloat16), gradients[1], gradients[2], gradients[3], gradients[4], gradients[5], gradients[6])
```

```python
import functools
import jax
import jax.numpy as jnp
from jax import lax
from jax.experimental import pallas as pl
from jax.experimental.pallas import tpu as pltpu
from jax.sharding import PartitionSpec as P

NB = 32
thresholds = (12, 16, 23, 32, 46, 64, 91)
BQ = 256
NEG = -1e30
bf16 = jnp.bfloat16
f32 = jnp.float32


def bucket_of(distance):
    magnitude = jnp.abs(distance)
    stepped = 8 + sum(((magnitude >= boundary).astype(jnp.int32) for boundary in thresholds))
    return jnp.where(magnitude < 8, magnitude, stepped) + 16 * (distance > 0).astype(jnp.int32)


def iota(shape, axis):
    return lax.broadcasted_iota(jnp.int32, shape, axis)


def to_bf16(mask):
    return jnp.where(mask, 1.0, 0.0).astype(bf16)


def key_features(labc, tab, k, feats, heads):
    length = labc.shape[0]
    for kind in (0, 1):
        chosen = to_bf16(iota((length, 256), 1) == labc[:, 2 + kind : 3 + kind])
        where_bucket = bucket_of(iota((256, 256), 0) - iota((256, 256), 1))
        for h in range(heads):
            row = tab[(1 + kind) * heads + h : (1 + kind) * heads + h + 1, :]
            wide = jnp.broadcast_to(row, (256, 128))
            toep = jnp.concatenate(
                [
                    jnp.take_along_axis(wide, where_bucket[:, c : c + 128], axis=1)
                    for c in (0, 128)
                ],
                axis=1,
            ).astype(bf16)
            feats[h, :, kind * 256 : kind * 256 + 256] = jnp.dot(
                chosen, toep, preferred_element_type=f32
            ).astype(bf16)
    lane = iota((length, 64), 1)
    mask = jnp.where(
        lane < 8,
        jnp.where(labc[:, 0:1] == lane, 0.0, NEG),
        jnp.where((lane == 8) & (labc[:, 4:5] != 1), NEG, 0.0),
    ).astype(bf16)
    for h in range(heads):
        feats[h, :, 512:576] = k[:, h * 64 : h * 64 + 64]
        feats[h, :, 576:640] = mask


def query_features(labr, first, a):
    def of(row):
        return labr[row : row + 1, pl.ds(first, BQ)]

    sub = iota((256, BQ), 0)
    a[0:256, :] = to_bf16(sub == of(2))
    a[256:512, :] = to_bf16(sub == of(3))
    low = iota((64, BQ), 0)
    a[576:640, :] = jnp.where(
        low < 8, jnp.where(of(0) == low, 1.0, 0.0), jnp.where(low == 8, 1.0, 0.0)
    ).astype(bf16)


def near_buckets(labr, labc, qb, idx, tiles):
    first = pl.multiple_of(qb * BQ, BQ)
    here = labr[1:2, pl.ds(first, BQ)]
    for n in range(4):
        t = 2 * qb - 1 + n

        @pl.when((t >= 0) & (t < tiles))
        def _():
            there = labc[pl.ds(pl.multiple_of(t * 128, 128), 128), 1:2]
            idx[n * 128 : n * 128 + 128, :] = bucket_of(there - here)


def add_near(s_ref, tab, idx, labr, qb, h, own, tiles):
    first = pl.multiple_of(qb * BQ, BQ)
    wide = jnp.broadcast_to(tab[h : h + 1, :], (128, 128))
    padded = labr[4:5, pl.ds(first, BQ)] != 1
    for n in range(4):
        t = 2 * qb - 1 + n

        @pl.when((t >= 0) & (t < tiles))
        def _():
            rows = pl.ds(pl.multiple_of(t * 128, 128), 128)
            got = jnp.concatenate(
                [
                    jnp.take_along_axis(wide, idx[n * 128 : n * 128 + 128, c : c + 128], axis=1)
                    for c in range(0, BQ, 128)
                ],
                axis=1,
            )
            s = s_ref[rows, :] + got
            if n in (1, 2):
                same = iota((128, BQ), 0) + (n - 1) * 128 == iota((128, BQ), 1)
                s = jnp.where(same & padded, own, s)
            s_ref[rows, :] = s


def own_scores(qt, k_block, tab, heads):
    kt = k_block.T.astype(f32)
    prod = qt.astype(f32) * kt
    out = []
    for h in range(heads):
        zero_bias = tab[h, 0] + tab[heads + h, 0] + tab[2 * heads + h, 0]
        out.append(jnp.sum(prod[h * 64 : h * 64 + 64], axis=0, keepdims=True) + zero_bias)
    return out


def far_constant(far, qb, t, h):
    return jnp.where(t < 2 * qb - 1, far[0, h], jnp.where(t > 2 * qb + 2, far[1, h], 0.0))


def rows_max(value):
    return functools.reduce(jnp.maximum, [value[i : i + 8] for i in range(0, value.shape[0], 8)])


def rows_sum(value):
    return functools.reduce(jnp.add, [value[i : i + 8] for i in range(0, value.shape[0], 8)])


def fwd_kernel(heads, far, labr, labc, tab, q, k, v, mixed, ot, lse, feats, a, s_ref, p_ref, vt, idx):
    labr, labc, q, k, v = labr.at[0], labc.at[0], q.at[0], k.at[0], v.at[0]
    mixed, ot, lse = mixed.at[0], ot.at[0], lse.at[0]
    length = labc.shape[0]
    tiles = length // 128
    qb = pl.program_id(1)
    first = pl.multiple_of(qb * BQ, BQ)

    @pl.when(qb == 0)
    def _():
        key_features(labc, tab, k, feats, heads)
        vt[...] = v[...].T

    query_features(labr, first, a)
    near_buckets(labr, labc, qb, idx, tiles)
    qt = q[...].T
    own = own_scores(qt, k[pl.ds(first, BQ), :], tab, heads)
    outs = []
    for h in range(heads):
        a[512:576, :] = qt[h * 64 : h * 64 + 64]
        s_ref[...] = jnp.dot(feats[h], a[...], preferred_element_type=f32)
        add_near(s_ref, tab, idx, labr, qb, h, own[h], tiles)
        top = None
        for t in range(tiles):
            here = rows_max(s_ref[t * 128 : t * 128 + 128, :]) + far_constant(far, qb, t, h)
            top = here if top is None else jnp.maximum(top, here)
        top = jnp.max(top, axis=0, keepdims=True)
        total = jnp.zeros((8, BQ), f32)
        for t in range(tiles):
            shift = top - far_constant(far, qb, t, h)
            p = jnp.exp(s_ref[t * 128 : t * 128 + 128, :] - shift)
            total = total + rows_sum(p)
            p_ref[t * 128 : t * 128 + 128, :] = p.astype(bf16)
        total = jnp.sum(total, axis=0, keepdims=True)
        o = jnp.dot(vt[h * 64 : h * 64 + 64, :], p_ref[...], preferred_element_type=f32)
        o = o * (1.0 / total)
        ot[h * 64 : h * 64 + 64, :] = o
        lse[h : h + 1, :] = top + jnp.log(total)
        outs.append(o)
    mixed[...] = jnp.concatenate(outs, axis=0).T.astype(bf16)


def bwd_kernel(
    heads, far, labr, labc, tab, spread, q, k, v, go, ot, lse,
    dqkv, tg,
    feats, a, s_ref, dp_ref, pd, ends, acc, cxy, cp, sums, idx,
):
    labr, labc, q, k, v = labr.at[0], labc.at[0], q.at[0], k.at[0], v.at[0]
    go, ot, lse, dqkv, tg = go.at[0], ot.at[0], lse.at[0], dqkv.at[0], tg.at[0]
    length = labc.shape[0]
    width = heads * 64
    tiles = length // 128
    qb = pl.program_id(1)
    first = pl.multiple_of(qb * BQ, BQ)

    @pl.when(qb == 0)
    def _():
        key_features(labc, tab, k, feats, heads)
        sub = iota((256, length), 0)
        ends[0:256, :] = to_bf16(sub == labr[2:3, :])
        ends[256:512, :] = to_bf16(sub == labr[3:4, :])
        acc[...] = jnp.zeros_like(acc)
        cxy[...] = jnp.zeros_like(cxy)
        cp[...] = jnp.zeros_like(cp)
        sums[...] = jnp.zeros_like(sums)
        ends[512 : 512 + width, :] = k[...].T

    query_features(labr, first, a)
    near_buckets(labr, labc, qb, idx, tiles)
    qt = q[...].T
    own = own_scores(qt, k[pl.ds(first, BQ), :], tab, heads)
    gt = go[...].T
    delta_all = gt.astype(f32) * ot[...]
    flipped = [
        to_bf16(255 - iota((BQ, 256), 1) == labc[pl.ds(first, BQ), 2 + kind : 3 + kind])
        for kind in (0, 1)
    ]
    zeros = jnp.zeros((BQ, 64), bf16)
    dqts = []
    for h in range(heads):
        cols = slice(h * 64, h * 64 + 64)
        a[512:576, :] = qt[cols]
        s_ref[...] = jnp.dot(feats[h], a[...], preferred_element_type=f32)
        dp_ref[...] = jnp.dot(v[:, cols], gt[cols], preferred_element_type=f32)
        add_near(s_ref, tab, idx, labr, qb, h, own[h], tiles)
        delta = jnp.sum(delta_all[cols], axis=0, keepdims=True)
        low = jnp.zeros((8, BQ), f32)
        high = jnp.zeros((8, BQ), f32)
        for t in range(tiles):
            rows = slice(t * 128, t * 128 + 128)
            shift = lse[h : h + 1, :] - far_constant(far, qb, t, h)
            p = jnp.exp(s_ref[rows, :] - shift)
            ds = p * (dp_ref[rows, :] - delta)
            pd[rows, 0:BQ] = p.astype(bf16)
            pd[rows, BQ : 2 * BQ] = ds.astype(bf16)
            after = (t * 128 - qb * BQ + iota((128, BQ), 0)) > iota((128, BQ), 1)
            high = high + rows_sum(jnp.where(after, ds, 0.0))
            low = low + rows_sum(ds)
        sums[h * 16 : h * 16 + 8, :] += low - high
        sums[h * 16 + 8 : h * 16 + 16, :] += high
        right = jnp.concatenate(
            [
                jnp.concatenate([go[:, cols], zeros], axis=1),
                jnp.concatenate([zeros, q[:, cols]], axis=1),
            ],
            axis=0,
        )
        acc[h] += jnp.dot(pd[...], right, preferred_element_type=f32)
        dst = pd[:, BQ : 2 * BQ]
        dqts.append(
            jnp.dot(ends[512 + h * 64 : 576 + h * 64, :], dst, preferred_element_type=f32)
        )
        placed = jnp.dot(ends[0:512, :], dst, preferred_element_type=f32)
        coarse = placed.astype(bf16)
        fine = (placed - coarse.astype(f32)).astype(bf16)
        for kind in (0, 1):
            part = slice(kind * 256, kind * 256 + 256)
            cxy[h, part, :] += jnp.dot(
                coarse[part], flipped[kind], preferred_element_type=f32
            ) + jnp.dot(fine[part], flipped[kind], preferred_element_type=f32)
        for half in (0, 1):
            start = qb * 2 + half
            base = pl.multiple_of(start * 128, 128)
            lo = jnp.clip(start - 1, 0, tiles - 3)
            window = pl.ds(pl.multiple_of(lo * 128, 128), 384)
            origin = labc[pl.ds(base, 8), 1:2][0:1, 0:1]
            slot = iota((512, 384), 0)
            rel = labr[1:2, window]
            into = to_bf16(slot == rel - origin + 128)
            put = jnp.dot(
                into,
                pd[window, BQ + half * 128 : BQ + half * 128 + 128],
                preferred_element_type=f32,
            ).astype(bf16)
            from_here = to_bf16(255 - iota((128, 256), 1) == labc[pl.ds(base, 128), 1:2] - origin)
            cp[h] += jnp.dot(put, from_here, preferred_element_type=f32)
    dqkv[pl.ds(first, BQ), 0:width] = jnp.concatenate(dqts, axis=0).T.astype(bf16)

    @pl.when(qb == pl.num_programs(1) - 1)
    def _():
        for h in range(0, heads, 2):
            one, two = acc[h], acc[h + 1]
            dqkv[:, width + h * 64 : width + h * 64 + 128] = jnp.concatenate(
                [one[:, 64:], two[:, 64:]], axis=1
            ).astype(bf16)
            dqkv[:, 2 * width + h * 64 : 2 * width + h * 64 + 128] = jnp.concatenate(
                [one[:, :64], two[:, :64]], axis=1
            ).astype(bf16)
        lines = []
        for kind in (0, 1, 2):
            for h in range(heads):
                c = cp[h] if kind == 0 else cxy[h, (kind - 1) * 256 : kind * 256, :]
                c = jnp.concatenate([c, jnp.zeros_like(c)], axis=1)
                c = pltpu.roll(c, 0, 1, stride=1, stride_axis=0)
                lines.append(jnp.sum(c, axis=0, keepdims=True))
        rel = jnp.dot(
            jnp.concatenate(lines[:heads], axis=0),
            spread[0],
            preferred_element_type=f32,
            precision=lax.Precision.HIGHEST,
        )
        box = jnp.dot(
            jnp.concatenate(lines[heads:], axis=0),
            spread[1],
            preferred_element_type=f32,
            precision=lax.Precision.HIGHEST,
        )
        lane = iota((heads, 128), 1)
        low_all = jnp.concatenate([jnp.sum(sums[h * 16 : h * 16 + 8, :]).reshape(1, 1) for h in range(heads)], axis=0)
        high_all = jnp.concatenate([jnp.sum(sums[h * 16 + 8 : h * 16 + 16, :]).reshape(1, 1) for h in range(heads)], axis=0)
        near_low = jnp.sum(jnp.where(lane < 15, rel, 0.0), axis=1, keepdims=True)
        near_high = jnp.sum(jnp.where((lane >= 16) & (lane < 31), rel, 0.0), axis=1, keepdims=True)
        rel = jnp.where(lane == 15, low_all - near_low, rel)
        rel = jnp.where(lane == 31, high_all - near_high, rel)
        tg[...] = jnp.concatenate([rel, box], axis=0)


def spread_tables():
    slot = jnp.arange(512)
    number = jnp.arange(128)
    rel_t = slot - 383
    rel = (bucket_of(rel_t)[:, None] == number[None]) & (jnp.abs(rel_t) < 91)[:, None]
    box = bucket_of(slot - 255)[:, None] == number[None]
    return jnp.stack([rel, box]).astype(f32)


def label_arrays(segments, positions, boxes, pad_mask):
    zero = jnp.zeros_like(segments)
    labr = jnp.stack([segments, positions, boxes[0], boxes[1], pad_mask, zero, zero, zero], axis=1)
    return labr, jnp.swapaxes(labr, 1, 2)


def table_rows(tables):
    kinds, _, heads = tables.shape
    rows = jnp.swapaxes(tables, 1, 2).reshape(kinds * heads, NB).astype(f32)
    far = jnp.stack([tables[0, 15], tables[0, 31]]).astype(f32)
    return jnp.pad(rows, ((0, 0), (0, 128 - NB))), far


def cost(flops, nbytes):
    return pl.CostEstimate(flops=flops, bytes_accessed=nbytes, transcendentals=0)


def attention_forward(qkv, labr, labc, tab, far):
    rows, length, wide = qkv.shape
    width = wide // 3
    heads = width // 64
    steps = length // BQ
    smem = pl.BlockSpec(memory_space=pltpu.SMEM)
    return pl.pallas_call(
        functools.partial(fwd_kernel, heads),
        out_shape=(
            jax.ShapeDtypeStruct((rows, length, width), bf16),
            jax.ShapeDtypeStruct((rows, width, length), f32),
            jax.ShapeDtypeStruct((rows, 8, length), f32),
        ),
        grid=(rows, steps),
        in_specs=[
            smem,
            pl.BlockSpec((1, 8, length), lambda r, i: (r, 0, 0)),
            pl.BlockSpec((1, length, 8), lambda r, i: (r, 0, 0)),
            pl.BlockSpec(tab.shape, lambda r, i: (0, 0)),
            pl.BlockSpec((1, BQ, width), lambda r, i: (r, i, 0)),
            pl.BlockSpec((1, length, width), lambda r, i: (r, 0, 1)),
            pl.BlockSpec((1, length, width), lambda r, i: (r, 0, 2)),
        ],
        out_specs=(
            pl.BlockSpec((1, BQ, width), lambda r, i: (r, i, 0)),
            pl.BlockSpec((1, width, BQ), lambda r, i: (r, 0, i)),
            pl.BlockSpec((1, 8, BQ), lambda r, i: (r, 0, i)),
        ),
        scratch_shapes=[
            pltpu.VMEM((heads, length, 640), bf16),
            pltpu.VMEM((640, BQ), bf16),
            pltpu.VMEM((length, BQ), f32),
            pltpu.VMEM((length, BQ), bf16),
            pltpu.VMEM((width, length), bf16),
            pltpu.VMEM((512, BQ), jnp.int32),
        ],
        compiler_params=pltpu.CompilerParams(vmem_limit_bytes=48 << 20),
        cost_estimate=cost(rows * heads * length * length * 1664, rows * length * wide * 4),
    )(far, labr, labc, tab, qkv, qkv, qkv)


def attention_backward(qkv, labr, labc, tab, far, go, ot, lse):
    rows, length, wide = qkv.shape
    width = wide // 3
    heads = width // 64
    steps = length // BQ
    spread = spread_tables()
    smem = pl.BlockSpec(memory_space=pltpu.SMEM)
    return pl.pallas_call(
        functools.partial(bwd_kernel, heads),
        out_shape=(
            jax.ShapeDtypeStruct((rows, length, wide), bf16),
            jax.ShapeDtypeStruct((rows, 3 * heads, 128), f32),
        ),
        grid=(rows, steps),
        in_specs=[
            smem,
            pl.BlockSpec((1, 8, length), lambda r, i: (r, 0, 0)),
            pl.BlockSpec((1, length, 8), lambda r, i: (r, 0, 0)),
            pl.BlockSpec(tab.shape, lambda r, i: (0, 0)),
            pl.BlockSpec(spread.shape, lambda r, i: (0, 0, 0)),
            pl.BlockSpec((1, BQ, width), lambda r, i: (r, i, 0)),
            pl.BlockSpec((1, length, width), lambda r, i: (r, 0, 1)),
            pl.BlockSpec((1, length, width), lambda r, i: (r, 0, 2)),
            pl.BlockSpec((1, BQ, width), lambda r, i: (r, i, 0)),
            pl.BlockSpec((1, width, BQ), lambda r, i: (r, 0, i)),
            pl.BlockSpec((1, 8, BQ), lambda r, i: (r, 0, i)),
        ],
        out_specs=(
            pl.BlockSpec((1, length, wide), lambda r, i: (r, 0, 0)),
            pl.BlockSpec((1, 3 * heads, 128), lambda r, i: (r, 0, 0)),
        ),
        scratch_shapes=[
            pltpu.VMEM((heads, length, 640), bf16),
            pltpu.VMEM((640, BQ), bf16),
            pltpu.VMEM((length, BQ), f32),
            pltpu.VMEM((length, BQ), f32),
            pltpu.VMEM((length, 2 * BQ), bf16),
            pltpu.VMEM((512 + width, length), bf16),
            pltpu.VMEM((heads, length, 128), f32),
            pltpu.VMEM((heads, 512, 256), f32),
            pltpu.VMEM((heads, 512, 256), f32),
            pltpu.VMEM((heads * 16, BQ), f32),
            pltpu.VMEM((512, BQ), jnp.int32),
        ],
        compiler_params=pltpu.CompilerParams(vmem_limit_bytes=56 << 20),
        cost_estimate=cost(rows * heads * length * length * 5000, rows * length * wide * 6),
    )(far, labr, labc, tab, spread, qkv, qkv, qkv, go, ot, lse)


epsilon = 1e-06
gelu_coefficient = 0.7978845608028654


def rms_scale(row_values, gain_row):
    return (
        row_values
        * lax.rsqrt(jnp.mean(row_values * row_values, axis=-1, keepdims=True) + epsilon)
        * gain_row
    )


def gelu_tanh(values):
    return (
        0.5
        * values
        * (1.0 + jnp.tanh(gelu_coefficient * (values + 0.044715 * values * values * values)))
    )


def gated_unit(gate_rows, up_rows):
    return gelu_tanh(gate_rows) * up_rows


def mm(spec, one, two):
    return jnp.einsum(spec, one, two, preferred_element_type=f32)


def on_device(
    inputs,
    segments,
    positions,
    boxes,
    pad_mask,
    w_qkv,
    w_out,
    w_gate_up,
    w_down,
    bias_tables,
    gains,
    out_grad,
):
    gain_values = gains.astype(f32)
    labr, labc = label_arrays(segments, positions, boxes, pad_mask)
    tab, far = table_rows(bias_tables)

    def over_dp(w, axis):
        return lax.all_gather(w, "dp", axis=axis, tiled=True)

    def rows_of(part):
        return lax.all_gather(part, "mp", axis=1, tiled=True)

    def scatter_rows(whole):
        return lax.psum_scatter(whole, "mp", scatter_dimension=1, tiled=True)

    x = inputs.astype(f32)
    normed_one = rows_of(rms_scale(x, gain_values[0]).astype(bf16))
    wq = over_dp(w_qkv, 1)
    wqkv = jnp.concatenate([wq[0], wq[1], wq[2]], axis=1)
    qkv = mm("rld,dm->rlm", normed_one, wqkv).astype(bf16)
    mixed, ot, lse = attention_forward(qkv, labr, labc, tab, far)
    wo = over_dp(w_out, 1)
    attn = scatter_rows(mm("rlm,md->rld", mixed, wo).astype(bf16)).astype(f32)
    middle = x + attn
    normed_two = rows_of(rms_scale(middle, gain_values[1]).astype(bf16))
    wgu = over_dp(w_gate_up, 1)
    wd = over_dp(w_down, 1)
    og = rows_of(out_grad)
    gate = mm("rld,df->rlf", normed_two, wgu[0])
    up = mm("rld,df->rlf", normed_two, wgu[1])
    hidden, gated_back = jax.vjp(gated_unit, gate, up)
    hidden = hidden.astype(bf16)
    down = scatter_rows(mm("rlf,fd->rld", hidden, wd).astype(bf16)).astype(f32)
    out = (middle + down).astype(bf16)
    hidden_grad = mm("rld,fd->rlf", og, wd)
    gate_grad, up_grad = gated_back(hidden_grad)
    gate_grad, up_grad = gate_grad.astype(bf16), up_grad.astype(bf16)
    n2g = scatter_rows(
        (mm("rlf,df->rld", gate_grad, wgu[0]) + mm("rlf,df->rld", up_grad, wgu[1])).astype(bf16)
    ).astype(f32)
    w_down_grad = mm("rlf,rld->fd", hidden, og)
    w_gate_grad = mm("rld,rlf->df", normed_two, gate_grad)
    w_up_grad = mm("rld,rlf->df", normed_two, up_grad)

    def grads_over_dp(whole, axis):
        return lax.psum_scatter(
            whole.astype(bf16), "dp", scatter_dimension=axis, tiled=True
        ).astype(f32)

    gate_up_out = grads_over_dp(jnp.stack([w_gate_grad, w_up_grad]), 1)
    down_out = grads_over_dp(w_down_grad, 1)
    unused, norm_back_two = jax.vjp(rms_scale, middle, gain_values[1])
    middle_part, gain_two = norm_back_two(n2g)
    middle_grad = middle_part + out_grad.astype(f32)
    attn_grad = rows_of(middle_grad.astype(bf16))
    mixed_grad = mm("rld,md->rlm", attn_grad, wo).astype(bf16)
    w_out_grad = mm("rlm,rld->md", mixed, attn_grad)
    dqkv, tg = attention_backward(qkv, labr, labc, tab, far, mixed_grad, ot, lse)
    width = mixed.shape[2]
    heads = width // 64
    n1g = scatter_rows(mm("rlm,dm->rld", dqkv, wqkv).astype(bf16)).astype(f32)
    w_qkv_grad = mm("rld,rlm->dm", normed_one, dqkv)
    w_qkv_grad = jnp.stack([w_qkv_grad[:, i * width : (i + 1) * width] for i in range(3)])
    qkv_out = grads_over_dp(w_qkv_grad, 1)
    out_out = grads_over_dp(w_out_grad, 1)
    tg = jnp.sum(tg, axis=0)[:, :NB].reshape(3, heads, NB)
    table_out = lax.psum_scatter(
        jnp.swapaxes(tg, 1, 2), "dp", scatter_dimension=1, tiled=True
    )
    unused, norm_back_one = jax.vjp(rms_scale, x, gain_values[0])
    input_part, gain_one = norm_back_one(n1g)
    input_grad = (input_part + middle_grad).astype(bf16)
    gain_out = lax.psum_scatter(
        jnp.stack([gain_one, gain_two]), ("dp", "mp"), scatter_dimension=1, tiled=True
    )
    return (out, input_grad, qkv_out, out_out, gate_up_out, down_out, table_out, gain_out)


def solution(mesh):
    placed = (
        P("dp", "mp", None),
        P("dp", None),
        P("dp", None),
        P(None, "dp", None),
        P("dp", None),
        P(None, "dp", "mp"),
        P("mp", "dp"),
        P(None, "dp", "mp"),
        P("mp", "dp"),
        P(None, None, "mp"),
        P(),
        P("dp", "mp", None),
    )
    return jax.shard_map(
        on_device,
        mesh=mesh,
        in_specs=placed,
        out_specs=(
            P("dp", "mp", None),
            P("dp", "mp", None),
            P(None, "dp", "mp"),
            P("mp", "dp"),
            P(None, "dp", "mp"),
            P("mp", "dp"),
            P(None, "dp", "mp"),
            P(None, ("dp", "mp")),
        ),
        check_vma=False,
    )
```

```python
import functools
import jax
import jax.numpy as jnp
from jax import lax
from jax.experimental import pallas as pl
from jax.experimental.pallas import tpu as pltpu
from jax.sharding import PartitionSpec as P

NB = 32
thresholds = (12, 16, 23, 32, 46, 64, 91)
BQ = 256
NEG = -1e30
bf16 = jnp.bfloat16
f32 = jnp.float32


def bucket_of(distance):
    magnitude = jnp.abs(distance)
    stepped = 8 + sum(((magnitude >= boundary).astype(jnp.int32) for boundary in thresholds))
    return jnp.where(magnitude < 8, magnitude, stepped) + 16 * (distance > 0).astype(jnp.int32)


def iota(shape, axis):
    return lax.broadcasted_iota(jnp.int32, shape, axis)


def to_bf16(mask):
    return jnp.where(mask, 1.0, 0.0).astype(bf16)


def key_features(labc, tab, k, feats, heads):
    length = labc.shape[0]
    for kind in (0, 1):
        chosen = to_bf16(iota((length, 256), 1) == labc[:, 2 + kind : 3 + kind])
        where_bucket = bucket_of(iota((256, 256), 0) - iota((256, 256), 1))
        for h in range(heads):
            row = tab[(1 + kind) * heads + h : (1 + kind) * heads + h + 1, :]
            wide = jnp.broadcast_to(row, (256, 128))
            toep = jnp.concatenate(
                [
                    jnp.take_along_axis(wide, where_bucket[:, c : c + 128], axis=1)
                    for c in (0, 128)
                ],
                axis=1,
            ).astype(bf16)
            feats[h, :, kind * 256 : kind * 256 + 256] = jnp.dot(
                chosen, toep, preferred_element_type=f32
            ).astype(bf16)
    lane = iota((length, 64), 1)
    mask = jnp.where(
        lane < 8,
        jnp.where(labc[:, 0:1] == lane, 0.0, NEG),
        jnp.where((lane == 8) & (labc[:, 4:5] != 1), NEG, 0.0),
    ).astype(bf16)
    for h in range(heads):
        feats[h, :, 512:576] = k[:, h * 64 : h * 64 + 64]
        feats[h, :, 576:640] = mask


def query_features(labr, first, a):
    def of(row):
        return labr[row : row + 1, pl.ds(first, BQ)]

    sub = iota((256, BQ), 0)
    a[0:256, :] = to_bf16(sub == of(2))
    a[256:512, :] = to_bf16(sub == of(3))
    low = iota((64, BQ), 0)
    a[576:640, :] = jnp.where(
        low < 8, jnp.where(of(0) == low, 1.0, 0.0), jnp.where(low == 8, 1.0, 0.0)
    ).astype(bf16)


def near_buckets(labr, labc, qb, idx, tiles):
    first = pl.multiple_of(qb * BQ, BQ)
    here = labr[1:2, pl.ds(first, BQ)]
    for n in range(4):
        t = 2 * qb - 1 + n

        @pl.when((t >= 0) & (t < tiles))
        def _():
            there = labc[pl.ds(pl.multiple_of(t * 128, 128), 128), 1:2]
            idx[n * 128 : n * 128 + 128, :] = bucket_of(there - here)


def add_near(s_ref, tab, idx, labr, qb, h, own, tiles):
    first = pl.multiple_of(qb * BQ, BQ)
    wide = jnp.broadcast_to(tab[h : h + 1, :], (128, 128))
    padded = labr[4:5, pl.ds(first, BQ)] != 1
    for n in range(4):
        t = 2 * qb - 1 + n

        @pl.when((t >= 0) & (t < tiles))
        def _():
            rows = pl.ds(pl.multiple_of(t * 128, 128), 128)
            got = jnp.concatenate(
                [
                    jnp.take_along_axis(wide, idx[n * 128 : n * 128 + 128, c : c + 128], axis=1)
                    for c in range(0, BQ, 128)
                ],
                axis=1,
            )
            s = s_ref[rows, :] + got
            if n in (1, 2):
                same = iota((128, BQ), 0) + (n - 1) * 128 == iota((128, BQ), 1)
                s = jnp.where(same & padded, own, s)
            s_ref[rows, :] = s


def own_scores(qt, k_block, tab, heads):
    kt = k_block.T.astype(f32)
    prod = qt.astype(f32) * kt
    out = []
    for h in range(heads):
        zero_bias = tab[h, 0] + tab[heads + h, 0] + tab[2 * heads + h, 0]
        out.append(jnp.sum(prod[h * 64 : h * 64 + 64], axis=0, keepdims=True) + zero_bias)
    return out


def far_constant(far, qb, t, h):
    return jnp.where(t < 2 * qb - 1, far[0, h], jnp.where(t > 2 * qb + 2, far[1, h], 0.0))


def rows_max(value):
    return functools.reduce(jnp.maximum, [value[i : i + 8] for i in range(0, value.shape[0], 8)])


def rows_sum(value):
    return functools.reduce(jnp.add, [value[i : i + 8] for i in range(0, value.shape[0], 8)])


def fwd_kernel(heads, far, labr, labc, tab, q, k, v, mixed, ot, lse, feats, a, s_ref, p_ref, vt, idx):
    labr, labc, q, k, v = labr.at[0], labc.at[0], q.at[0], k.at[0], v.at[0]
    mixed, ot, lse = mixed.at[0], ot.at[0], lse.at[0]
    length = labc.shape[0]
    tiles = length // 128
    qb = pl.program_id(1)
    first = pl.multiple_of(qb * BQ, BQ)

    @pl.when(qb == 0)
    def _():
        key_features(labc, tab, k, feats, heads)
        vt[...] = v[...].T

    query_features(labr, first, a)
    near_buckets(labr, labc, qb, idx, tiles)
    qt = q[...].T
    own = own_scores(qt, k[pl.ds(first, BQ), :], tab, heads)
    outs = []
    for h in range(heads):
        a[512:576, :] = qt[h * 64 : h * 64 + 64]
        s_ref[...] = jnp.dot(feats[h], a[...], preferred_element_type=f32)
        add_near(s_ref, tab, idx, labr, qb, h, own[h], tiles)
        top = None
        for t in range(tiles):
            here = rows_max(s_ref[t * 128 : t * 128 + 128, :]) + far_constant(far, qb, t, h)
            top = here if top is None else jnp.maximum(top, here)
        top = jnp.max(top, axis=0, keepdims=True)
        total = jnp.zeros((8, BQ), f32)
        for t in range(tiles):
            shift = top - far_constant(far, qb, t, h)
            p = jnp.exp(s_ref[t * 128 : t * 128 + 128, :] - shift)
            total = total + rows_sum(p)
            p_ref[t * 128 : t * 128 + 128, :] = p.astype(bf16)
        total = jnp.sum(total, axis=0, keepdims=True)
        o = jnp.dot(vt[h * 64 : h * 64 + 64, :], p_ref[...], preferred_element_type=f32)
        o = o * (1.0 / total)
        ot[h * 64 : h * 64 + 64, :] = o
        lse[h : h + 1, :] = top + jnp.log(total)
        outs.append(o)
    mixed[...] = jnp.concatenate(outs, axis=0).T.astype(bf16)


def bwd_kernel(
    heads, far, labr, labc, tab, spread, q, k, v, go, ot, lse,
    dqkv, tg,
    feats, a, s_ref, dp_ref, pd, ends, acc, cxy, cp, sums, idx,
):
    labr, labc, q, k, v = labr.at[0], labc.at[0], q.at[0], k.at[0], v.at[0]
    go, ot, lse, dqkv, tg = go.at[0], ot.at[0], lse.at[0], dqkv.at[0], tg.at[0]
    length = labc.shape[0]
    width = heads * 64
    tiles = length // 128
    qb = pl.program_id(1)
    first = pl.multiple_of(qb * BQ, BQ)

    @pl.when(qb == 0)
    def _():
        key_features(labc, tab, k, feats, heads)
        sub = iota((256, length), 0)
        ends[0:256, :] = to_bf16(sub == labr[2:3, :])
        ends[256:512, :] = to_bf16(sub == labr[3:4, :])
        acc[...] = jnp.zeros_like(acc)
        cxy[...] = jnp.zeros_like(cxy)
        cp[...] = jnp.zeros_like(cp)
        sums[...] = jnp.zeros_like(sums)
        ends[512 : 512 + width, :] = k[...].T

    query_features(labr, first, a)
    near_buckets(labr, labc, qb, idx, tiles)
    qt = q[...].T
    own = own_scores(qt, k[pl.ds(first, BQ), :], tab, heads)
    gt = go[...].T
    delta_all = gt.astype(f32) * ot[...]
    flipped = [
        to_bf16(255 - iota((BQ, 256), 1) == labc[pl.ds(first, BQ), 2 + kind : 3 + kind])
        for kind in (0, 1)
    ]
    zeros = jnp.zeros((BQ, 64), bf16)
    dqts = []
    for h in range(heads):
        cols = slice(h * 64, h * 64 + 64)
        a[512:576, :] = qt[cols]
        s_ref[...] = jnp.dot(feats[h], a[...], preferred_element_type=f32)
        dp_ref[...] = jnp.dot(v[:, cols], gt[cols], preferred_element_type=f32)
        add_near(s_ref, tab, idx, labr, qb, h, own[h], tiles)
        delta = jnp.sum(delta_all[cols], axis=0, keepdims=True)
        low = jnp.zeros((8, BQ), f32)
        high = jnp.zeros((8, BQ), f32)
        for t in range(tiles):
            rows = slice(t * 128, t * 128 + 128)
            shift = lse[h : h + 1, :] - far_constant(far, qb, t, h)
            p = jnp.exp(s_ref[rows, :] - shift)
            ds = p * (dp_ref[rows, :] - delta)
            pd[rows, 0:BQ] = p.astype(bf16)
            pd[rows, BQ : 2 * BQ] = ds.astype(bf16)
            after = (t * 128 - qb * BQ + iota((128, BQ), 0)) > iota((128, BQ), 1)
            high = high + rows_sum(jnp.where(after, ds, 0.0))
            low = low + rows_sum(ds)
        sums[h * 16 : h * 16 + 8, :] += low - high
        sums[h * 16 + 8 : h * 16 + 16, :] += high
        right = jnp.concatenate(
            [
                jnp.concatenate([go[:, cols], zeros], axis=1),
                jnp.concatenate([zeros, q[:, cols]], axis=1),
            ],
            axis=0,
        )
        acc[h] += jnp.dot(pd[...], right, preferred_element_type=f32)
        dst = pd[:, BQ : 2 * BQ]
        dqts.append(
            jnp.dot(ends[512 + h * 64 : 576 + h * 64, :], dst, preferred_element_type=f32)
        )
        placed = jnp.dot(ends[0:512, :], dst, preferred_element_type=f32)
        coarse = placed.astype(bf16)
        fine = (placed - coarse.astype(f32)).astype(bf16)
        for kind in (0, 1):
            part = slice(kind * 256, kind * 256 + 256)
            cxy[h, part, :] += jnp.dot(
                coarse[part], flipped[kind], preferred_element_type=f32
            ) + jnp.dot(fine[part], flipped[kind], preferred_element_type=f32)
        for half in (0, 1):
            start = qb * 2 + half
            base = pl.multiple_of(start * 128, 128)
            lo = jnp.clip(start - 1, 0, tiles - 3)
            window = pl.ds(pl.multiple_of(lo * 128, 128), 384)
            origin = labc[pl.ds(base, 8), 1:2][0:1, 0:1]
            slot = iota((512, 384), 0)
            rel = labr[1:2, window]
            into = to_bf16(slot == rel - origin + 128)
            put = jnp.dot(
                into,
                pd[window, BQ + half * 128 : BQ + half * 128 + 128],
                preferred_element_type=f32,
            ).astype(bf16)
            from_here = to_bf16(255 - iota((128, 256), 1) == labc[pl.ds(base, 128), 1:2] - origin)
            cp[h] += jnp.dot(put, from_here, preferred_element_type=f32)
    dqkv[pl.ds(first, BQ), 0:width] = jnp.concatenate(dqts, axis=0).T.astype(bf16)

    @pl.when(qb == pl.num_programs(1) - 1)
    def _():
        for h in range(0, heads, 2):
            one, two = acc[h], acc[h + 1]
            dqkv[:, width + h * 64 : width + h * 64 + 128] = jnp.concatenate(
                [one[:, 64:], two[:, 64:]], axis=1
            ).astype(bf16)
            dqkv[:, 2 * width + h * 64 : 2 * width + h * 64 + 128] = jnp.concatenate(
                [one[:, :64], two[:, :64]], axis=1
            ).astype(bf16)
        lines = []
        for kind in (0, 1, 2):
            for h in range(heads):
                c = cp[h] if kind == 0 else cxy[h, (kind - 1) * 256 : kind * 256, :]
                c = jnp.concatenate([c, jnp.zeros_like(c)], axis=1)
                c = pltpu.roll(c, 0, 1, stride=1, stride_axis=0)
                lines.append(jnp.sum(c, axis=0, keepdims=True))
        rel = jnp.dot(
            jnp.concatenate(lines[:heads], axis=0),
            spread[0],
            preferred_element_type=f32,
            precision=lax.Precision.HIGHEST,
        )
        box = jnp.dot(
            jnp.concatenate(lines[heads:], axis=0),
            spread[1],
            preferred_element_type=f32,
            precision=lax.Precision.HIGHEST,
        )
        lane = iota((heads, 128), 1)
        low_all = jnp.concatenate([jnp.sum(sums[h * 16 : h * 16 + 8, :]).reshape(1, 1) for h in range(heads)], axis=0)
        high_all = jnp.concatenate([jnp.sum(sums[h * 16 + 8 : h * 16 + 16, :]).reshape(1, 1) for h in range(heads)], axis=0)
        near_low = jnp.sum(jnp.where(lane < 15, rel, 0.0), axis=1, keepdims=True)
        near_high = jnp.sum(jnp.where((lane >= 16) & (lane < 31), rel, 0.0), axis=1, keepdims=True)
        rel = jnp.where(lane == 15, low_all - near_low, rel)
        rel = jnp.where(lane == 31, high_all - near_high, rel)
        tg[...] = jnp.concatenate([rel, box], axis=0)


def spread_tables():
    slot = jnp.arange(512)
    number = jnp.arange(128)
    rel_t = slot - 383
    rel = (bucket_of(rel_t)[:, None] == number[None]) & (jnp.abs(rel_t) < 91)[:, None]
    box = bucket_of(slot - 255)[:, None] == number[None]
    return jnp.stack([rel, box]).astype(f32)


def label_arrays(segments, positions, boxes, pad_mask):
    zero = jnp.zeros_like(segments)
    labr = jnp.stack([segments, positions, boxes[0], boxes[1], pad_mask, zero, zero, zero], axis=1)
    return labr, jnp.swapaxes(labr, 1, 2)


def table_rows(tables):
    kinds, _, heads = tables.shape
    rows = jnp.swapaxes(tables, 1, 2).reshape(kinds * heads, NB).astype(f32)
    far = jnp.stack([tables[0, 15], tables[0, 31]]).astype(f32)
    return jnp.pad(rows, ((0, 0), (0, 128 - NB))), far


def cost(flops, nbytes):
    return pl.CostEstimate(flops=flops, bytes_accessed=nbytes, transcendentals=0)


def attention_forward(qkv, labr, labc, tab, far):
    rows, length, wide = qkv.shape
    width = wide // 3
    heads = width // 64
    steps = length // BQ
    smem = pl.BlockSpec(memory_space=pltpu.SMEM)
    return pl.pallas_call(
        functools.partial(fwd_kernel, heads),
        out_shape=(
            jax.ShapeDtypeStruct((rows, length, width), bf16),
            jax.ShapeDtypeStruct((rows, width, length), f32),
            jax.ShapeDtypeStruct((rows, 8, length), f32),
        ),
        grid=(rows, steps),
        in_specs=[
            smem,
            pl.BlockSpec((1, 8, length), lambda r, i: (r, 0, 0)),
            pl.BlockSpec((1, length, 8), lambda r, i: (r, 0, 0)),
            pl.BlockSpec(tab.shape, lambda r, i: (0, 0)),
            pl.BlockSpec((1, BQ, width), lambda r, i: (r, i, 0)),
            pl.BlockSpec((1, length, width), lambda r, i: (r, 0, 1)),
            pl.BlockSpec((1, length, width), lambda r, i: (r, 0, 2)),
        ],
        out_specs=(
            pl.BlockSpec((1, BQ, width), lambda r, i: (r, i, 0)),
            pl.BlockSpec((1, width, BQ), lambda r, i: (r, 0, i)),
            pl.BlockSpec((1, 8, BQ), lambda r, i: (r, 0, i)),
        ),
        scratch_shapes=[
            pltpu.VMEM((heads, length, 640), bf16),
            pltpu.VMEM((640, BQ), bf16),
            pltpu.VMEM((length, BQ), f32),
            pltpu.VMEM((length, BQ), bf16),
            pltpu.VMEM((width, length), bf16),
            pltpu.VMEM((512, BQ), jnp.int32),
        ],
        compiler_params=pltpu.CompilerParams(vmem_limit_bytes=48 << 20),
        cost_estimate=cost(rows * heads * length * length * 1664, rows * length * wide * 4),
    )(far, labr, labc, tab, qkv, qkv, qkv)


def attention_backward(qkv, labr, labc, tab, far, go, ot, lse):
    rows, length, wide = qkv.shape
    width = wide // 3
    heads = width // 64
    steps = length // BQ
    spread = spread_tables()
    smem = pl.BlockSpec(memory_space=pltpu.SMEM)
    return pl.pallas_call(
        functools.partial(bwd_kernel, heads),
        out_shape=(
            jax.ShapeDtypeStruct((rows, length, wide), bf16),
            jax.ShapeDtypeStruct((rows, 3 * heads, 128), f32),
        ),
        grid=(rows, steps),
        in_specs=[
            smem,
            pl.BlockSpec((1, 8, length), lambda r, i: (r, 0, 0)),
            pl.BlockSpec((1, length, 8), lambda r, i: (r, 0, 0)),
            pl.BlockSpec(tab.shape, lambda r, i: (0, 0)),
            pl.BlockSpec(spread.shape, lambda r, i: (0, 0, 0)),
            pl.BlockSpec((1, BQ, width), lambda r, i: (r, i, 0)),
            pl.BlockSpec((1, length, width), lambda r, i: (r, 0, 1)),
            pl.BlockSpec((1, length, width), lambda r, i: (r, 0, 2)),
            pl.BlockSpec((1, BQ, width), lambda r, i: (r, i, 0)),
            pl.BlockSpec((1, width, BQ), lambda r, i: (r, 0, i)),
            pl.BlockSpec((1, 8, BQ), lambda r, i: (r, 0, i)),
        ],
        out_specs=(
            pl.BlockSpec((1, length, wide), lambda r, i: (r, 0, 0)),
            pl.BlockSpec((1, 3 * heads, 128), lambda r, i: (r, 0, 0)),
        ),
        scratch_shapes=[
            pltpu.VMEM((heads, length, 640), bf16),
            pltpu.VMEM((640, BQ), bf16),
            pltpu.VMEM((length, BQ), f32),
            pltpu.VMEM((length, BQ), f32),
            pltpu.VMEM((length, 2 * BQ), bf16),
            pltpu.VMEM((512 + width, length), bf16),
            pltpu.VMEM((heads, length, 128), f32),
            pltpu.VMEM((heads, 512, 256), f32),
            pltpu.VMEM((heads, 512, 256), f32),
            pltpu.VMEM((heads * 16, BQ), f32),
            pltpu.VMEM((512, BQ), jnp.int32),
        ],
        compiler_params=pltpu.CompilerParams(vmem_limit_bytes=56 << 20),
        cost_estimate=cost(rows * heads * length * length * 5000, rows * length * wide * 6),
    )(far, labr, labc, tab, spread, qkv, qkv, qkv, go, ot, lse)


def dot_nt(one, two):
    return lax.dot_general(one, two, (((1,), (1,)), ((), ())), preferred_element_type=f32)


def dot_nn(one, two):
    return jnp.dot(one, two, preferred_element_type=f32)


def ffn_kernel(n2, og, w, down, n2g, dw, n2t, ogt, gate, up, hg, hid, dgate, dup):
    depth = n2.shape[1]
    wide = w.shape[3]
    wg = w[:, 0].reshape(depth, wide)
    wu = w[:, 1].reshape(depth, wide)
    wd = w[:, 2].reshape(depth, wide)
    gate[...] = dot_nn(n2[...], wg)
    up[...] = dot_nn(n2[...], wu)
    hg[...] = dot_nn(og[...], wd)
    n2t[...] = n2[...].T
    ogt[...] = og[...].T

    def chunk(c, _):
        rows = pl.ds(pl.multiple_of(c * 16, 16), 16)
        g, u, back = gate[rows, :], up[rows, :], hg[rows, :]
        square = g * g
        t = jnp.tanh(gelu_coefficient * (g + 0.044715 * square * g))
        half = 0.5 * (1.0 + t)
        act = g * half
        slope = half + 0.5 * g * (1.0 - t * t) * (
            gelu_coefficient * (1.0 + 0.134145 * square)
        )
        hid[rows, :] = (act * u).astype(bf16)
        dgate[rows, :] = (back * u * slope).astype(bf16)
        dup[rows, :] = (back * act).astype(bf16)
        return 0

    lax.fori_loop(0, n2.shape[0] // 16, chunk, 0, unroll=2)
    n2g[...] = dot_nt(dgate[...], wg) + dot_nt(dup[...], wu)
    down[...] = dot_nt(hid[...], wd)
    parts = dw.shape[0]
    dw[:, 0] = dot_nn(n2t[...], dgate[...]).astype(bf16).reshape(parts, -1, wide)
    dw[:, 1] = dot_nn(n2t[...], dup[...]).astype(bf16).reshape(parts, -1, wide)
    dw[:, 2] = dot_nn(ogt[...], hid[...]).astype(bf16).reshape(parts, -1, wide)


def ffn(n2, og, w):
    tokens, depth = n2.shape
    wide = w.shape[3]
    vmem = pl.BlockSpec(memory_space=pltpu.VMEM)
    return pl.pallas_call(
        ffn_kernel,
        out_shape=(
            jax.ShapeDtypeStruct((tokens, depth), f32),
            jax.ShapeDtypeStruct((tokens, depth), f32),
            jax.ShapeDtypeStruct(w.shape, bf16),
        ),
        in_specs=[vmem] * 3,
        out_specs=(vmem,) * 3,
        scratch_shapes=[
            pltpu.VMEM((depth, tokens), bf16),
            pltpu.VMEM((depth, tokens), bf16),
            pltpu.VMEM((tokens, wide), f32),
            pltpu.VMEM((tokens, wide), f32),
            pltpu.VMEM((tokens, wide), f32),
            pltpu.VMEM((tokens, wide), bf16),
            pltpu.VMEM((tokens, wide), bf16),
            pltpu.VMEM((tokens, wide), bf16),
        ],
        compiler_params=pltpu.CompilerParams(vmem_limit_bytes=56 << 20),
        cost_estimate=cost(18 * tokens * depth * wide, 4 * w.size + 12 * tokens * depth),
    )(n2, og, w)


epsilon = 1e-06
gelu_coefficient = 0.7978845608028654


def rms_scale(row_values, gain_row):
    return (
        row_values
        * lax.rsqrt(jnp.mean(row_values * row_values, axis=-1, keepdims=True) + epsilon)
        * gain_row
    )


def mm(spec, one, two):
    return jnp.einsum(spec, one, two, preferred_element_type=f32)


def bits_of(size):
    return [1 << b for b in reversed(range(size.bit_length() - 1))]


def swap(value, axis, size, distance):
    return lax.ppermute(value, axis, [(j, j ^ distance) for j in range(size)])


def gather_xor(own, axis, size, bits):
    held = {0: own}
    for b in bits:
        held.update({k ^ b: swap(v, axis, size, b) for k, v in list(held.items())})
    return held


def scatter_xor(parts, axis, size, bits):
    held = dict(parts)
    for b in reversed(bits):
        for k in [k for k in held if not k & b]:
            held[k] = held[k] + swap(held.pop(k | b).astype(bf16), axis, size, b).astype(f32)
    return held[0]


def scatter_dp(whole, size):
    me = lax.axis_index("dp")
    b = 1
    while b < size:
        pairs = whole.reshape((whole.shape[0] // 2, 2) + whole.shape[1:])
        mine = (me // b) % 2
        keep = lax.dynamic_index_in_dim(pairs, mine, 1, keepdims=False)
        send = lax.dynamic_index_in_dim(pairs, 1 - mine, 1, keepdims=False)
        whole = keep.astype(f32) + swap(send.astype(bf16), "dp", size, b).astype(f32)
        b *= 2
    return whole[0]


def on_device(
    dp,
    mp,
    inputs,
    segments,
    positions,
    boxes,
    pad_mask,
    w_qkv,
    w_out,
    w_gate_up,
    w_down,
    bias_tables,
    gains,
    out_grad,
):
    gain_values = gains.astype(f32)
    labr, labc = label_arrays(segments, positions, boxes, pad_mask)
    tab, far = table_rows(bias_tables)
    here = lax.axis_index("mp")
    rows, part, depth = inputs.shape
    width = w_out.shape[0]
    heads = width // 64
    slice_rows = w_qkv.shape[1]
    wide = w_down.shape[0]
    all_bits = bits_of(mp)
    near_bit, far_bits = 1, all_bits[:-1]

    def in_order(held):
        stacked = jnp.stack([held[k] for k in range(mp)])
        return jnp.concatenate(
            [lax.dynamic_index_in_dim(stacked, here ^ m, 0, keepdims=False) for m in range(mp)],
            axis=1,
        )

    def block_for(whole, k):
        return lax.dynamic_slice_in_dim(whole, (here ^ k) * part, part, 1)

    def exchange(blocks):
        return {k: v if k == 0 else swap(v, "mp", mp, k) for k, v in blocks.items()}

    wqkv = lax.all_gather(
        jnp.swapaxes(w_qkv, 0, 1).reshape(slice_rows, 3 * width), "dp", axis=0, tiled=True
    )
    x = inputs.astype(f32)
    n1 = gather_xor(rms_scale(x, gain_values[0]).astype(bf16), "mp", mp, all_bits)
    normed_one = in_order(n1)
    wo_held = gather_xor(w_out.T, "mp", mp, all_bits)
    wo = lax.all_gather(
        jnp.concatenate([wo_held[k] for k in range(mp)], axis=1), "dp", axis=0, tiled=True
    )
    packed = jnp.concatenate([w_gate_up, w_down.T[None]], axis=0)
    packs = gather_xor(packed, "mp", mp, far_bits)
    ffn_w = {
        k: lax.all_gather(v.reshape(3 * slice_rows, wide), "dp", axis=0, tiled=True).reshape(
            dp, 3, slice_rows, wide
        )
        for k, v in packs.items()
    }

    qkv = mm("rld,dm->rlm", normed_one, wqkv).astype(bf16)
    mixed, ot, lse = attention_forward(qkv, labr, labc, tab, far)
    mixed_in = exchange({k: block_for(mixed, k) for k in range(mp)})
    mixed_all = jnp.concatenate([mixed_in[k] for k in range(mp)], axis=2)
    attn = mm("rlm,dm->rld", mixed_all, wo)
    middle = x + attn

    normed_two = rms_scale(middle, gain_values[1]).astype(bf16)

    def beside(own):
        return jnp.concatenate([own, swap(own, "mp", mp, near_bit)], axis=1).reshape(-1, depth)

    n2 = beside(normed_two)
    og = beside(out_grad)
    down, n2g, w_grads = None, None, {}
    for k, w in ffn_w.items():
        down_k, n2g_k, w_grads[k] = ffn(n2, og, w)
        down = down_k if down is None else down + down_k
        n2g = n2g_k if n2g is None else n2g + n2g_k

    def own_sum(both):
        both = both.reshape(rows, 2 * part, depth)
        return both[:, :part] + swap(both[:, part:].astype(bf16), "mp", mp, near_bit).astype(f32)

    n2g = own_sum(n2g)
    out = (middle + own_sum(down)).astype(bf16)
    unused, norm_back_two = jax.vjp(lambda v: rms_scale(v, gain_values[1]), middle)
    middle_grad = norm_back_two(n2g)[0] + out_grad.astype(f32)
    attn_grad = middle_grad.astype(bf16)

    own_terms = {
        k: lax.psum_scatter(
            g.reshape(dp * 3 * slice_rows, wide), "dp", scatter_dimension=0, tiled=True
        ).astype(f32)
        for k, g in w_grads.items()
    }
    w_grad = scatter_xor(own_terms, "mp", mp, far_bits).reshape(3, slice_rows, wide)
    gate_up_out = w_grad[:2]
    down_out = w_grad[2].T

    mixed_grad = mm("rld,dm->rlm", attn_grad, wo).astype(bf16)
    go = in_order(
        exchange({k: mixed_grad[:, :, k * width : (k + 1) * width] for k in range(mp)})
    )
    dqkv, tg = attention_backward(qkv, labr, labc, tab, far, go, ot, lse)
    n1g_all = mm("rlm,dm->rld", dqkv, wqkv)
    n1g = scatter_xor({k: block_for(n1g_all, k) for k in range(mp)}, "mp", mp, all_bits)
    qkv_term = mm("rld,rlm->dm", normed_one, dqkv)
    qkv_sum = scatter_dp(qkv_term.reshape(dp, slice_rows, 3 * width), dp)
    qkv_out = jnp.swapaxes(qkv_sum.reshape(slice_rows, 3, width), 0, 1)
    out_term = mm("rld,rlm->dm", attn_grad, mixed_all)
    out_sum = scatter_dp(out_term.reshape(dp, slice_rows, mp * width), dp)
    out_out = scatter_xor(
        {k: out_sum[:, k * width : (k + 1) * width] for k in range(mp)}, "mp", mp, all_bits
    ).T
    tg = jnp.sum(tg, axis=0)[:, :NB].reshape(3 * heads, dp, NB // dp)
    table_sum = scatter_dp(jnp.swapaxes(tg, 0, 1), dp)
    table_out = jnp.swapaxes(table_sum.reshape(3, heads, NB // dp), 1, 2)
    unused, norm_back_one = jax.vjp(lambda v: rms_scale(v, gain_values[0]), x)
    input_grad = (norm_back_one(n1g)[0] + middle_grad).astype(bf16)

    own_gains = lax.dynamic_slice_in_dim(
        gain_values, lax.axis_index("dp") * slice_rows, slice_rows, 1
    )
    products = (
        jnp.stack(
            [
                jnp.sum(qkv_out * w_qkv.astype(f32), axis=(0, 2)),
                jnp.sum(gate_up_out * w_gate_up.astype(f32), axis=(0, 2)),
            ]
        )
        / own_gains
    ).reshape(2, mp, slice_rows // mp)
    held = {
        k: lax.dynamic_index_in_dim(products, here ^ k, 1, keepdims=False) for k in range(mp)
    }
    for b in reversed(all_bits):
        for k in [k for k in held if not k & b]:
            held[k] = held[k] + swap(held.pop(k | b), "mp", mp, b)
    gain_out = held[0]
    return (out, input_grad, qkv_out, out_out, gate_up_out, down_out, table_out, gain_out)


def solution(mesh):
    placed = (
        P("dp", "mp", None),
        P("dp", None),
        P("dp", None),
        P(None, "dp", None),
        P("dp", None),
        P(None, "dp", "mp"),
        P("mp", "dp"),
        P(None, "dp", "mp"),
        P("mp", "dp"),
        P(None, None, "mp"),
        P(),
        P("dp", "mp", None),
    )
    return jax.shard_map(
        functools.partial(on_device, mesh.shape["dp"], mesh.shape["mp"]),
        mesh=mesh,
        in_specs=placed,
        out_specs=(
            P("dp", "mp", None),
            P("dp", "mp", None),
            P(None, "dp", "mp"),
            P("mp", "dp"),
            P(None, "dp", "mp"),
            P("mp", "dp"),
            P(None, "dp", "mp"),
            P(None, ("dp", "mp")),
        ),
        check_vma=False,
    )
```

```python
import functools
import jax
import jax.numpy as jnp
from jax import lax
from jax.experimental import pallas as pl
from jax.experimental.pallas import tpu as pltpu
from jax.sharding import PartitionSpec as P

NB = 32
thresholds = (12, 16, 23, 32, 46, 64, 91)
BQ = 256
PAD = 128
REACH = 448
TR = 64
UNIT = 256
UNROLL = 2
NEG = -1e30
bf16 = jnp.bfloat16
f32 = jnp.float32


def bucket_of(distance):
    magnitude = jnp.abs(distance)
    stepped = 8 + sum(((magnitude >= boundary).astype(jnp.int32) for boundary in thresholds))
    return jnp.where(magnitude < 8, magnitude, stepped) + 16 * (distance > 0).astype(jnp.int32)


def iota(shape, axis):
    return lax.broadcasted_iota(jnp.int32, shape, axis)


def to_bf16(mask):
    return jnp.where(mask, 1.0, 0.0).astype(bf16)


def key_features(labc_padded, tab, k, feats, heads):
    length = k.shape[0]
    labc = labc_padded[PAD : PAD + length, :]
    for kind in (0, 1):
        chosen = to_bf16(iota((length, 256), 1) == labc[:, 2 + kind : 3 + kind])
        where_bucket = bucket_of(iota((256, 256), 0) - iota((256, 256), 1))
        for h in range(heads):
            row = tab[(1 + kind) * heads + h : (1 + kind) * heads + h + 1, :]
            wide = jnp.broadcast_to(row, (256, 128))
            toep = jnp.concatenate(
                [
                    jnp.take_along_axis(wide, where_bucket[:, c : c + 128], axis=1)
                    for c in (0, 128)
                ],
                axis=1,
            ).astype(bf16)
            feats[h, 0:length, kind * 256 : kind * 256 + 256] = jnp.dot(
                chosen, toep, preferred_element_type=f32
            ).astype(bf16)
    lane = iota((length, 64), 1)
    mask = jnp.where(
        lane < 8,
        jnp.where(labc[:, 0:1] == lane, 0.0, NEG),
        jnp.where((lane == 8) & (labc[:, 4:5] != 1), NEG, 0.0),
    ).astype(bf16)
    for h in range(heads):
        feats[h, 0:length, 512:576] = k[:, h * 64 : h * 64 + 64]
        feats[h, 0:length, 576:640] = mask
        feats[h, length:, 0:512] = jnp.zeros((PAD, 512), bf16)
        feats[h, length:, 512:640] = jnp.where(iota((PAD, 128), 1) == 72, NEG, 0.0).astype(bf16)


def query_features(labr, first, a):
    def of(row):
        return labr[row : row + 1, pl.ds(first, BQ)]

    sub = iota((256, BQ), 0)
    a[0:256, :] = to_bf16(sub == of(2))
    a[256:512, :] = to_bf16(sub == of(3))
    low = iota((64, BQ), 0)
    a[576:640, :] = jnp.where(
        low < 8, jnp.where(of(0) == low, 1.0, 0.0), jnp.where(low == 8, 1.0, 0.0)
    ).astype(bf16)


def near_buckets(labr, labc, first, idx):
    here = labr[1:2, pl.ds(first, BQ)]
    idx[...] = bucket_of(labc[pl.ds(first, 2 * BQ), 1:2] - here)


def add_near(s_ref, tab, idx, padded, first, h, own):
    wide = jnp.broadcast_to(tab[pl.ds(h, 1), :], (TR, 128))
    for n in range(0, 2 * BQ, TR):
        rows = pl.ds(pl.multiple_of(first + n, TR), TR)
        got = jnp.concatenate(
            [
                jnp.take_along_axis(wide, idx[n : n + TR, c : c + 128], axis=1)
                for c in range(0, BQ, 128)
            ],
            axis=1,
        )
        s = s_ref[rows, :] + got
        if 128 <= n < 128 + BQ:
            same = iota((TR, BQ), 0) + (n - 128) == iota((TR, BQ), 1)
            s = jnp.where(same & padded, own, s)
        s_ref[rows, :] = s


def own_scores(own, qt, k_block, tab, heads):
    prod = qt[...].astype(f32) * k_block.T.astype(f32)
    for h in range(heads):
        zero_bias = tab[h, 0] + tab[heads + h, 0] + tab[2 * heads + h, 0]
        own[h] = jnp.broadcast_to(
            jnp.sum(prod[h * 64 : h * 64 + 64], axis=0, keepdims=True) + zero_bias, (8, BQ)
        )


def far_constant(far, qb, t, h):
    return jnp.where(t < 2 * qb - 1, far[0, h], jnp.where(t > 2 * qb + 2, far[1, h], 0.0))


def rows_max(value):
    return functools.reduce(jnp.maximum, [value[i : i + 8] for i in range(0, value.shape[0], 8)])


def rows_sum(value):
    return functools.reduce(jnp.add, [value[i : i + 8] for i in range(0, value.shape[0], 8)])


def for_each_size(count, limit, body):
    for n in range(1, limit + 1):
        if n * UNIT >= min(BQ, limit * UNIT):
            pl.when(count == n)(functools.partial(body, n))


def fwd_kernel(
    heads, far, spans, labr, labc, tab, q, k, v, mixed, ot, lse,
    feats, vt, idx, qt, own, o_all, *pairs
):
    a, s_all, p_all = (pairs[i * UNROLL : (i + 1) * UNROLL] for i in range(3))
    labr, labc, q, k, v = labr.at[0], labc.at[0], q.at[0], k.at[0], v.at[0]
    mixed, ot, lse = mixed.at[0], ot.at[0], lse.at[0]
    length = k.shape[0]
    qb = pl.program_id(1)
    first = pl.multiple_of(qb * BQ, BQ)
    block = pl.program_id(0) * pl.num_programs(1) + qb
    begin = pl.multiple_of(spans[0, block] * 128, 128)
    count = spans[1, block]

    @pl.when(qb == 0)
    def _():
        key_features(labc, tab, k, feats, heads)
        vt[:, 0:length] = v[...].T
        vt[:, length:] = jnp.zeros((heads * 64, PAD), bf16)

    for par in range(UNROLL):
        query_features(labr, first, a[par])
    near_buckets(labr, labc, first, idx)
    qt[...] = q[...].T
    own_scores(own, qt, k[pl.ds(first, BQ), :], tab, heads)
    padded = labr[4:5, pl.ds(first, BQ)] != 1

    def constant(h, row):
        return far_constant(far, qb, spans[0, block] + row // 128, h)

    def some_heads(i, n):
        size = n * UNIT
        span = pl.ds(begin, size)
        turns = [(par, i * UNROLL + par) for par in range(UNROLL)]
        rows_of = lambda row: pl.ds(pl.multiple_of(begin + PAD + row, TR), TR)
        for par, h in turns:
            a[par][512:576, :] = qt[pl.ds(pl.multiple_of(h * 64, 64), 64), :]
            s_all[par][pl.ds(begin + PAD, size), :] = jnp.dot(
                feats[h, span, :], a[par][...], preferred_element_type=f32
            )
        for par, h in turns:
            add_near(s_all[par], tab, idx, padded, first, h, own[h, 0:1, :])
        tops = []
        for par, h in turns:
            top = None
            for row in range(0, size, TR):
                here = rows_max(s_all[par][rows_of(row), :]) + constant(h, row)
                top = here if top is None else jnp.maximum(top, here)
            tops.append(jnp.max(top, axis=0, keepdims=True))
        totals = []
        for par, h in turns:
            total = jnp.zeros((8, BQ), f32)
            for row in range(0, size, TR):
                p = jnp.exp(s_all[par][rows_of(row), :] - (tops[par] - constant(h, row)))
                total = total + rows_sum(p)
                p_all[par][row : row + TR, :] = p.astype(bf16)
            totals.append(jnp.sum(total, axis=0, keepdims=True))
        for par, h in turns:
            cols = pl.ds(pl.multiple_of(h * 64, 64), 64)
            o = jnp.dot(vt[cols, span], p_all[par][0:size, :], preferred_element_type=f32)
            o_all[cols, :] = o * (1.0 / totals[par])
            lse[pl.ds(h, 1), :] = tops[par] + jnp.log(totals[par])

    def body(n):
        def step(i, _):
            some_heads(i, n)
            return 0

        lax.fori_loop(0, heads // UNROLL, step, 0)

    for_each_size(count, length // UNIT, body)
    ot[...] = o_all[...]
    mixed[...] = o_all[...].T.astype(bf16)


def bwd_kernel(
    heads, skip, far, spans, labr, labc, tab, spread, q, k, v, go, ot, lse,
    dqkv, tg,
    feats, ends, vs, acc, cxy, cp, sums, idx, into, at_here,
    qt, gt, own, delta, flipped, right, dqt, *pairs
):
    a, s_all, dp_all, pd_all = (pairs[i * UNROLL : (i + 1) * UNROLL] for i in range(4))
    labr, labc, q, k, v = labr.at[0], labc.at[0], q.at[0], k.at[0], v.at[0]
    go, ot, lse, dqkv, tg = go.at[0], ot.at[0], lse.at[0], dqkv.at[0], tg.at[0]
    length = k.shape[0]
    width = heads * 64
    tiles = length // 128
    qb = pl.program_id(1)
    first = pl.multiple_of(qb * BQ, BQ)
    block = pl.program_id(0) * pl.num_programs(1) + qb
    begin = pl.multiple_of(spans[0, block] * 128, 128)
    count = spans[1, block]

    @pl.when(qb == 0)
    def _():
        key_features(labc, tab, k, feats, heads)
        sub = iota((256, length), 0)
        ends[0:256, 0:length] = to_bf16(sub == labr[2:3, :])
        ends[256:512, 0:length] = to_bf16(sub == labr[3:4, :])
        ends[512 : 512 + width, 0:length] = k[...].T
        ends[:, length:] = jnp.zeros((512 + width, PAD), bf16)
        for h in range(heads):
            vs[h, 0:length, :] = v[:, h * 64 : h * 64 + 64]
            vs[h, length:, :] = jnp.zeros((PAD, 64), bf16)
        acc[...] = jnp.zeros_like(acc)
        cxy[...] = jnp.zeros_like(cxy)
        cp[...] = jnp.zeros_like(cp)
        sums[...] = jnp.zeros_like(sums)

    near = pl.ds(pl.multiple_of(first, 128), 2 * BQ)
    for par in range(UNROLL):
        query_features(labr, first, a[par])
        pd_all[par][near, BQ : 2 * BQ] = jnp.zeros((2 * BQ, BQ), bf16)
    near_buckets(labr, labc, first, idx)
    here_cols = labc[pl.ds(first + PAD, BQ), :]
    windows = []
    for half in (0, 1):
        lo = jnp.clip(qb * 2 + half - 1, 0, tiles - 3)
        windows.append(pl.multiple_of(lo * 128, 128))
        origin = here_cols[half * 128 : half * 128 + 1, 1:2]
        into[half] = to_bf16(
            iota((REACH, 384), 0) == labr[1:2, pl.ds(windows[half], 384)] - origin + 92
        )
        at_here[half * 128 : half * 128 + 128, :] = to_bf16(
            255 - iota((128, 256), 1) == here_cols[half * 128 : half * 128 + 128, 1:2] - origin
        )

    qt[...] = q[...].T
    gt[...] = go[...].T
    own_scores(own, qt, k[pl.ds(first, BQ), :], tab, heads)
    padded = labr[4:5, pl.ds(first, BQ)] != 1
    delta_all = gt[...].astype(f32) * ot[...]
    zeros = jnp.zeros((BQ, 64), bf16)
    for h in range(heads):
        cols = slice(h * 64, h * 64 + 64)
        delta[h] = jnp.broadcast_to(jnp.sum(delta_all[cols], axis=0, keepdims=True), (8, BQ))
        right[h, 0:BQ] = jnp.concatenate([go[:, cols], zeros], axis=1)
        right[h, BQ : 2 * BQ] = jnp.concatenate([zeros, q[:, cols]], axis=1)
    for kind in (0, 1):
        flipped[kind] = to_bf16(
            255 - iota((BQ, 256), 1) == here_cols[:, 2 + kind : 3 + kind]
        )

    def some_heads(i, n):
        size = n * UNIT
        span = pl.ds(begin, size)
        span_padded = pl.ds(pl.multiple_of(begin + PAD, 128), size)
        turns = [(par, i * UNROLL + par) for par in range(UNROLL)]
        cols_of = lambda h: pl.ds(pl.multiple_of(h * 64, 64), 64)
        for par, h in turns:
            a[par][512:576, :] = qt[cols_of(h), :]
            s_all[par][span_padded, :] = jnp.dot(
                feats[h, span, :], a[par][...], preferred_element_type=f32
            )
            dp_all[par][0:size, :] = jnp.dot(
                vs[h, span, :], gt[cols_of(h), :], preferred_element_type=f32
            )
        for par, h in turns:
            add_near(s_all[par], tab, idx, padded, first, h, own[h, 0:1, :])
        for par, h in turns:
            pd = pd_all[par]
            lse_row = lse[pl.ds(skip + h, 1), :]
            delta_row = delta[h, 0:1, :]
            every = jnp.zeros((8, BQ), f32)
            high = jnp.zeros((8, BQ), f32)
            for row in range(0, size, TR):
                t = spans[0, block] + row // 128
                rows = pl.ds(pl.multiple_of(begin + PAD + row, TR), TR)
                p = jnp.exp(s_all[par][rows, :] - (lse_row - far_constant(far, qb, t, h)))
                ds = p * (dp_all[par][row : row + TR, :] - delta_row)
                pd[rows, 0:BQ] = p.astype(bf16)
                pd[rows, BQ : 2 * BQ] = ds.astype(bf16)
                part = rows_sum(ds)
                every = every + part
                high = high + jnp.where(t >= 2 * qb + 2, part, 0.0)
            for row in range(0, BQ, TR):
                ds = pd[pl.ds(pl.multiple_of(first + PAD + row, TR), TR), BQ : 2 * BQ].astype(f32)
                high = high + rows_sum(
                    jnp.where(iota((TR, BQ), 0) + row > iota((TR, BQ), 1), ds, 0.0)
                )
            sums[h, 0:8, :] += every - high
            sums[h, 8:16, :] += high
        placed = []
        for par, h in turns:
            acc[h, span, :] += jnp.dot(
                pd_all[par][span_padded, :], right[h], preferred_element_type=f32
            )
            dst = pd_all[par][span_padded, BQ : 2 * BQ]
            dqt[cols_of(h), :] = jnp.dot(
                ends[pl.ds(pl.multiple_of(512 + h * 64, 64), 64), span],
                dst,
                preferred_element_type=f32,
            )
            placed.append(
                jnp.dot(ends[0:512, span], dst, preferred_element_type=f32).astype(bf16)
            )
        puts = []
        for par, h in turns:
            puts.append(
                jnp.concatenate(
                    [
                        jnp.dot(
                            into[half],
                            pd_all[par][
                                pl.ds(pl.multiple_of(windows[half] + PAD, 128), 384),
                                BQ + half * 128 : BQ + half * 128 + 128,
                            ],
                            preferred_element_type=f32,
                        ).astype(bf16)
                        for half in (0, 1)
                    ],
                    axis=1,
                )
            )
        for par, h in turns:
            for kind in (0, 1):
                part = slice(kind * 256, kind * 256 + 256)
                cxy[h, part, :] += jnp.dot(
                    placed[par][part], flipped[kind], preferred_element_type=f32
                )
            cp[h] += jnp.dot(puts[par], at_here[...], preferred_element_type=f32)

    def body(n):
        def step(i, _):
            some_heads(i, n)
            return 0

        lax.fori_loop(0, heads // UNROLL, step, 0)

    for_each_size(count, length // UNIT, body)
    dqkv[pl.ds(first, BQ), 0:width] = dqt[...].T.astype(bf16)

    @pl.when(qb == pl.num_programs(1) - 1)
    def _():
        for h in range(0, heads, 2):
            one, two = acc[h, 0:length, :], acc[h + 1, 0:length, :]
            dqkv[:, width + h * 64 : width + h * 64 + 128] = jnp.concatenate(
                [one[:, 64:], two[:, 64:]], axis=1
            ).astype(bf16)
            dqkv[:, 2 * width + h * 64 : 2 * width + h * 64 + 128] = jnp.concatenate(
                [one[:, :64], two[:, :64]], axis=1
            ).astype(bf16)
        lines = []
        for kind in (0, 1, 2):
            for h in range(heads):
                c = cp[h] if kind == 0 else cxy[h, (kind - 1) * 256 : kind * 256, :]
                c = jnp.concatenate([c, jnp.zeros_like(c)], axis=1)
                c = pltpu.roll(c, 0, 1, stride=1, stride_axis=0)
                lines.append(jnp.sum(c, axis=0, keepdims=True))
        rel = jnp.dot(
            jnp.concatenate(lines[:heads], axis=0),
            spread[0],
            preferred_element_type=f32,
            precision=lax.Precision.HIGHEST,
        )
        box = jnp.dot(
            jnp.concatenate(lines[heads:], axis=0),
            spread[1],
            preferred_element_type=f32,
            precision=lax.Precision.HIGHEST,
        )
        lane = iota((heads, 128), 1)
        low_all = jnp.concatenate([jnp.sum(sums[h, 0:8, :]).reshape(1, 1) for h in range(heads)], axis=0)
        high_all = jnp.concatenate([jnp.sum(sums[h, 8:16, :]).reshape(1, 1) for h in range(heads)], axis=0)
        near_low = jnp.sum(jnp.where(lane < 15, rel, 0.0), axis=1, keepdims=True)
        near_high = jnp.sum(jnp.where((lane >= 16) & (lane < 31), rel, 0.0), axis=1, keepdims=True)
        rel = jnp.where(lane == 15, low_all - near_low, rel)
        rel = jnp.where(lane == 31, high_all - near_high, rel)
        tg[...] = jnp.concatenate([rel, box], axis=0)


def spread_tables():
    slot = jnp.arange(512)
    number = jnp.arange(128)
    rel_t = slot - 347
    rel = (bucket_of(rel_t)[:, None] == number[None]) & (jnp.abs(rel_t) < 91)[:, None]
    box = bucket_of(slot - 255)[:, None] == number[None]
    return jnp.stack([rel, box]).astype(f32)


def key_spans(segments):
    starts = segments[:, ::BQ]
    ends = segments[:, BQ - 1 :: BQ]
    lo = jnp.sum(segments[:, None, :] < starts[:, :, None], axis=2) // 128
    hi = jnp.sum(segments[:, None, :] <= ends[:, :, None], axis=2)
    count = (hi - lo * 128 + UNIT - 1) // UNIT
    return jnp.stack([lo.reshape(-1), count.reshape(-1)]).astype(jnp.int32)


def label_arrays(segments, positions, boxes, pad_mask):
    zero = jnp.zeros_like(segments)
    labr = jnp.stack([segments, positions, boxes[0], boxes[1], pad_mask, zero, zero, zero], axis=1)
    return labr, jnp.pad(jnp.swapaxes(labr, 1, 2), ((0, 0), (PAD, PAD), (0, 0)))


def table_rows(tables):
    kinds, _, heads = tables.shape
    rows = jnp.swapaxes(tables, 1, 2).reshape(kinds * heads, NB).astype(f32)
    far = jnp.stack([tables[0, 15], tables[0, 31]]).astype(f32)
    return jnp.pad(rows, ((0, 0), (0, 128 - NB))), far


def cost(flops, nbytes):
    return pl.CostEstimate(flops=flops, bytes_accessed=nbytes, transcendentals=0)


def attention_forward(qkv, spans, labr, labc, tab, far):
    rows, length, wide = qkv.shape
    width = wide // 3
    heads = width // 64
    steps = length // BQ
    smem = pl.BlockSpec(memory_space=pltpu.SMEM)
    return pl.pallas_call(
        functools.partial(fwd_kernel, heads),
        out_shape=(
            jax.ShapeDtypeStruct((rows, length, width), bf16),
            jax.ShapeDtypeStruct((rows, width, length), f32),
            jax.ShapeDtypeStruct((rows, 8, length), f32),
        ),
        grid=(rows, steps),
        in_specs=[
            smem,
            smem,
            pl.BlockSpec((1, 8, length), lambda r, i: (r, 0, 0)),
            pl.BlockSpec((1, length + 2 * PAD, 8), lambda r, i: (r, 0, 0)),
            pl.BlockSpec(tab.shape, lambda r, i: (0, 0)),
            pl.BlockSpec((1, BQ, width), lambda r, i: (r, i, 0)),
            pl.BlockSpec((1, length, width), lambda r, i: (r, 0, 1)),
            pl.BlockSpec((1, length, width), lambda r, i: (r, 0, 2)),
        ],
        out_specs=(
            pl.BlockSpec((1, BQ, width), lambda r, i: (r, i, 0)),
            pl.BlockSpec((1, width, BQ), lambda r, i: (r, 0, i)),
            pl.BlockSpec((1, 8, BQ), lambda r, i: (r, 0, i)),
        ),
        scratch_shapes=[
            pltpu.VMEM((heads, length + PAD, 640), bf16),
            pltpu.VMEM((width, length + PAD), bf16),
            pltpu.VMEM((512, BQ), jnp.int32),
            pltpu.VMEM((width, BQ), bf16),
            pltpu.VMEM((heads, 8, BQ), f32),
            pltpu.VMEM((width, BQ), f32),
            *[pltpu.VMEM((640, BQ), bf16)] * UNROLL,
            *[pltpu.VMEM((length + 2 * PAD, BQ), f32)] * UNROLL,
            *[pltpu.VMEM((length, BQ), bf16)] * UNROLL,
        ],
        compiler_params=pltpu.CompilerParams(vmem_limit_bytes=59 << 20),
        cost_estimate=cost(rows * heads * length * length * 4000, rows * length * wide * 4),
    )(far, spans, labr, labc, tab, qkv, qkv, qkv)


def attention_backward(qkv, spans, labr, labc, tables, go, ot, lse, part, parts):
    rows, length, wide = qkv.shape
    wide = wide // parts
    width = wide // 3
    count = tables.shape[2] // parts
    tab, far = table_rows(tables[:, :, part * count : (part + 1) * count])
    heads = width // 64
    steps = length // BQ
    spread = spread_tables()
    smem = pl.BlockSpec(memory_space=pltpu.SMEM)
    return pl.pallas_call(
        functools.partial(bwd_kernel, heads, part * heads),
        out_shape=(
            jax.ShapeDtypeStruct((rows, length, wide), bf16),
            jax.ShapeDtypeStruct((rows, 3 * heads, 128), f32),
        ),
        grid=(rows, steps),
        in_specs=[
            smem,
            smem,
            pl.BlockSpec((1, 8, length), lambda r, i: (r, 0, 0)),
            pl.BlockSpec((1, length + 2 * PAD, 8), lambda r, i: (r, 0, 0)),
            pl.BlockSpec(tab.shape, lambda r, i: (0, 0)),
            pl.BlockSpec(spread.shape, lambda r, i: (0, 0, 0)),
            pl.BlockSpec((1, BQ, width), lambda r, i: (r, i, part)),
            pl.BlockSpec((1, length, width), lambda r, i: (r, 0, parts + part)),
            pl.BlockSpec((1, length, width), lambda r, i: (r, 0, 2 * parts + part)),
            pl.BlockSpec((1, BQ, width), lambda r, i: (r, i, part)),
            pl.BlockSpec((1, width, BQ), lambda r, i: (r, part, i)),
            pl.BlockSpec((1, 8, BQ), lambda r, i: (r, 0, i)),
        ],
        out_specs=(
            pl.BlockSpec((1, length, wide), lambda r, i: (r, 0, 0)),
            pl.BlockSpec((1, 3 * heads, 128), lambda r, i: (r, 0, 0)),
        ),
        scratch_shapes=[
            pltpu.VMEM((heads, length + PAD, 640), bf16),
            pltpu.VMEM((512 + width, length + PAD), bf16),
            pltpu.VMEM((heads, length + PAD, 64), bf16),
            pltpu.VMEM((heads, length + PAD, 128), f32),
            pltpu.VMEM((heads, 512, 256), f32),
            pltpu.VMEM((heads, REACH, 256), f32),
            pltpu.VMEM((heads, 16, BQ), f32),
            pltpu.VMEM((512, BQ), jnp.int32),
            pltpu.VMEM((2, REACH, 384), bf16),
            pltpu.VMEM((BQ, 256), bf16),
            pltpu.VMEM((width, BQ), bf16),
            pltpu.VMEM((width, BQ), bf16),
            pltpu.VMEM((heads, 8, BQ), f32),
            pltpu.VMEM((heads, 8, BQ), f32),
            pltpu.VMEM((2, BQ, 256), bf16),
            pltpu.VMEM((heads, 2 * BQ, 128), bf16),
            pltpu.VMEM((width, BQ), f32),
            *[pltpu.VMEM((640, BQ), bf16)] * UNROLL,
            *[pltpu.VMEM((length + 2 * PAD, BQ), f32)] * UNROLL,
            *[pltpu.VMEM((length, BQ), f32)] * UNROLL,
            *[pltpu.VMEM((length + 2 * PAD, 2 * BQ), bf16)] * UNROLL,
        ],
        compiler_params=pltpu.CompilerParams(vmem_limit_bytes=59 << 20),
        cost_estimate=cost(rows * heads * length * length * 8500, rows * length * wide * 6),
    )(far, spans, labr, labc, tab, spread, qkv, qkv, qkv, go, ot, lse)


epsilon = 1e-06
gelu_coefficient = 0.7978845608028654
CHUNKS = 2


def dot_nt(one, two):
    return lax.dot_general(one, two, (((1,), (1,)), ((), ())), preferred_element_type=f32)


def dot_nn(one, two):
    return jnp.dot(one, two, preferred_element_type=f32)


def ffn_kernel(slots, n2_own, n2_other, og_own, og_other, *refs):
    weights = refs[:slots]
    down, down_send, n2g, n2g_send, *terms = refs[slots : 2 * slots + 4]
    wt, gate, up, hg, hid, dgate, dup, down_sum, n2g_sum, n2, og, n2t, ogt, sems, stage, out_sems = refs[2 * slots + 4 :]
    slices, kinds, wide, lanes = weights[0].shape
    whole_lanes = lanes % 128 == 0
    slot = pl.program_id(0)

    def fetch(j, c, d):
        return pltpu.make_async_copy(
            weights[j].at[d, c],
            wt.at[j, c, :, pl.ds(d * lanes, lanes)],
            sems.at[j, c, d],
        )

    @pl.when(slot == 0)
    def _():
        for j in range(slots):
            for c in range(kinds):
                for d in range(slices):
                    if whole_lanes:
                        fetch(j, c, d).start()
                    else:
                        wt[j, c, :, d * lanes : (d + 1) * lanes] = weights[j][d, c]
        half = n2_own.shape[0]
        n2[:half, :] = n2_own[...]
        n2[half:, :] = n2_other[...]
        og[:half, :] = og_own[...]
        og[half:, :] = og_other[...]
        n2t[...] = n2[...].T
        ogt[...] = og[...].T

    if whole_lanes:
        for j in range(slots):

            @pl.when(slot == j)
            def _():
                for c in range(kinds):
                    for d in range(slices):
                        fetch(j, c, d).wait()

    gate[...] = dot_nn(wt[slot, 0], n2t[...])
    up[...] = dot_nn(wt[slot, 1], n2t[...])
    hg[...] = dot_nn(wt[slot, 2], ogt[...])

    def chunk(c, _):
        rows = pl.ds(pl.multiple_of(c * 16, 16), 16)
        g, u, back = gate[rows, :], up[rows, :], hg[rows, :]
        square = g * g
        t = jnp.tanh(gelu_coefficient * (g + 0.044715 * square * g))
        mid = 0.5 * (1.0 + t)
        act = g * mid
        slope = mid + 0.5 * g * (1.0 - t * t) * (gelu_coefficient * (1.0 + 0.134145 * square))
        hid[rows, :] = (act * u).astype(bf16)
        dgate[rows, :] = (back * u * slope).astype(bf16)
        dup[rows, :] = (back * act).astype(bf16)
        return 0

    lax.fori_loop(0, wide // 16, chunk, 0, unroll=CHUNKS)
    n2g_all = dot_nn(dgate[...].T, wt[slot, 0]) + dot_nn(dup[...].T, wt[slot, 1])
    down_all = dot_nn(hid[...].T, wt[slot, 2])

    @pl.when(slot == 0)
    def _():
        n2g_sum[...] = n2g_all
        down_sum[...] = down_all

    @pl.when(slot > 0)
    def _():
        n2g_sum[...] += n2g_all
        down_sum[...] += down_all

    for c, (one, two) in enumerate(((dgate, n2), (dup, n2), (hid, og))):
        term = dot_nn(one[...], two[...]).astype(bf16)
        for d in range(slices):
            stage[slot, d, c] = term[:, d * lanes : (d + 1) * lanes]

    def hand_out(j):
        return pltpu.make_async_copy(stage.at[j], terms[j], out_sems.at[j])

    for j in range(slots):

        @pl.when(slot == j)
        def _():
            hand_out(j).start()

    @pl.when(slot == pl.num_programs(0) - 1)
    def _():
        part = n2.shape[0] // 2
        n2g[...] = n2g_sum[:part, :]
        n2g_send[...] = n2g_sum[part:, :].astype(bf16)
        down[...] = down_sum[:part, :]
        down_send[...] = down_sum[part:, :].astype(bf16)
        for j in range(slots):
            hand_out(j).wait()


def ffn(n2_own, n2_other, og_own, og_other, weights):
    tokens, depth = 2 * n2_own.shape[0], n2_own.shape[1]
    slots = len(weights)
    slices, kinds, wide, lanes = weights[0].shape
    terms = jax.ShapeDtypeStruct((slices, kinds, wide, lanes), bf16)
    if lanes % 128 == 0:
        source = pl.BlockSpec(memory_space=pl.ANY)
    else:
        source = pl.BlockSpec(
            weights[0].shape, lambda i: (0, 0, 0, 0), pipeline_mode=pl.Buffered(1)
        )
    whole = lambda shape: pl.BlockSpec(shape, lambda i: (0,) * len(shape))
    own = jax.ShapeDtypeStruct((tokens // 2, depth), f32)
    send = jax.ShapeDtypeStruct((tokens // 2, depth), bf16)
    return pl.pallas_call(
        functools.partial(ffn_kernel, slots),
        out_shape=(own, send, own, send) + (terms,) * slots,
        grid=(slots,),
        in_specs=[whole(n2_own.shape)] * 4 + [source] * slots,
        out_specs=(whole(own.shape),) * 4
        + (pl.BlockSpec(memory_space=pl.ANY),) * slots,
        scratch_shapes=[
            pltpu.VMEM((slots, kinds, wide, depth), bf16),
            *[pltpu.VMEM((wide, tokens), f32)] * 3,
            *[pltpu.VMEM((wide, tokens), bf16)] * 3,
            *[pltpu.VMEM((tokens, depth), f32)] * 2,
            *[pltpu.VMEM((tokens, depth), bf16)] * 2,
            *[pltpu.VMEM((depth, tokens), bf16)] * 2,
            pltpu.SemaphoreType.DMA((slots, kinds, slices)),
            pltpu.VMEM((slots, slices, kinds, wide, lanes), bf16),
            pltpu.SemaphoreType.DMA((slots,)),
        ],
        compiler_params=pltpu.CompilerParams(vmem_limit_bytes=59 << 20),
        cost_estimate=cost(
            20 * slots * tokens * depth * wide, 4 * slots * weights[0].size + 8 * tokens * depth
        ),
    )(n2_own, n2_other, og_own, og_other, *weights)


def whole_blocks(arrays):
    return [pl.BlockSpec(a.shape, lambda i, n=len(a.shape): (0,) * n) for a in arrays]


def project_kernel(count, here, *refs):
    blocks, (w, qkv, kept) = refs[:count], refs[count:]
    for k in range(count):

        @pl.when(pl.program_id(0) == k)
        def _():
            kept[...] = blocks[k][...]
            qkv[...] = dot_nn(blocks[k][...], w[...]).astype(bf16)


def project(here, blocks, w):
    count = len(blocks)
    part, depth = blocks[0].shape
    wide = w.shape[1]
    whole = lambda shape: pl.BlockSpec(shape, lambda k, here: (0, 0))
    placed = lambda width: pl.BlockSpec((part, width), lambda k, here: (here[0] ^ k, 0))
    return pl.pallas_call(
        functools.partial(project_kernel, count),
        out_shape=(
            jax.ShapeDtypeStruct((count * part, wide), bf16),
            jax.ShapeDtypeStruct((count * part, depth), bf16),
        ),
        grid_spec=pltpu.PrefetchScalarGridSpec(
            num_scalar_prefetch=1,
            grid=(count,),
            in_specs=[whole((part, depth))] * count + [whole(w.shape)],
            out_specs=(placed(wide), placed(depth)),
        ),
        compiler_params=pltpu.CompilerParams(vmem_limit_bytes=40 << 20),
        cost_estimate=cost(2 * count * part * depth * wide, 2 * depth * wide + 4 * count * part * depth),
    )(here, *blocks, w)


def join_kernel(count, me, *refs):
    parts, (half, other, x, gain, mixed, middle, n2, w) = refs[:count], refs[count:]
    for k in range(count):
        mixed[:, k * parts[0].shape[1] : (k + 1) * parts[0].shape[1]] = parts[k][...]
    slices, rows, _ = half.shape
    for j in range(slices):
        for low, source in enumerate((half, other)):
            at = me[0] ^ (2 * j + low)
            w[pl.ds(pl.multiple_of(at * rows, rows), rows), :] = source[j]
    total = x[...].astype(f32) + dot_nt(mixed[...], w[...])
    middle[...] = total
    scale = lax.rsqrt(jnp.mean(total * total, axis=1, keepdims=True) + epsilon)
    n2[...] = (total * scale * gain[...]).astype(bf16)


def join(me, parts, half, other, x, gain):
    count = len(parts)
    part, width = parts[0].shape
    depth = x.shape[1]
    outs = (
        jax.ShapeDtypeStruct((part, count * width), bf16),
        jax.ShapeDtypeStruct((part, depth), f32),
        jax.ShapeDtypeStruct((part, depth), bf16),
        jax.ShapeDtypeStruct((depth, count * width), bf16),
    )
    return pl.pallas_call(
        functools.partial(join_kernel, count),
        out_shape=outs,
        grid=(1,),
        in_specs=[pl.BlockSpec(memory_space=pltpu.SMEM)]
        + whole_blocks([*parts, half, other, x, gain]),
        out_specs=tuple(whole_blocks(outs)),
        compiler_params=pltpu.CompilerParams(vmem_limit_bytes=59 << 20),
        cost_estimate=cost(4 * part * half.size, 8 * half.size + 12 * part * depth),
    )(me, *parts, half, other, x, gain)


def store_halves(core, term, keep, send):
    slices, rows, _ = keep.shape
    for j in range(slices):
        low = term[2 * j * rows : (2 * j + 1) * rows]
        high = term[(2 * j + 1) * rows : (2 * j + 2) * rows]
        keep[j] = jnp.where(core == 0, low, high).astype(bf16)
        send[j] = jnp.where(core == 0, high, low).astype(bf16)


def split_kernel(count, core, own, other, middle, og, gain, mixed, w, *refs):
    middle_grad, keep, send = refs[:3]
    outs = refs[3:]
    total = middle[...]
    scale = lax.rsqrt(jnp.mean(total * total, axis=1, keepdims=True) + epsilon)
    a = (own[...] + other[...].astype(f32)) * gain[...]
    grad = (
        og[...].astype(f32)
        + scale * a
        - total * (scale * scale * scale) * jnp.mean(a * total, axis=1, keepdims=True)
    )
    middle_grad[...] = grad
    low = grad.astype(bf16)
    back = dot_nn(low, w[...]).astype(bf16)
    width = outs[0].shape[1]
    for k in range(count):
        outs[k][...] = back[:, k * width : (k + 1) * width]
    store_halves(core[0], dot_nn(low.T, mixed[...]), keep, send)


def split(core, own, other, middle, og, gain, mixed, w, count, dp):
    part, depth = middle.shape
    columns = w.shape[1]
    slices = (dp // 2, depth // dp, columns)
    outs = (
        jax.ShapeDtypeStruct((part, depth), f32),
        jax.ShapeDtypeStruct(slices, bf16),
        jax.ShapeDtypeStruct(slices, bf16),
    ) + (jax.ShapeDtypeStruct((part, columns // count), bf16),) * count
    return pl.pallas_call(
        functools.partial(split_kernel, count),
        out_shape=outs,
        grid=(1,),
        in_specs=[pl.BlockSpec(memory_space=pltpu.SMEM)]
        + whole_blocks([own, other, middle, og, gain, mixed, w]),
        out_specs=tuple(whole_blocks(outs)),
        compiler_params=pltpu.CompilerParams(vmem_limit_bytes=59 << 20),
        cost_estimate=cost(4 * part * w.size, 10 * w.size + 16 * part * depth),
    )(core, own, other, middle, og, gain, mixed, w)


def part_columns(w, part, parts):
    width = w.shape[1] // 3
    size = width // parts
    return [slice(c * width + part * size, c * width + (part + 1) * size) for c in range(3)]


def finish_kernel(count, parts, here, *refs):
    grads, w, outs = refs[:parts], refs[parts], refs[parts + 1 :]
    total = None
    for part in range(parts):
        columns = jnp.concatenate([w[:, at] for at in part_columns(w, part, parts)], axis=1)
        term = dot_nt(grads[part][...], columns)
        total = term if total is None else total + term
    for j, out in enumerate(outs):

        @pl.when(pl.program_id(0) == j)
        def _():
            out[...] = total.astype(out.dtype)


def finish(here, grads, w, count):
    parts = len(grads)
    length, wide = grads[0].shape
    depth = w.shape[0]
    rows = length // count
    whole = lambda shape: pl.BlockSpec(shape, lambda k, here: (0,) * len(shape))
    return pl.pallas_call(
        functools.partial(finish_kernel, count, parts),
        out_shape=(jax.ShapeDtypeStruct((rows, depth), f32),)
        + (jax.ShapeDtypeStruct((rows, depth), bf16),) * (count - 1),
        grid_spec=pltpu.PrefetchScalarGridSpec(
            num_scalar_prefetch=1,
            grid=(count,),
            in_specs=[pl.BlockSpec((rows, wide), lambda k, here: (here[0] ^ k, 0))] * parts
            + [whole(w.shape)],
            out_specs=(whole((rows, depth)),) * count,
        ),
        compiler_params=pltpu.CompilerParams(vmem_limit_bytes=40 << 20),
        cost_estimate=cost(2 * length * w.size, 2 * w.size + 4 * length * depth),
    )(here, *grads, w)


def weight_kernel(parts, core, *refs):
    grads, (kept, tables, keep, send) = refs[:parts], refs[parts:]
    slices, rows, _ = keep.shape
    rows -= 16
    turned = kept[...].T
    for part in range(parts):
        term = dot_nn(turned, grads[part][...])
        size = term.shape[1] // 3
        for c, at in enumerate(part_columns(keep.at[0], part, parts)):
            columns = pl.ds(at.start, size)
            store_halves(
                core[0],
                term[:, c * size : (c + 1) * size],
                keep.at[:, pl.ds(0, rows), columns],
                send.at[:, pl.ds(0, rows), columns],
            )
    count = tables.shape[0]
    number = NB // (2 * slices)
    for j in range(slices):
        low = tables[:, 2 * j * number : (2 * j + 1) * number]
        high = tables[:, (2 * j + 1) * number : (2 * j + 2) * number]
        keep[j, rows:, :] = jnp.zeros((16, keep.shape[2]), bf16)
        send[j, rows:, :] = jnp.zeros((16, keep.shape[2]), bf16)
        keep[j, rows : rows + count, 0:number] = jnp.where(core[0] == 0, low, high).astype(bf16)
        send[j, rows : rows + count, 0:number] = jnp.where(core[0] == 0, high, low).astype(bf16)


def weight_term(core, grads, kept, tables, dp):
    parts = len(grads)
    wide, depth = parts * grads[0].shape[1], kept.shape[1]
    slices = (dp // 2, depth // dp + 16, wide)
    outs = (jax.ShapeDtypeStruct(slices, bf16),) * 2
    return pl.pallas_call(
        functools.partial(weight_kernel, parts),
        out_shape=outs,
        grid=(1,),
        in_specs=[pl.BlockSpec(memory_space=pltpu.SMEM)] + whole_blocks([*grads, kept, tables]),
        out_specs=tuple(whole_blocks(outs)),
        compiler_params=pltpu.CompilerParams(vmem_limit_bytes=40 << 20),
        cost_estimate=cost(2 * kept.size * wide, 8 * depth * wide + 4 * kept.size),
    )(core, *grads, kept, tables)


def bits_of(size):
    return [1 << b for b in reversed(range(size.bit_length() - 1))]


def swap(value, axis, size, distance):
    return lax.ppermute(value, axis, [(j, j ^ distance) for j in range(size)])


def after(value, *others):
    return lax.optimization_barrier((value,) + others)[0]


def scatter_begin(parts, size, bits, first):
    held = {k: [v] for k, v in parts.items()}
    total = lambda terms: sum(v.astype(f32) for v in terms)
    for b in reversed(bits[1:]):
        arrived = []
        for k in sorted([k for k in held if not k & b], reverse=True):
            send = total(held.pop(k | b)).astype(bf16)
            if k == 0 and arrived:
                send = after(send, *arrived)
            arrived.append(swap(send, ("mq", "mr"), size, b))
            held[k].append(arrived[-1])
    *early, newest = held[bits[0]]
    return held[0], total(early + [(after(newest, *first) if first else newest)]).astype(bf16)


def join_pair(own, other, b, axis):
    low = (lax.axis_index("dp") // b) % 2 == 0
    pair = (jnp.where(low, own, other), jnp.where(low, other, own))
    return jnp.concatenate(pair, axis=axis)


def halve(whole, b):
    pairs = whole.reshape((whole.shape[0] // 2, 2) + whole.shape[1:])
    mine = (lax.axis_index("dp") // b) % 2
    kept = lax.dynamic_index_in_dim(pairs, mine, 1, keepdims=False)
    sent = lax.dynamic_index_in_dim(pairs, 1 - mine, 1, keepdims=False)
    return kept, sent.astype(bf16)


def scatter_dp(kept, sent, size, b, ahead=()):
    while True:
        other = swap(sent, "dp", size, b)
        other = after(other, *ahead) if ahead else other
        whole = kept.astype(f32) + other.astype(f32)
        b, ahead = 2 * b, ()
        if b >= size:
            return whole.reshape(whole.shape[1:])
        kept, sent = halve(whole, b)


def on_device(
    dp,
    mp,
    inputs,
    segments,
    positions,
    boxes,
    pad_mask,
    w_qkv,
    w_out,
    w_gate_up,
    w_down,
    bias_tables,
    gains,
    out_grad,
):
    gain_values = gains.astype(f32)
    here = lax.axis_index(("mq", "mr"))
    me = lax.axis_index("dp")
    here_ref = here.astype(jnp.int32).reshape(1)
    me_ref = me.astype(jnp.int32).reshape(1)
    core_ref = (me % 2).astype(jnp.int32).reshape(1)
    rows, part, depth = inputs.shape
    width = w_out.shape[0]
    heads = width // 64
    slice_rows = w_qkv.shape[1]
    wide = w_down.shape[0]
    all_bits = bits_of(mp)
    near_bit = 1
    x = inputs.reshape(part, depth)
    og_own = out_grad.reshape(part, depth)

    def trade(blocks):
        return [blocks[0]] + [swap(blocks[k], ("mq", "mr"), mp, k) for k in range(1, mp)]

    wqkv_own = jnp.concatenate([w_qkv[c] for c in range(3)], axis=1)
    wqkv = lax.all_gather(wqkv_own, "dp", axis=0, tiled=True)
    wide_x = x.astype(f32)
    scale_one = lax.rsqrt(jnp.mean(wide_x * wide_x, axis=1, keepdims=True) + epsilon)
    n1 = {0: (wide_x * scale_one * gain_values[0:1]).astype(bf16)}
    wo_held = {0: w_out.T}
    for b in all_bits:
        for k in list(wo_held):
            wo_held[k ^ b] = swap(wo_held[k], ("mq", "mr"), mp, b)
    wo_half = jnp.concatenate([wo_held[k] for k in range(mp)], axis=1)
    for b in all_bits:
        for k in list(n1):
            send = after(n1[k], wo_half) if k else n1[k]
            n1[k ^ b] = swap(send, ("mq", "mr"), mp, b)
    wo_half = wo_half[None]
    chip_bits = [1 << j for j in range(1, dp.bit_length() - 1)]
    for b in chip_bits[:-1]:
        wo_half = jnp.concatenate([wo_half, swap(wo_half, "dp", dp, b)], axis=0)
    packed = jnp.concatenate([jnp.swapaxes(w_gate_up, 1, 2), w_down[None]], axis=0)
    packs = {0: packed.reshape(3 * wide, slice_rows)}

    labr, labc = label_arrays(segments, positions, boxes, pad_mask)
    tab, far = table_rows(bias_tables)
    spans = key_spans(segments)
    qkv, normed_one = project(
        here_ref, [n1[k] for k in range(mp)], after(wqkv, wo_half)
    )
    qkv = qkv.reshape(rows, mp * part, 3 * width)
    for b in all_bits[:-1]:
        for k in list(packs):
            packs[k ^ b] = swap(after(packs[k], n1[mp - 1]), ("mq", "mr"), mp, b)
    og_other = swap(after(og_own, n1[mp - 1]), ("mq", "mr"), mp, near_bit)
    wo_other = swap(wo_half, "dp", dp, chip_bits[-1])
    mixed, ot, lse = attention_forward(qkv, spans, labr, labc, tab, far)
    mixed_rows = mixed.reshape(mp * part, width)
    mixed_in = trade(
        [lax.dynamic_slice_in_dim(mixed_rows, (here ^ k) * part, part, 0) for k in range(mp)]
    )
    wo_half = jnp.concatenate([wo_half, after(wo_other, *mixed_in[1:])], axis=0)
    wo_other = swap(wo_half, "dp", dp, 1)
    ffn_w = []
    for k, v in packs.items():
        ahead = (mixed,) if k else ()
        v = lax.all_gather(after(v, *ahead) if k else v, "dp", axis=0, tiled=True)
        ffn_w.append(v.reshape(dp, 3, wide, slice_rows))
    mixed_all, middle, normed_two, wo = join(
        me_ref, mixed_in, wo_half, wo_other, x, gain_values[1:2]
    )

    n2_other = swap(normed_two, ("mq", "mr"), mp, near_bit)
    down, down_send, n2g, n2g_send, *ffn_terms = ffn(
        normed_two, n2_other, og_own, og_other, ffn_w
    )
    n2g_other = swap(n2g_send, ("mq", "mr"), mp, near_bit)
    terms = {}
    for k, term in zip(packs, ffn_terms):
        term = term if k else after(term, n2g_other)
        terms[k] = lax.psum_scatter(
            term.reshape(-1, slice_rows), "dp", scatter_dimension=0, tiled=True
        )

    split_out = split(
        core_ref,
        n2g,
        n2g_other,
        middle,
        og_own,
        gain_values[1:2],
        mixed_all,
        wo,
        mp,
        dp,
    )
    middle_grad, out_keep, out_send = split_out[:3]
    out_whole = out_keep.astype(f32) + swap(out_send, "dp", dp, 1).astype(f32)
    out_kept, out_sent = halve(out_whole, 2)
    go_in = trade(list(split_out[3:]))
    go_in = jnp.stack(go_in[:1] + [after(v, out_sent) for v in go_in[1:]])
    go = jnp.concatenate(
        [lax.dynamic_index_in_dim(go_in, here ^ m, 0, keepdims=False) for m in range(mp)], axis=0
    )
    go, down_send, out_sent = lax.optimization_barrier((go, down_send, out_sent))
    down_other = swap(down_send, ("mq", "mr"), mp, near_bit)
    out_other = swap(out_sent, "dp", dp, 2)
    go = go.reshape(rows, mp * part, width)
    halves = 2 if width % 256 == 0 else 1
    back = functools.partial(attention_backward, qkv, spans, labr, labc, bias_tables)
    dqkv, tg = zip(back(go, ot, lse, 0, halves))
    far_sums = {k: v for k, v in terms.items() if k}
    if halves == 2:
        go = after(go, dqkv[0], down_other, out_other, *far_sums.values())
        second = back(go, ot, lse, 1, halves)
        dqkv, tg = dqkv + second[:1], tg + second[1:]
    w_grad = {0: terms[0], **far_sums}
    for b in reversed(all_bits[:-1]):
        for k in [k for k in w_grad if k and not k & b and k | b in w_grad]:
            w_grad[k] = w_grad[k].astype(f32) + swap(
                w_grad.pop(k | b).astype(bf16), ("mq", "mr"), mp, b
            ).astype(f32)
    far_other = [
        swap(v.astype(bf16), ("mq", "mr"), mp, k) for k, v in w_grad.items() if k
    ]
    dqkv = lax.optimization_barrier(tuple(dqkv) + (down_other, out_other) + tuple(far_other))
    far_other = dqkv[halves + 2 :]
    dqkv = [v.reshape(mp * part, -1) for v in dqkv[:halves]]
    parts = finish(here_ref, dqkv, wqkv, mp)
    tg = jnp.sum(jnp.stack(tg), axis=1).reshape(halves, 3, heads // halves, 128)
    tg = jnp.swapaxes(tg, 0, 1).reshape(3 * heads, 128)
    own_terms, last_send = scatter_begin(dict(enumerate(parts)), mp, all_bits, ())
    qkv_keep, qkv_send = weight_term(
        core_ref, [after(v, parts[-1]) for v in dqkv], normed_one, tg, dp
    )
    qkv_whole = qkv_keep.astype(f32) + swap(qkv_send, "dp", dp, 1).astype(f32)
    out_whole = out_kept.astype(f32) + after(out_other, qkv_whole).astype(f32)
    out_sum = scatter_dp(*halve(out_whole, 4), dp, 4)
    last = swap(last_send, ("mq", "mr"), mp, all_bits[0])
    qkv_kept, qkv_sent = halve(qkv_whole, 2)
    qkv_sum = scatter_dp(qkv_kept, qkv_sent, dp, 2, (last_send,))
    qkv_sum, own_sum = lax.optimization_barrier((qkv_sum, terms[0]))
    table_sum = qkv_sum[slice_rows : slice_rows + 3 * heads, : NB // dp]
    qkv_sum = qkv_sum[:slice_rows]
    out = (middle + down + after(down_other, last_send).astype(f32)).astype(bf16)
    qkv_out = jnp.stack([qkv_sum[:, c * width : (c + 1) * width] for c in range(3)])
    w_grad = own_sum.astype(f32) + sum(v.astype(f32) for v in far_other)
    w_grad = lax.optimization_barrier(w_grad.reshape(3, wide, slice_rows))
    gate_up_out = jnp.swapaxes(w_grad[:2], 1, 2)
    down_out = w_grad[2]
    table_out = jnp.swapaxes(table_sum.reshape(3, heads, NB // dp), 1, 2)

    own_gains = lax.dynamic_slice_in_dim(gain_values, me * slice_rows, slice_rows, 1)
    products = jnp.stack(
        [
            jnp.sum(qkv_sum * wqkv_own.astype(f32), axis=1),
            jnp.sum(gate_up_out * w_gate_up.astype(f32), axis=(0, 2)),
        ]
    )
    products = (products / own_gains).reshape(2, mp, slice_rows // mp)
    products = jnp.stack(
        [lax.dynamic_index_in_dim(products, here ^ k, 1, keepdims=False) for k in range(mp)], axis=1
    )
    products = jnp.pad(products, ((0, 14), (0, 0), (0, width - slice_rows // mp)))
    sums = jnp.concatenate([out_sum, products.reshape(16, mp * width)], axis=0).astype(bf16)
    sums = trade([sums[:, k * width : (k + 1) * width] for k in range(mp)])
    sums = sum(v.astype(f32) for v in sums)
    sums, last = lax.optimization_barrier((sums, last))
    n1g = sum(v.astype(f32) for v in own_terms + [last])
    a = n1g * gain_values[0:1]
    input_grad = (
        middle_grad
        + scale_one * a
        - wide_x
        * (scale_one * scale_one * scale_one)
        * jnp.mean(a * wide_x, axis=1, keepdims=True)
    ).astype(bf16)
    out_out = sums[:slice_rows].T
    gain_out = sums[slice_rows : slice_rows + 2, : slice_rows // mp]
    shape = inputs.shape
    return (
        out.reshape(shape),
        input_grad.reshape(shape),
        qkv_out,
        out_out,
        gate_up_out,
        down_out,
        table_out,
        gain_out,
    )


def solution(mesh):
    dp, mp = mesh.shape["dp"], mesh.shape["mp"]
    split_mesh = jax.sharding.Mesh(mesh.devices.reshape(dp, mp // 2, 2), ("dp", "mq", "mr"))
    both = ("mq", "mr")
    placed = (
        P("dp", both, None),
        P("dp", None),
        P("dp", None),
        P(None, "dp", None),
        P("dp", None),
        P(None, "dp", both),
        P(both, "dp"),
        P(None, "dp", both),
        P(both, "dp"),
        P(None, None, both),
        P(),
        P("dp", both, None),
    )
    return jax.shard_map(
        functools.partial(on_device, dp, mp),
        mesh=split_mesh,
        in_specs=placed,
        out_specs=(
            P("dp", both, None),
            P("dp", both, None),
            P(None, "dp", both),
            P(both, "dp"),
            P(None, "dp", both),
            P(both, "dp"),
            P(None, "dp", both),
            P(None, ("dp", "mq", "mr")),
        ),
        check_vma=False,
    )
```

```python
import functools
import jax
import jax.numpy as jnp
from jax import lax
from jax.experimental import pallas as pl
from jax.experimental.pallas import tpu as pltpu
from jax.sharding import PartitionSpec as P

NB = 32
thresholds = (12, 16, 23, 32, 46, 64, 91)
BQ = 256
PAD = 128
REACH = 448
TR = 64
UNIT = 256
UNROLL = 2
NEG = -1e30
bf16 = jnp.bfloat16
f32 = jnp.float32


def bucket_of(distance):
    magnitude = jnp.abs(distance)
    stepped = 8 + sum(((magnitude >= boundary).astype(jnp.int32) for boundary in thresholds))
    return jnp.where(magnitude < 8, magnitude, stepped) + 16 * (distance > 0).astype(jnp.int32)


def iota(shape, axis):
    return lax.broadcasted_iota(jnp.int32, shape, axis)


def to_bf16(mask):
    return jnp.where(mask, 1.0, 0.0).astype(bf16)


def key_features(labc_padded, tab, k, feats, heads):
    length = k.shape[0]
    labc = labc_padded[PAD : PAD + length, :]
    for kind in (0, 1):
        chosen = to_bf16(iota((length, 256), 1) == labc[:, 2 + kind : 3 + kind])
        where_bucket = bucket_of(iota((256, 256), 0) - iota((256, 256), 1))
        for h in range(heads):
            row = tab[(1 + kind) * heads + h : (1 + kind) * heads + h + 1, :]
            wide = jnp.broadcast_to(row, (256, 128))
            toep = jnp.concatenate(
                [
                    jnp.take_along_axis(wide, where_bucket[:, c : c + 128], axis=1)
                    for c in (0, 128)
                ],
                axis=1,
            ).astype(bf16)
            feats[h, 0:length, kind * 256 : kind * 256 + 256] = jnp.dot(
                chosen, toep, preferred_element_type=f32
            ).astype(bf16)
    lane = iota((length, 64), 1)
    mask = jnp.where(
        lane < 8,
        jnp.where(labc[:, 0:1] == lane, 0.0, NEG),
        jnp.where((lane == 8) & (labc[:, 4:5] != 1), NEG, 0.0),
    ).astype(bf16)
    for h in range(heads):
        feats[h, 0:length, 512:576] = k[:, h * 64 : h * 64 + 64]
        feats[h, 0:length, 576:640] = mask
        feats[h, length:, 0:512] = jnp.zeros((PAD, 512), bf16)
        feats[h, length:, 512:640] = jnp.where(iota((PAD, 128), 1) == 72, NEG, 0.0).astype(bf16)


def query_features(labr, first, a):
    def of(row):
        return labr[row : row + 1, pl.ds(first, BQ)]

    sub = iota((256, BQ), 0)
    a[0:256, :] = to_bf16(sub == of(2))
    a[256:512, :] = to_bf16(sub == of(3))
    low = iota((64, BQ), 0)
    a[576:640, :] = jnp.where(
        low < 8, jnp.where(of(0) == low, 1.0, 0.0), jnp.where(low == 8, 1.0, 0.0)
    ).astype(bf16)


def near_buckets(labr, labc, first, idx):
    here = labr[1:2, pl.ds(first, BQ)]
    idx[...] = bucket_of(labc[pl.ds(first, 2 * BQ), 1:2] - here)


def add_near(s_ref, tab, idx, padded, first, h, own):
    wide = jnp.broadcast_to(tab[pl.ds(h, 1), :], (TR, 128))
    for n in range(0, 2 * BQ, TR):
        rows = pl.ds(pl.multiple_of(first + n, TR), TR)
        got = jnp.concatenate(
            [
                jnp.take_along_axis(wide, idx[n : n + TR, c : c + 128], axis=1)
                for c in range(0, BQ, 128)
            ],
            axis=1,
        )
        s = s_ref[rows, :] + got
        if 128 <= n < 128 + BQ:
            same = iota((TR, BQ), 0) + (n - 128) == iota((TR, BQ), 1)
            s = jnp.where(same & padded, own, s)
        s_ref[rows, :] = s


def own_scores(own, qt, k_block, tab, heads):
    prod = qt[...].astype(f32) * k_block.T.astype(f32)
    for h in range(heads):
        zero_bias = tab[h, 0] + tab[heads + h, 0] + tab[2 * heads + h, 0]
        own[h] = jnp.broadcast_to(
            jnp.sum(prod[h * 64 : h * 64 + 64], axis=0, keepdims=True) + zero_bias, (8, BQ)
        )


def far_constant(far, qb, t, h):
    return jnp.where(t < 2 * qb - 1, far[0, h], jnp.where(t > 2 * qb + 2, far[1, h], 0.0))


def rows_max(value):
    return functools.reduce(jnp.maximum, [value[i : i + 8] for i in range(0, value.shape[0], 8)])


def rows_sum(value):
    return functools.reduce(jnp.add, [value[i : i + 8] for i in range(0, value.shape[0], 8)])


def for_each_size(count, limit, body):
    for n in range(1, limit + 1):
        if n * UNIT >= min(BQ, limit * UNIT):
            pl.when(count == n)(functools.partial(body, n))


def fwd_kernel(
    heads, far, spans, labr, labc, tab, q, k, v, mixed, ot, lse,
    feats, vt, idx, qt, own, o_all, *pairs
):
    a, s_all, p_all = (pairs[i * UNROLL : (i + 1) * UNROLL] for i in range(3))
    labr, labc, q, k, v = labr.at[0], labc.at[0], q.at[0], k.at[0], v.at[0]
    mixed, ot, lse = mixed.at[0], ot.at[0], lse.at[0]
    length = k.shape[0]
    qb = pl.program_id(1)
    first = pl.multiple_of(qb * BQ, BQ)
    block = pl.program_id(0) * pl.num_programs(1) + qb
    begin = pl.multiple_of(spans[0, block] * 128, 128)
    count = spans[1, block]

    @pl.when(qb == 0)
    def _():
        key_features(labc, tab, k, feats, heads)
        vt[:, 0:length] = v[...].T
        vt[:, length:] = jnp.zeros((heads * 64, PAD), bf16)

    for par in range(UNROLL):
        query_features(labr, first, a[par])
    near_buckets(labr, labc, first, idx)
    qt[...] = q[...].T
    own_scores(own, qt, k[pl.ds(first, BQ), :], tab, heads)
    padded = labr[4:5, pl.ds(first, BQ)] != 1

    def constant(h, row):
        return far_constant(far, qb, spans[0, block] + row // 128, h)

    def some_heads(i, n):
        size = n * UNIT
        span = pl.ds(begin, size)
        turns = [(par, i * UNROLL + par) for par in range(UNROLL)]
        rows_of = lambda row: pl.ds(pl.multiple_of(begin + PAD + row, TR), TR)
        for par, h in turns:
            a[par][512:576, :] = qt[pl.ds(pl.multiple_of(h * 64, 64), 64), :]
            s_all[par][pl.ds(begin + PAD, size), :] = jnp.dot(
                feats[h, span, :], a[par][...], preferred_element_type=f32
            )
        for par, h in turns:
            add_near(s_all[par], tab, idx, padded, first, h, own[h, 0:1, :])
        tops = []
        for par, h in turns:
            top = None
            for row in range(0, size, TR):
                here = rows_max(s_all[par][rows_of(row), :]) + constant(h, row)
                top = here if top is None else jnp.maximum(top, here)
            tops.append(jnp.max(top, axis=0, keepdims=True))
        totals = []
        for par, h in turns:
            total = jnp.zeros((8, BQ), f32)
            for row in range(0, size, TR):
                p = jnp.exp(s_all[par][rows_of(row), :] - (tops[par] - constant(h, row)))
                total = total + rows_sum(p)
                p_all[par][row : row + TR, :] = p.astype(bf16)
            totals.append(jnp.sum(total, axis=0, keepdims=True))
        for par, h in turns:
            cols = pl.ds(pl.multiple_of(h * 64, 64), 64)
            o = jnp.dot(vt[cols, span], p_all[par][0:size, :], preferred_element_type=f32)
            o_all[cols, :] = o * (1.0 / totals[par])
            lse[pl.ds(h, 1), :] = tops[par] + jnp.log(totals[par])

    def body(n):
        def step(i, _):
            some_heads(i, n)
            return 0

        lax.fori_loop(0, heads // UNROLL, step, 0)

    for_each_size(count, length // UNIT, body)
    ot[...] = o_all[...]
    mixed[...] = o_all[...].T.astype(bf16)


def bwd_kernel(
    heads, skip, far, spans, labr, labc, tab, spread, q, k, v, go, ot, lse,
    dqkv, tg,
    feats, ends, vs, acc, cxy, cp, sums, idx, into, at_here,
    qt, gt, own, delta, flipped, right, dqt, *pairs
):
    a, s_all, dp_all, pd_all = (pairs[i * UNROLL : (i + 1) * UNROLL] for i in range(4))
    labr, labc, q, k, v = labr.at[0], labc.at[0], q.at[0], k.at[0], v.at[0]
    go, ot, lse, dqkv, tg = go.at[0], ot.at[0], lse.at[0], dqkv.at[0], tg.at[0]
    length = k.shape[0]
    width = heads * 64
    tiles = length // 128
    qb = pl.program_id(1)
    first = pl.multiple_of(qb * BQ, BQ)
    block = pl.program_id(0) * pl.num_programs(1) + qb
    begin = pl.multiple_of(spans[0, block] * 128, 128)
    count = spans[1, block]

    @pl.when(qb == 0)
    def _():
        key_features(labc, tab, k, feats, heads)
        sub = iota((256, length), 0)
        ends[0:256, 0:length] = to_bf16(sub == labr[2:3, :])
        ends[256:512, 0:length] = to_bf16(sub == labr[3:4, :])
        ends[512 : 512 + width, 0:length] = k[...].T
        ends[:, length:] = jnp.zeros((512 + width, PAD), bf16)
        for h in range(heads):
            vs[h, 0:length, :] = v[:, h * 64 : h * 64 + 64]
            vs[h, length:, :] = jnp.zeros((PAD, 64), bf16)
        acc[...] = jnp.zeros_like(acc)
        cxy[...] = jnp.zeros_like(cxy)
        cp[...] = jnp.zeros_like(cp)
        sums[...] = jnp.zeros_like(sums)

    near = pl.ds(pl.multiple_of(first, 128), 2 * BQ)
    for par in range(UNROLL):
        query_features(labr, first, a[par])
        pd_all[par][near, BQ : 2 * BQ] = jnp.zeros((2 * BQ, BQ), bf16)
    near_buckets(labr, labc, first, idx)
    here_cols = labc[pl.ds(first + PAD, BQ), :]
    windows = []
    for half in (0, 1):
        lo = jnp.clip(qb * 2 + half - 1, 0, tiles - 3)
        windows.append(pl.multiple_of(lo * 128, 128))
        origin = here_cols[half * 128 : half * 128 + 1, 1:2]
        into[half] = to_bf16(
            iota((REACH, 384), 0) == labr[1:2, pl.ds(windows[half], 384)] - origin + 92
        )
        at_here[half * 128 : half * 128 + 128, :] = to_bf16(
            255 - iota((128, 256), 1) == here_cols[half * 128 : half * 128 + 128, 1:2] - origin
        )

    qt[...] = q[...].T
    gt[...] = go[...].T
    own_scores(own, qt, k[pl.ds(first, BQ), :], tab, heads)
    padded = labr[4:5, pl.ds(first, BQ)] != 1
    delta_all = gt[...].astype(f32) * ot[...]
    zeros = jnp.zeros((BQ, 64), bf16)
    for h in range(heads):
        cols = slice(h * 64, h * 64 + 64)
        delta[h] = jnp.broadcast_to(jnp.sum(delta_all[cols], axis=0, keepdims=True), (8, BQ))
        right[h, 0:BQ] = jnp.concatenate([go[:, cols], zeros], axis=1)
        right[h, BQ : 2 * BQ] = jnp.concatenate([zeros, q[:, cols]], axis=1)
    for kind in (0, 1):
        flipped[kind] = to_bf16(
            255 - iota((BQ, 256), 1) == here_cols[:, 2 + kind : 3 + kind]
        )

    def some_heads(i, n):
        size = n * UNIT
        span = pl.ds(begin, size)
        span_padded = pl.ds(pl.multiple_of(begin + PAD, 128), size)
        turns = [(par, i * UNROLL + par) for par in range(UNROLL)]
        cols_of = lambda h: pl.ds(pl.multiple_of(h * 64, 64), 64)
        for par, h in turns:
            a[par][512:576, :] = qt[cols_of(h), :]
            s_all[par][span_padded, :] = jnp.dot(
                feats[h, span, :], a[par][...], preferred_element_type=f32
            )
            dp_all[par][0:size, :] = jnp.dot(
                vs[h, span, :], gt[cols_of(h), :], preferred_element_type=f32
            )
        for par, h in turns:
            add_near(s_all[par], tab, idx, padded, first, h, own[h, 0:1, :])
        for par, h in turns:
            pd = pd_all[par]
            lse_row = lse[pl.ds(skip + h, 1), :]
            delta_row = delta[h, 0:1, :]
            every = jnp.zeros((8, BQ), f32)
            high = jnp.zeros((8, BQ), f32)
            for row in range(0, size, TR):
                t = spans[0, block] + row // 128
                rows = pl.ds(pl.multiple_of(begin + PAD + row, TR), TR)
                p = jnp.exp(s_all[par][rows, :] - (lse_row - far_constant(far, qb, t, h)))
                ds = p * (dp_all[par][row : row + TR, :] - delta_row)
                pd[rows, 0:BQ] = p.astype(bf16)
                pd[rows, BQ : 2 * BQ] = ds.astype(bf16)
                part = rows_sum(ds)
                every = every + part
                high = high + jnp.where(t >= 2 * qb + 2, part, 0.0)
            for row in range(0, BQ, TR):
                ds = pd[pl.ds(pl.multiple_of(first + PAD + row, TR), TR), BQ : 2 * BQ].astype(f32)
                high = high + rows_sum(
                    jnp.where(iota((TR, BQ), 0) + row > iota((TR, BQ), 1), ds, 0.0)
                )
            sums[h, 0:8, :] += every - high
            sums[h, 8:16, :] += high
        placed = []
        for par, h in turns:
            acc[h, span, :] += jnp.dot(
                pd_all[par][span_padded, :], right[h], preferred_element_type=f32
            )
            dst = pd_all[par][span_padded, BQ : 2 * BQ]
            dqt[cols_of(h), :] = jnp.dot(
                ends[pl.ds(pl.multiple_of(512 + h * 64, 64), 64), span],
                dst,
                preferred_element_type=f32,
            )
            placed.append(
                jnp.dot(ends[0:512, span], dst, preferred_element_type=f32).astype(bf16)
            )
        puts = []
        for par, h in turns:
            puts.append(
                jnp.concatenate(
                    [
                        jnp.dot(
                            into[half],
                            pd_all[par][
                                pl.ds(pl.multiple_of(windows[half] + PAD, 128), 384),
                                BQ + half * 128 : BQ + half * 128 + 128,
                            ],
                            preferred_element_type=f32,
                        ).astype(bf16)
                        for half in (0, 1)
                    ],
                    axis=1,
                )
            )
        for par, h in turns:
            for kind in (0, 1):
                part = slice(kind * 256, kind * 256 + 256)
                cxy[h, part, :] += jnp.dot(
                    placed[par][part], flipped[kind], preferred_element_type=f32
                )
            cp[h] += jnp.dot(puts[par], at_here[...], preferred_element_type=f32)

    def body(n):
        def step(i, _):
            some_heads(i, n)
            return 0

        lax.fori_loop(0, heads // UNROLL, step, 0)

    for_each_size(count, length // UNIT, body)
    dqkv[pl.ds(first, BQ), 0:width] = dqt[...].T.astype(bf16)

    @pl.when(qb == pl.num_programs(1) - 1)
    def _():
        for h in range(0, heads, 2):
            one, two = acc[h, 0:length, :], acc[h + 1, 0:length, :]
            dqkv[:, width + h * 64 : width + h * 64 + 128] = jnp.concatenate(
                [one[:, 64:], two[:, 64:]], axis=1
            ).astype(bf16)
            dqkv[:, 2 * width + h * 64 : 2 * width + h * 64 + 128] = jnp.concatenate(
                [one[:, :64], two[:, :64]], axis=1
            ).astype(bf16)
        lines = []
        for kind in (0, 1, 2):
            for h in range(heads):
                c = cp[h] if kind == 0 else cxy[h, (kind - 1) * 256 : kind * 256, :]
                c = jnp.concatenate([c, jnp.zeros_like(c)], axis=1)
                c = pltpu.roll(c, 0, 1, stride=1, stride_axis=0)
                lines.append(jnp.sum(c, axis=0, keepdims=True))
        rel = jnp.dot(
            jnp.concatenate(lines[:heads], axis=0),
            spread[0],
            preferred_element_type=f32,
            precision=lax.Precision.HIGHEST,
        )
        box = jnp.dot(
            jnp.concatenate(lines[heads:], axis=0),
            spread[1],
            preferred_element_type=f32,
            precision=lax.Precision.HIGHEST,
        )
        lane = iota((heads, 128), 1)
        low_all = jnp.concatenate([jnp.sum(sums[h, 0:8, :]).reshape(1, 1) for h in range(heads)], axis=0)
        high_all = jnp.concatenate([jnp.sum(sums[h, 8:16, :]).reshape(1, 1) for h in range(heads)], axis=0)
        near_low = jnp.sum(jnp.where(lane < 15, rel, 0.0), axis=1, keepdims=True)
        near_high = jnp.sum(jnp.where((lane >= 16) & (lane < 31), rel, 0.0), axis=1, keepdims=True)
        rel = jnp.where(lane == 15, low_all - near_low, rel)
        rel = jnp.where(lane == 31, high_all - near_high, rel)
        tg[...] = jnp.concatenate([rel, box], axis=0)


def spread_tables():
    slot = jnp.arange(512)
    number = jnp.arange(128)
    rel_t = slot - 347
    rel = (bucket_of(rel_t)[:, None] == number[None]) & (jnp.abs(rel_t) < 91)[:, None]
    box = bucket_of(slot - 255)[:, None] == number[None]
    return jnp.stack([rel, box]).astype(f32)


def key_spans(segments):
    starts = segments[:, ::BQ]
    ends = segments[:, BQ - 1 :: BQ]
    lo = jnp.sum(segments[:, None, :] < starts[:, :, None], axis=2) // 128
    hi = jnp.sum(segments[:, None, :] <= ends[:, :, None], axis=2)
    count = (hi - lo * 128 + UNIT - 1) // UNIT
    return jnp.stack([lo.reshape(-1), count.reshape(-1)]).astype(jnp.int32)


def label_arrays(segments, positions, boxes, pad_mask):
    zero = jnp.zeros_like(segments)
    labr = jnp.stack([segments, positions, boxes[0], boxes[1], pad_mask, zero, zero, zero], axis=1)
    return labr, jnp.pad(jnp.swapaxes(labr, 1, 2), ((0, 0), (PAD, PAD), (0, 0)))


def table_rows(tables):
    kinds, _, heads = tables.shape
    rows = jnp.swapaxes(tables, 1, 2).reshape(kinds * heads, NB).astype(f32)
    far = jnp.stack([tables[0, 15], tables[0, 31]]).astype(f32)
    return jnp.pad(rows, ((0, 0), (0, 128 - NB))), far


def cost(flops, nbytes):
    return pl.CostEstimate(flops=flops, bytes_accessed=nbytes, transcendentals=0)


def attention_forward(qkv, spans, labr, labc, tab, far):
    rows, length, wide = qkv.shape
    width = wide // 3
    heads = width // 64
    steps = length // BQ
    smem = pl.BlockSpec(memory_space=pltpu.SMEM)
    return pl.pallas_call(
        functools.partial(fwd_kernel, heads),
        out_shape=(
            jax.ShapeDtypeStruct((rows, length, width), bf16),
            jax.ShapeDtypeStruct((rows, width, length), f32),
            jax.ShapeDtypeStruct((rows, 8, length), f32),
        ),
        grid=(rows, steps),
        in_specs=[
            smem,
            smem,
            pl.BlockSpec((1, 8, length), lambda r, i: (r, 0, 0)),
            pl.BlockSpec((1, length + 2 * PAD, 8), lambda r, i: (r, 0, 0)),
            pl.BlockSpec(tab.shape, lambda r, i: (0, 0)),
            pl.BlockSpec((1, BQ, width), lambda r, i: (r, i, 0)),
            pl.BlockSpec((1, length, width), lambda r, i: (r, 0, 1)),
            pl.BlockSpec((1, length, width), lambda r, i: (r, 0, 2)),
        ],
        out_specs=(
            pl.BlockSpec((1, BQ, width), lambda r, i: (r, i, 0)),
            pl.BlockSpec((1, width, BQ), lambda r, i: (r, 0, i)),
            pl.BlockSpec((1, 8, BQ), lambda r, i: (r, 0, i)),
        ),
        scratch_shapes=[
            pltpu.VMEM((heads, length + PAD, 640), bf16),
            pltpu.VMEM((width, length + PAD), bf16),
            pltpu.VMEM((512, BQ), jnp.int32),
            pltpu.VMEM((width, BQ), bf16),
            pltpu.VMEM((heads, 8, BQ), f32),
            pltpu.VMEM((width, BQ), f32),
            *[pltpu.VMEM((640, BQ), bf16)] * UNROLL,
            *[pltpu.VMEM((length + 2 * PAD, BQ), f32)] * UNROLL,
            *[pltpu.VMEM((length, BQ), bf16)] * UNROLL,
        ],
        compiler_params=pltpu.CompilerParams(vmem_limit_bytes=59 << 20),
        cost_estimate=cost(rows * heads * length * length * 4000, rows * length * wide * 4),
    )(far, spans, labr, labc, tab, qkv, qkv, qkv)


def attention_backward(qkv, spans, labr, labc, tables, go, ot, lse, part, parts):
    rows, length, wide = qkv.shape
    wide = wide // parts
    width = wide // 3
    count = tables.shape[2] // parts
    tab, far = table_rows(tables[:, :, part * count : (part + 1) * count])
    heads = width // 64
    steps = length // BQ
    spread = spread_tables()
    smem = pl.BlockSpec(memory_space=pltpu.SMEM)
    return pl.pallas_call(
        functools.partial(bwd_kernel, heads, part * heads),
        out_shape=(
            jax.ShapeDtypeStruct((rows, length, wide), bf16),
            jax.ShapeDtypeStruct((rows, 3 * heads, 128), f32),
        ),
        grid=(rows, steps),
        in_specs=[
            smem,
            smem,
            pl.BlockSpec((1, 8, length), lambda r, i: (r, 0, 0)),
            pl.BlockSpec((1, length + 2 * PAD, 8), lambda r, i: (r, 0, 0)),
            pl.BlockSpec(tab.shape, lambda r, i: (0, 0)),
            pl.BlockSpec(spread.shape, lambda r, i: (0, 0, 0)),
            pl.BlockSpec((1, BQ, width), lambda r, i: (r, i, part)),
            pl.BlockSpec((1, length, width), lambda r, i: (r, 0, parts + part)),
            pl.BlockSpec((1, length, width), lambda r, i: (r, 0, 2 * parts + part)),
            pl.BlockSpec((1, BQ, width), lambda r, i: (r, i, part)),
            pl.BlockSpec((1, width, BQ), lambda r, i: (r, part, i)),
            pl.BlockSpec((1, 8, BQ), lambda r, i: (r, 0, i)),
        ],
        out_specs=(
            pl.BlockSpec((1, length, wide), lambda r, i: (r, 0, 0)),
            pl.BlockSpec((1, 3 * heads, 128), lambda r, i: (r, 0, 0)),
        ),
        scratch_shapes=[
            pltpu.VMEM((heads, length + PAD, 640), bf16),
            pltpu.VMEM((512 + width, length + PAD), bf16),
            pltpu.VMEM((heads, length + PAD, 64), bf16),
            pltpu.VMEM((heads, length + PAD, 128), f32),
            pltpu.VMEM((heads, 512, 256), f32),
            pltpu.VMEM((heads, REACH, 256), f32),
            pltpu.VMEM((heads, 16, BQ), f32),
            pltpu.VMEM((512, BQ), jnp.int32),
            pltpu.VMEM((2, REACH, 384), bf16),
            pltpu.VMEM((BQ, 256), bf16),
            pltpu.VMEM((width, BQ), bf16),
            pltpu.VMEM((width, BQ), bf16),
            pltpu.VMEM((heads, 8, BQ), f32),
            pltpu.VMEM((heads, 8, BQ), f32),
            pltpu.VMEM((2, BQ, 256), bf16),
            pltpu.VMEM((heads, 2 * BQ, 128), bf16),
            pltpu.VMEM((width, BQ), f32),
            *[pltpu.VMEM((640, BQ), bf16)] * UNROLL,
            *[pltpu.VMEM((length + 2 * PAD, BQ), f32)] * UNROLL,
            *[pltpu.VMEM((length, BQ), f32)] * UNROLL,
            *[pltpu.VMEM((length + 2 * PAD, 2 * BQ), bf16)] * UNROLL,
        ],
        compiler_params=pltpu.CompilerParams(vmem_limit_bytes=59 << 20),
        cost_estimate=cost(rows * heads * length * length * 8500, rows * length * wide * 6),
    )(far, spans, labr, labc, tab, spread, qkv, qkv, qkv, go, ot, lse)


epsilon = 1e-06
gelu_coefficient = 0.7978845608028654
CHUNKS = 2


def dot_nt(one, two):
    return lax.dot_general(one, two, (((1,), (1,)), ((), ())), preferred_element_type=f32)


def dot_nn(one, two):
    return jnp.dot(one, two, preferred_element_type=f32)


def ffn_kernel(slots, n2_own, n2_other, og_own, og_other, *refs):
    weights = refs[:slots]
    down, down_send, n2g, n2g_send, *terms = refs[slots : 2 * slots + 4]
    wt, gate, up, hg, hid, dgate, dup, down_sum, n2g_sum, n2, og, n2t, ogt, sems, stage, out_sems = refs[2 * slots + 4 :]
    slices, kinds, wide, lanes = weights[0].shape
    whole_lanes = lanes % 128 == 0
    slot = pl.program_id(0)

    def fetch(j, c, d):
        return pltpu.make_async_copy(
            weights[j].at[d, c],
            wt.at[j, c, :, pl.ds(d * lanes, lanes)],
            sems.at[j, c, d],
        )

    @pl.when(slot == 0)
    def _():
        for j in range(slots):
            for c in range(kinds):
                for d in range(slices):
                    if whole_lanes:
                        fetch(j, c, d).start()
                    else:
                        wt[j, c, :, d * lanes : (d + 1) * lanes] = weights[j][d, c]
        half = n2_own.shape[0]
        n2[:half, :] = n2_own[...]
        n2[half:, :] = n2_other[...]
        og[:half, :] = og_own[...]
        og[half:, :] = og_other[...]
        n2t[...] = n2[...].T
        ogt[...] = og[...].T

    if whole_lanes:
        for j in range(slots):

            @pl.when(slot == j)
            def _():
                for c in range(kinds):
                    for d in range(slices):
                        fetch(j, c, d).wait()

    gate[...] = dot_nn(wt[slot, 0], n2t[...])
    up[...] = dot_nn(wt[slot, 1], n2t[...])
    hg[...] = dot_nn(wt[slot, 2], ogt[...])

    def chunk(c, _):
        rows = pl.ds(pl.multiple_of(c * 16, 16), 16)
        g, u, back = gate[rows, :], up[rows, :], hg[rows, :]
        square = g * g
        t = jnp.tanh(gelu_coefficient * (g + 0.044715 * square * g))
        mid = 0.5 * (1.0 + t)
        act = g * mid
        slope = mid + 0.5 * g * (1.0 - t * t) * (gelu_coefficient * (1.0 + 0.134145 * square))
        hid[rows, :] = (act * u).astype(bf16)
        dgate[rows, :] = (back * u * slope).astype(bf16)
        dup[rows, :] = (back * act).astype(bf16)
        return 0

    lax.fori_loop(0, wide // 16, chunk, 0, unroll=CHUNKS)
    n2g_all = dot_nn(dgate[...].T, wt[slot, 0]) + dot_nn(dup[...].T, wt[slot, 1])
    down_all = dot_nn(hid[...].T, wt[slot, 2])

    @pl.when(slot == 0)
    def _():
        n2g_sum[...] = n2g_all
        down_sum[...] = down_all

    @pl.when(slot > 0)
    def _():
        n2g_sum[...] += n2g_all
        down_sum[...] += down_all

    for c, (one, two) in enumerate(((dgate, n2), (dup, n2), (hid, og))):
        term = dot_nn(one[...], two[...]).astype(bf16)
        for d in range(slices):
            stage[slot, d, c] = term[:, d * lanes : (d + 1) * lanes]

    def hand_out(j):
        return pltpu.make_async_copy(stage.at[j], terms[j], out_sems.at[j])

    for j in range(slots):

        @pl.when(slot == j)
        def _():
            hand_out(j).start()

    @pl.when(slot == pl.num_programs(0) - 1)
    def _():
        part = n2.shape[0] // 2
        n2g[...] = n2g_sum[:part, :]
        n2g_send[...] = n2g_sum[part:, :].astype(bf16)
        down[...] = down_sum[:part, :]
        down_send[...] = down_sum[part:, :].astype(bf16)
        for j in range(slots):
            hand_out(j).wait()


def ffn(n2_own, n2_other, og_own, og_other, weights):
    tokens, depth = 2 * n2_own.shape[0], n2_own.shape[1]
    slots = len(weights)
    slices, kinds, wide, lanes = weights[0].shape
    terms = jax.ShapeDtypeStruct((slices, kinds, wide, lanes), bf16)
    if lanes % 128 == 0:
        source = pl.BlockSpec(memory_space=pl.ANY)
    else:
        source = pl.BlockSpec(
            weights[0].shape, lambda i: (0, 0, 0, 0), pipeline_mode=pl.Buffered(1)
        )
    whole = lambda shape: pl.BlockSpec(shape, lambda i: (0,) * len(shape))
    own = jax.ShapeDtypeStruct((tokens // 2, depth), f32)
    send = jax.ShapeDtypeStruct((tokens // 2, depth), bf16)
    return pl.pallas_call(
        functools.partial(ffn_kernel, slots),
        out_shape=(own, send, own, send) + (terms,) * slots,
        grid=(slots,),
        in_specs=[whole(n2_own.shape)] * 4 + [source] * slots,
        out_specs=(whole(own.shape),) * 4
        + (pl.BlockSpec(memory_space=pl.ANY),) * slots,
        scratch_shapes=[
            pltpu.VMEM((slots, kinds, wide, depth), bf16),
            *[pltpu.VMEM((wide, tokens), f32)] * 3,
            *[pltpu.VMEM((wide, tokens), bf16)] * 3,
            *[pltpu.VMEM((tokens, depth), f32)] * 2,
            *[pltpu.VMEM((tokens, depth), bf16)] * 2,
            *[pltpu.VMEM((depth, tokens), bf16)] * 2,
            pltpu.SemaphoreType.DMA((slots, kinds, slices)),
            pltpu.VMEM((slots, slices, kinds, wide, lanes), bf16),
            pltpu.SemaphoreType.DMA((slots,)),
        ],
        compiler_params=pltpu.CompilerParams(vmem_limit_bytes=59 << 20),
        cost_estimate=cost(
            20 * slots * tokens * depth * wide, 4 * slots * weights[0].size + 8 * tokens * depth
        ),
    )(n2_own, n2_other, og_own, og_other, *weights)


def whole_blocks(arrays):
    return [pl.BlockSpec(a.shape, lambda i, n=len(a.shape): (0,) * n) for a in arrays]


def project_kernel(count, here, *refs):
    blocks, (w, qkv, kept) = refs[:count], refs[count:]
    for k in range(count):

        @pl.when(pl.program_id(0) == k)
        def _():
            kept[...] = blocks[k][...]
            qkv[...] = dot_nn(blocks[k][...], w[...]).astype(bf16)


def project(here, blocks, w):
    count = len(blocks)
    part, depth = blocks[0].shape
    wide = w.shape[1]
    whole = lambda shape: pl.BlockSpec(shape, lambda k, here: (0, 0))
    placed = lambda width: pl.BlockSpec((part, width), lambda k, here: (here[0] ^ k, 0))
    return pl.pallas_call(
        functools.partial(project_kernel, count),
        out_shape=(
            jax.ShapeDtypeStruct((count * part, wide), bf16),
            jax.ShapeDtypeStruct((count * part, depth), bf16),
        ),
        grid_spec=pltpu.PrefetchScalarGridSpec(
            num_scalar_prefetch=1,
            grid=(count,),
            in_specs=[whole((part, depth))] * count + [whole(w.shape)],
            out_specs=(placed(wide), placed(depth)),
        ),
        compiler_params=pltpu.CompilerParams(vmem_limit_bytes=40 << 20),
        cost_estimate=cost(2 * count * part * depth * wide, 2 * depth * wide + 4 * count * part * depth),
    )(here, *blocks, w)


def join_kernel(count, me, *refs):
    parts, (half, other, x, gain, mixed, middle, n2, w) = refs[:count], refs[count:]
    for k in range(count):
        mixed[:, k * parts[0].shape[1] : (k + 1) * parts[0].shape[1]] = parts[k][...]
    slices, rows, _ = half.shape
    for j in range(slices):
        for low, source in enumerate((half, other)):
            at = me[0] ^ (2 * j + low)
            w[pl.ds(pl.multiple_of(at * rows, rows), rows), :] = source[j]
    total = x[...].astype(f32) + dot_nt(mixed[...], w[...])
    middle[...] = total
    scale = lax.rsqrt(jnp.mean(total * total, axis=1, keepdims=True) + epsilon)
    n2[...] = (total * scale * gain[...]).astype(bf16)


def join(me, parts, half, other, x, gain):
    count = len(parts)
    part, width = parts[0].shape
    depth = x.shape[1]
    outs = (
        jax.ShapeDtypeStruct((part, count * width), bf16),
        jax.ShapeDtypeStruct((part, depth), f32),
        jax.ShapeDtypeStruct((part, depth), bf16),
        jax.ShapeDtypeStruct((depth, count * width), bf16),
    )
    return pl.pallas_call(
        functools.partial(join_kernel, count),
        out_shape=outs,
        grid=(1,),
        in_specs=[pl.BlockSpec(memory_space=pltpu.SMEM)]
        + whole_blocks([*parts, half, other, x, gain]),
        out_specs=tuple(whole_blocks(outs)),
        compiler_params=pltpu.CompilerParams(vmem_limit_bytes=59 << 20),
        cost_estimate=cost(4 * part * half.size, 8 * half.size + 12 * part * depth),
    )(me, *parts, half, other, x, gain)


def store_halves(core, term, keep, send):
    slices, rows, _ = keep.shape
    for j in range(slices):
        low = term[2 * j * rows : (2 * j + 1) * rows]
        high = term[(2 * j + 1) * rows : (2 * j + 2) * rows]
        keep[j] = jnp.where(core == 0, low, high).astype(bf16)
        send[j] = jnp.where(core == 0, high, low).astype(bf16)


def split_kernel(count, core, own, other, middle, og, gain, mixed, w, *refs):
    middle_grad, keep, send = refs[:3]
    outs = refs[3:]
    total = middle[...]
    scale = lax.rsqrt(jnp.mean(total * total, axis=1, keepdims=True) + epsilon)
    a = (own[...] + other[...].astype(f32)) * gain[...]
    grad = (
        og[...].astype(f32)
        + scale * a
        - total * (scale * scale * scale) * jnp.mean(a * total, axis=1, keepdims=True)
    )
    middle_grad[...] = grad
    low = grad.astype(bf16)
    back = dot_nn(low, w[...]).astype(bf16)
    width = outs[0].shape[1]
    for k in range(count):
        outs[k][...] = back[:, k * width : (k + 1) * width]
    store_halves(core[0], dot_nn(low.T, mixed[...]), keep, send)


def split(core, own, other, middle, og, gain, mixed, w, count, dp):
    part, depth = middle.shape
    columns = w.shape[1]
    slices = (dp // 2, depth // dp, columns)
    outs = (
        jax.ShapeDtypeStruct((part, depth), f32),
        jax.ShapeDtypeStruct(slices, bf16),
        jax.ShapeDtypeStruct(slices, bf16),
    ) + (jax.ShapeDtypeStruct((part, columns // count), bf16),) * count
    return pl.pallas_call(
        functools.partial(split_kernel, count),
        out_shape=outs,
        grid=(1,),
        in_specs=[pl.BlockSpec(memory_space=pltpu.SMEM)]
        + whole_blocks([own, other, middle, og, gain, mixed, w]),
        out_specs=tuple(whole_blocks(outs)),
        compiler_params=pltpu.CompilerParams(vmem_limit_bytes=59 << 20),
        cost_estimate=cost(4 * part * w.size, 10 * w.size + 16 * part * depth),
    )(core, own, other, middle, og, gain, mixed, w)


def part_columns(w, part, parts):
    width = w.shape[1] // 3
    size = width // parts
    return [slice(c * width + part * size, c * width + (part + 1) * size) for c in range(3)]


def finish_kernel(count, parts, here, *refs):
    grads, w, outs = refs[:parts], refs[parts], refs[parts + 1 :]
    total = None
    for part in range(parts):
        columns = jnp.concatenate([w[:, at] for at in part_columns(w, part, parts)], axis=1)
        term = dot_nt(grads[part][...], columns)
        total = term if total is None else total + term
    for j, out in enumerate(outs):

        @pl.when(pl.program_id(0) == j)
        def _():
            out[...] = total.astype(out.dtype)


def finish(here, grads, w, count):
    parts = len(grads)
    length, wide = grads[0].shape
    depth = w.shape[0]
    rows = length // count
    whole = lambda shape: pl.BlockSpec(shape, lambda k, here: (0,) * len(shape))
    return pl.pallas_call(
        functools.partial(finish_kernel, count, parts),
        out_shape=(jax.ShapeDtypeStruct((rows, depth), f32),)
        + (jax.ShapeDtypeStruct((rows, depth), bf16),) * (count - 1),
        grid_spec=pltpu.PrefetchScalarGridSpec(
            num_scalar_prefetch=1,
            grid=(count,),
            in_specs=[pl.BlockSpec((rows, wide), lambda k, here: (here[0] ^ k, 0))] * parts
            + [whole(w.shape)],
            out_specs=(whole((rows, depth)),) * count,
        ),
        compiler_params=pltpu.CompilerParams(vmem_limit_bytes=40 << 20),
        cost_estimate=cost(2 * length * w.size, 2 * w.size + 4 * length * depth),
    )(here, *grads, w)


def weight_kernel(parts, core, *refs):
    grads, (kept, tables, keep, send) = refs[:parts], refs[parts:]
    slices, rows, _ = keep.shape
    rows -= 16
    turned = kept[...].T
    for part in range(parts):
        term = dot_nn(turned, grads[part][...])
        size = term.shape[1] // 3
        for c, at in enumerate(part_columns(keep.at[0], part, parts)):
            columns = pl.ds(at.start, size)
            store_halves(
                core[0],
                term[:, c * size : (c + 1) * size],
                keep.at[:, pl.ds(0, rows), columns],
                send.at[:, pl.ds(0, rows), columns],
            )
    count = tables.shape[0]
    number = NB // (2 * slices)
    for j in range(slices):
        low = tables[:, 2 * j * number : (2 * j + 1) * number]
        high = tables[:, (2 * j + 1) * number : (2 * j + 2) * number]
        keep[j, rows:, :] = jnp.zeros((16, keep.shape[2]), bf16)
        send[j, rows:, :] = jnp.zeros((16, keep.shape[2]), bf16)
        keep[j, rows : rows + count, 0:number] = jnp.where(core[0] == 0, low, high).astype(bf16)
        send[j, rows : rows + count, 0:number] = jnp.where(core[0] == 0, high, low).astype(bf16)


def weight_term(core, grads, kept, tables, dp):
    parts = len(grads)
    wide, depth = parts * grads[0].shape[1], kept.shape[1]
    slices = (dp // 2, depth // dp + 16, wide)
    outs = (jax.ShapeDtypeStruct(slices, bf16),) * 2
    return pl.pallas_call(
        functools.partial(weight_kernel, parts),
        out_shape=outs,
        grid=(1,),
        in_specs=[pl.BlockSpec(memory_space=pltpu.SMEM)] + whole_blocks([*grads, kept, tables]),
        out_specs=tuple(whole_blocks(outs)),
        compiler_params=pltpu.CompilerParams(vmem_limit_bytes=40 << 20),
        cost_estimate=cost(2 * kept.size * wide, 8 * depth * wide + 4 * kept.size),
    )(core, *grads, kept, tables)


def bits_of(size):
    return [1 << b for b in reversed(range(size.bit_length() - 1))]


def swap(value, axis, size, distance):
    return lax.ppermute(value, axis, [(j, j ^ distance) for j in range(size)])


def after(value, *others):
    return lax.optimization_barrier((value,) + others)[0]


def scatter_begin(parts, size, bits):
    held = {k: [v] for k, v in parts.items()}
    total = lambda terms: sum(v.astype(f32) for v in terms)
    for b in reversed(bits[1:]):
        arrived = []
        for k in sorted([k for k in held if not k & b], reverse=True):
            send = total(held.pop(k | b)).astype(bf16)
            if k == 0 and arrived:
                send = after(send, *arrived)
            arrived.append(swap(send, ("mq", "mr"), size, b))
            held[k].append(arrived[-1])
    return held[0], held[bits[0]]


def join_pair(own, other, b, axis):
    low = (lax.axis_index("dp") // b) % 2 == 0
    pair = (jnp.where(low, own, other), jnp.where(low, other, own))
    return jnp.concatenate(pair, axis=axis)


def halve(whole, b):
    pairs = whole.reshape((whole.shape[0] // 2, 2) + whole.shape[1:])
    mine = (lax.axis_index("dp") // b) % 2
    kept = lax.dynamic_index_in_dim(pairs, mine, 1, keepdims=False)
    sent = lax.dynamic_index_in_dim(pairs, 1 - mine, 1, keepdims=False)
    return kept, sent.astype(bf16)


def scatter_dp(kept, sent, size, b, ahead=()):
    while True:
        other = swap(sent, "dp", size, b)
        other = after(other, *ahead) if ahead else other
        whole = kept.astype(f32) + other.astype(f32)
        b, ahead = 2 * b, ()
        if b >= size:
            return whole.reshape(whole.shape[1:])
        kept, sent = halve(whole, b)


def on_device(
    dp,
    mp,
    inputs,
    segments,
    positions,
    boxes,
    pad_mask,
    w_qkv,
    w_out,
    w_gate_up,
    w_down,
    bias_tables,
    gains,
    out_grad,
):
    gain_values = gains.astype(f32)
    here = lax.axis_index(("mq", "mr"))
    me = lax.axis_index("dp")
    here_ref = here.astype(jnp.int32).reshape(1)
    me_ref = me.astype(jnp.int32).reshape(1)
    core_ref = (me % 2).astype(jnp.int32).reshape(1)
    rows, part, depth = inputs.shape
    width = w_out.shape[0]
    heads = width // 64
    slice_rows = w_qkv.shape[1]
    wide = w_down.shape[0]
    all_bits = bits_of(mp)
    near_bit = 1
    x = inputs.reshape(part, depth)
    og_own = out_grad.reshape(part, depth)

    def trade(blocks):
        return [blocks[0]] + [swap(blocks[k], ("mq", "mr"), mp, k) for k in range(1, mp)]

    wqkv_own = jnp.concatenate([w_qkv[c] for c in range(3)], axis=1)
    wqkv = lax.all_gather(wqkv_own, "dp", axis=0, tiled=True)
    wide_x = x.astype(f32)
    scale_one = lax.rsqrt(jnp.mean(wide_x * wide_x, axis=1, keepdims=True) + epsilon)
    n1 = {0: (wide_x * scale_one * gain_values[0:1]).astype(bf16)}
    wo_held = {0: w_out.T}
    for b in all_bits:
        for k in list(wo_held):
            wo_held[k ^ b] = swap(wo_held[k], ("mq", "mr"), mp, b)
    wo_half = jnp.concatenate([wo_held[k] for k in range(mp)], axis=1)
    for b in all_bits:
        for k in list(n1):
            send = after(n1[k], wo_half) if k else n1[k]
            n1[k ^ b] = swap(send, ("mq", "mr"), mp, b)
    wo_half = wo_half[None]
    chip_bits = [1 << j for j in range(1, dp.bit_length() - 1)]
    for b in chip_bits[:-1]:
        wo_half = jnp.concatenate([wo_half, swap(wo_half, "dp", dp, b)], axis=0)
    packed = jnp.concatenate([jnp.swapaxes(w_gate_up, 1, 2), w_down[None]], axis=0)
    packs = {0: packed.reshape(3 * wide, slice_rows)}

    labr, labc = label_arrays(segments, positions, boxes, pad_mask)
    tab, far = table_rows(bias_tables)
    spans = key_spans(segments)
    qkv, normed_one = project(
        here_ref, [n1[k] for k in range(mp)], after(wqkv, wo_half)
    )
    qkv = qkv.reshape(rows, mp * part, 3 * width)
    for b in all_bits[:-1]:
        for k in list(packs):
            packs[k ^ b] = swap(after(packs[k], n1[mp - 1]), ("mq", "mr"), mp, b)
    og_other = swap(after(og_own, n1[mp - 1]), ("mq", "mr"), mp, near_bit)
    wo_other = swap(wo_half, "dp", dp, chip_bits[-1])
    mixed, ot, lse = attention_forward(qkv, spans, labr, labc, tab, far)
    mixed_rows = mixed.reshape(mp * part, width)
    mixed_in = trade(
        [lax.dynamic_slice_in_dim(mixed_rows, (here ^ k) * part, part, 0) for k in range(mp)]
    )
    wo_half = jnp.concatenate([wo_half, after(wo_other, *mixed_in[1:])], axis=0)
    wo_other = swap(wo_half, "dp", dp, 1)
    ffn_w = []
    for k, v in packs.items():
        ahead = (mixed,) if k else ()
        v = lax.all_gather(after(v, *ahead) if k else v, "dp", axis=0, tiled=True)
        ffn_w.append(v.reshape(dp, 3, wide, slice_rows))
    mixed_all, middle, normed_two, wo = join(
        me_ref, mixed_in, wo_half, wo_other, x, gain_values[1:2]
    )

    n2_other = swap(normed_two, ("mq", "mr"), mp, near_bit)
    down, down_send, n2g, n2g_send, *ffn_terms = ffn(
        normed_two, n2_other, og_own, og_other, ffn_w
    )
    n2g_other = swap(n2g_send, ("mq", "mr"), mp, near_bit)
    terms = {}
    for k, term in zip(packs, ffn_terms):
        term = term if k else after(term, n2g_other)
        terms[k] = lax.psum_scatter(
            term.reshape(-1, slice_rows), "dp", scatter_dimension=0, tiled=True
        )

    split_out = split(
        core_ref,
        n2g,
        n2g_other,
        middle,
        og_own,
        gain_values[1:2],
        mixed_all,
        wo,
        mp,
        dp,
    )
    middle_grad, out_keep, out_send = split_out[:3]
    out_whole = out_keep.astype(f32) + swap(out_send, "dp", dp, 1).astype(f32)
    out_kept, out_sent = halve(out_whole, 2)
    go_in = trade(list(split_out[3:]))
    go_in = jnp.stack(go_in[:1] + [after(v, out_sent) for v in go_in[1:]])
    go = jnp.concatenate(
        [lax.dynamic_index_in_dim(go_in, here ^ m, 0, keepdims=False) for m in range(mp)], axis=0
    )
    go, down_send, out_sent = lax.optimization_barrier((go, down_send, out_sent))
    down_other = swap(down_send, ("mq", "mr"), mp, near_bit)
    out_other = swap(out_sent, "dp", dp, 2)
    go = go.reshape(rows, mp * part, width)
    halves = 2 if width % 256 == 0 else 1
    back = functools.partial(attention_backward, qkv, spans, labr, labc, bias_tables)
    dqkv, tg = zip(back(go, ot, lse, 0, halves))
    far_sums = {k: v for k, v in terms.items() if k}
    if halves == 2:
        go = after(go, dqkv[0], down_other, out_other, *far_sums.values())
        second = back(go, ot, lse, 1, halves)
        dqkv, tg = dqkv + second[:1], tg + second[1:]
    w_grad = {0: terms[0], **far_sums}
    for b in reversed(all_bits[:-1]):
        for k in [k for k in w_grad if k and not k & b and k | b in w_grad]:
            w_grad[k] = w_grad[k].astype(f32) + swap(
                w_grad.pop(k | b).astype(bf16), ("mq", "mr"), mp, b
            ).astype(f32)
    far_other = [
        swap(v.astype(bf16), ("mq", "mr"), mp, k) for k, v in w_grad.items() if k
    ]
    dqkv = lax.optimization_barrier(tuple(dqkv) + (down_other, out_other) + tuple(far_other))
    far_other = dqkv[halves + 2 :]
    dqkv = [v.reshape(mp * part, -1) for v in dqkv[:halves]]
    parts = finish(here_ref, dqkv, wqkv, mp)
    tg = jnp.sum(jnp.stack(tg), axis=1).reshape(halves, 3, heads // halves, 128)
    tg = jnp.swapaxes(tg, 0, 1).reshape(3 * heads, 128)
    own_terms, last_terms = scatter_begin(dict(enumerate(parts)), mp, all_bits)
    qkv_keep, qkv_send = weight_term(
        core_ref, [after(v, parts[-1]) for v in dqkv], normed_one, tg, dp
    )
    qkv_send, last_terms[-1] = lax.optimization_barrier((qkv_send, last_terms[-1]))
    last_send = sum(v.astype(f32) for v in last_terms).astype(bf16)
    qkv_other = after(swap(qkv_send, "dp", dp, 1), last_send)
    qkv_whole = qkv_keep.astype(f32) + qkv_other.astype(f32)
    out_whole = out_kept.astype(f32) + after(out_other, qkv_whole).astype(f32)
    out_sum = scatter_dp(*halve(out_whole, 4), dp, 4)
    last = swap(last_send, ("mq", "mr"), mp, all_bits[0])
    qkv_kept, qkv_sent = halve(qkv_whole, 2)
    qkv_sum = scatter_dp(qkv_kept, qkv_sent, dp, 2)
    qkv_sum, own_sum = lax.optimization_barrier((qkv_sum, terms[0]))
    table_sum = qkv_sum[slice_rows : slice_rows + 3 * heads, : NB // dp]
    qkv_sum = qkv_sum[:slice_rows]
    out = (middle + down + after(down_other, last_send).astype(f32)).astype(bf16)
    qkv_out = jnp.stack([qkv_sum[:, c * width : (c + 1) * width] for c in range(3)])
    w_grad = own_sum.astype(f32) + sum(v.astype(f32) for v in far_other)
    w_grad = lax.optimization_barrier(w_grad.reshape(3, wide, slice_rows))
    gate_up_out = jnp.swapaxes(w_grad[:2], 1, 2)
    down_out = w_grad[2]
    table_out = jnp.swapaxes(table_sum.reshape(3, heads, NB // dp), 1, 2)

    own_gains = lax.dynamic_slice_in_dim(gain_values, me * slice_rows, slice_rows, 1)
    products = jnp.stack(
        [
            jnp.sum(qkv_sum * wqkv_own.astype(f32), axis=1),
            jnp.sum(gate_up_out * w_gate_up.astype(f32), axis=(0, 2)),
        ]
    )
    products = (products / own_gains).reshape(2, mp, slice_rows // mp)
    products = jnp.stack(
        [lax.dynamic_index_in_dim(products, here ^ k, 1, keepdims=False) for k in range(mp)], axis=1
    )
    products = jnp.pad(products, ((0, 14), (0, 0), (0, width - slice_rows // mp)))
    sums = jnp.concatenate([out_sum, products.reshape(16, mp * width)], axis=0).astype(bf16)
    sums = trade([sums[:, k * width : (k + 1) * width] for k in range(mp)])
    sums = sum(v.astype(f32) for v in sums)
    sums, last = lax.optimization_barrier((sums, last))
    n1g = sum(v.astype(f32) for v in own_terms + [last])
    a = n1g * gain_values[0:1]
    input_grad = (
        middle_grad
        + scale_one * a
        - wide_x
        * (scale_one * scale_one * scale_one)
        * jnp.mean(a * wide_x, axis=1, keepdims=True)
    ).astype(bf16)
    out_out = sums[:slice_rows].T
    gain_out = sums[slice_rows : slice_rows + 2, : slice_rows // mp]
    shape = inputs.shape
    return (
        out.reshape(shape),
        input_grad.reshape(shape),
        qkv_out,
        out_out,
        gate_up_out,
        down_out,
        table_out,
        gain_out,
    )


def solution(mesh):
    dp, mp = mesh.shape["dp"], mesh.shape["mp"]
    split_mesh = jax.sharding.Mesh(mesh.devices.reshape(dp, mp // 2, 2), ("dp", "mq", "mr"))
    both = ("mq", "mr")
    placed = (
        P("dp", both, None),
        P("dp", None),
        P("dp", None),
        P(None, "dp", None),
        P("dp", None),
        P(None, "dp", both),
        P(both, "dp"),
        P(None, "dp", both),
        P(both, "dp"),
        P(None, None, both),
        P(),
        P("dp", both, None),
    )
    return jax.shard_map(
        functools.partial(on_device, dp, mp),
        mesh=split_mesh,
        in_specs=placed,
        out_specs=(
            P("dp", both, None),
            P("dp", both, None),
            P(None, "dp", both),
            P(both, "dp"),
            P(None, "dp", both),
            P(both, "dp"),
            P(None, "dp", both),
            P(None, ("dp", "mq", "mr")),
        ),
        check_vma=False,
    )
```

```python
import functools
import jax
import jax.numpy as jnp
from jax import lax
from jax.experimental import pallas as pl
from jax.experimental.pallas import tpu as pltpu
from jax.sharding import PartitionSpec as P

NB = 32
thresholds = (12, 16, 23, 32, 46, 64, 91)
BQ = 256
PAD = 128
REACH = 448
TR = 64
UNIT = 256
UNROLL = 2
NEG = -1e30
bf16 = jnp.bfloat16
f32 = jnp.float32


def bucket_of(distance):
    magnitude = jnp.abs(distance)
    stepped = 8 + sum(((magnitude >= boundary).astype(jnp.int32) for boundary in thresholds))
    return jnp.where(magnitude < 8, magnitude, stepped) + 16 * (distance > 0).astype(jnp.int32)


def iota(shape, axis):
    return lax.broadcasted_iota(jnp.int32, shape, axis)


def to_bf16(mask):
    return jnp.where(mask, 1.0, 0.0).astype(bf16)


def key_features(labc_padded, tab, k, feats, heads):
    length = k.shape[0]
    labc = labc_padded[PAD : PAD + length, :]
    for kind in (0, 1):
        chosen = to_bf16(iota((length, 256), 1) == labc[:, 2 + kind : 3 + kind])
        where_bucket = bucket_of(iota((256, 256), 0) - iota((256, 256), 1))
        for h in range(heads):
            row = tab[(1 + kind) * heads + h : (1 + kind) * heads + h + 1, :]
            wide = jnp.broadcast_to(row, (256, 128))
            toep = jnp.concatenate(
                [
                    jnp.take_along_axis(wide, where_bucket[:, c : c + 128], axis=1)
                    for c in (0, 128)
                ],
                axis=1,
            ).astype(bf16)
            feats[h, 0:length, kind * 256 : kind * 256 + 256] = jnp.dot(
                chosen, toep, preferred_element_type=f32
            ).astype(bf16)
    lane = iota((length, 64), 1)
    mask = jnp.where(
        lane < 8,
        jnp.where(labc[:, 0:1] == lane, 0.0, NEG),
        jnp.where((lane == 8) & (labc[:, 4:5] != 1), NEG, 0.0),
    ).astype(bf16)
    for h in range(heads):
        feats[h, 0:length, 512:576] = k[:, h * 64 : h * 64 + 64]
        feats[h, 0:length, 576:640] = mask
        feats[h, length:, 0:512] = jnp.zeros((PAD, 512), bf16)
        feats[h, length:, 512:640] = jnp.where(iota((PAD, 128), 1) == 72, NEG, 0.0).astype(bf16)


def query_features(labr, first, a):
    def of(row):
        return labr[row : row + 1, pl.ds(first, BQ)]

    sub = iota((256, BQ), 0)
    a[0:256, :] = to_bf16(sub == of(2))
    a[256:512, :] = to_bf16(sub == of(3))
    low = iota((64, BQ), 0)
    a[576:640, :] = jnp.where(
        low < 8, jnp.where(of(0) == low, 1.0, 0.0), jnp.where(low == 8, 1.0, 0.0)
    ).astype(bf16)


def near_buckets(labr, labc, first, idx):
    here = labr[1:2, pl.ds(first, BQ)]
    idx[...] = bucket_of(labc[pl.ds(first, 2 * BQ), 1:2] - here)


def add_near(s_ref, tab, idx, padded, first, h, own):
    wide = jnp.broadcast_to(tab[pl.ds(h, 1), :], (TR, 128))
    for n in range(0, 2 * BQ, TR):
        rows = pl.ds(pl.multiple_of(first + n, TR), TR)
        got = jnp.concatenate(
            [
                jnp.take_along_axis(wide, idx[n : n + TR, c : c + 128], axis=1)
                for c in range(0, BQ, 128)
            ],
            axis=1,
        )
        s = s_ref[rows, :] + got
        if 128 <= n < 128 + BQ:
            same = iota((TR, BQ), 0) + (n - 128) == iota((TR, BQ), 1)
            s = jnp.where(same & padded, own, s)
        s_ref[rows, :] = s


def own_scores(own, qt, k_block, tab, heads):
    prod = qt[...].astype(f32) * k_block.T.astype(f32)
    for h in range(heads):
        zero_bias = tab[h, 0] + tab[heads + h, 0] + tab[2 * heads + h, 0]
        own[h] = jnp.broadcast_to(
            jnp.sum(prod[h * 64 : h * 64 + 64], axis=0, keepdims=True) + zero_bias, (8, BQ)
        )


def far_constant(far, qb, t, h):
    return jnp.where(t < 2 * qb - 1, far[0, h], jnp.where(t > 2 * qb + 2, far[1, h], 0.0))


def rows_max(value):
    return functools.reduce(jnp.maximum, [value[i : i + 8] for i in range(0, value.shape[0], 8)])


def rows_sum(value):
    return functools.reduce(jnp.add, [value[i : i + 8] for i in range(0, value.shape[0], 8)])


def for_each_size(count, limit, body):
    for n in range(1, limit + 1):
        if n * UNIT >= min(BQ, limit * UNIT):
            pl.when(count == n)(functools.partial(body, n))


def fwd_kernel(
    heads, far, spans, labr, labc, tab, q, k, v, mixed, ot, lse,
    feats, vt, idx, qt, own, o_all, *pairs
):
    a, s_all, p_all = (pairs[i * UNROLL : (i + 1) * UNROLL] for i in range(3))
    labr, labc, q, k, v = labr.at[0], labc.at[0], q.at[0], k.at[0], v.at[0]
    mixed, ot, lse = mixed.at[0], ot.at[0], lse.at[0]
    length = k.shape[0]
    qb = pl.program_id(1)
    first = pl.multiple_of(qb * BQ, BQ)
    block = pl.program_id(0) * pl.num_programs(1) + qb
    begin = pl.multiple_of(spans[0, block] * 128, 128)
    count = spans[1, block]

    @pl.when(qb == 0)
    def _():
        key_features(labc, tab, k, feats, heads)
        vt[:, 0:length] = v[...].T
        vt[:, length:] = jnp.zeros((heads * 64, PAD), bf16)

    for par in range(UNROLL):
        query_features(labr, first, a[par])
    near_buckets(labr, labc, first, idx)
    qt[...] = q[...].T
    own_scores(own, qt, k[pl.ds(first, BQ), :], tab, heads)
    padded = labr[4:5, pl.ds(first, BQ)] != 1

    def constant(h, row):
        return far_constant(far, qb, spans[0, block] + row // 128, h)

    def some_heads(i, n):
        size = n * UNIT
        span = pl.ds(begin, size)
        turns = [(par, i * UNROLL + par) for par in range(UNROLL)]
        rows_of = lambda row: pl.ds(pl.multiple_of(begin + PAD + row, TR), TR)
        for par, h in turns:
            a[par][512:576, :] = qt[pl.ds(pl.multiple_of(h * 64, 64), 64), :]
            s_all[par][pl.ds(begin + PAD, size), :] = jnp.dot(
                feats[h, span, :], a[par][...], preferred_element_type=f32
            )
        for par, h in turns:
            add_near(s_all[par], tab, idx, padded, first, h, own[h, 0:1, :])
        tops = []
        for par, h in turns:
            top = None
            for row in range(0, size, TR):
                here = rows_max(s_all[par][rows_of(row), :]) + constant(h, row)
                top = here if top is None else jnp.maximum(top, here)
            tops.append(jnp.max(top, axis=0, keepdims=True))
        totals = []
        for par, h in turns:
            total = jnp.zeros((8, BQ), f32)
            for row in range(0, size, TR):
                p = jnp.exp(s_all[par][rows_of(row), :] - (tops[par] - constant(h, row)))
                total = total + rows_sum(p)
                p_all[par][row : row + TR, :] = p.astype(bf16)
            totals.append(jnp.sum(total, axis=0, keepdims=True))
        for par, h in turns:
            cols = pl.ds(pl.multiple_of(h * 64, 64), 64)
            o = jnp.dot(vt[cols, span], p_all[par][0:size, :], preferred_element_type=f32)
            o_all[cols, :] = o * (1.0 / totals[par])
            lse[pl.ds(h, 1), :] = tops[par] + jnp.log(totals[par])

    def body(n):
        def step(i, _):
            some_heads(i, n)
            return 0

        lax.fori_loop(0, heads // UNROLL, step, 0)

    for_each_size(count, length // UNIT, body)
    ot[...] = o_all[...]
    mixed[...] = o_all[...].T.astype(bf16)


def bwd_kernel(
    heads, skip, far, spans, labr, labc, tab, spread, q, k, v, go, ot, lse,
    dqkv, tg,
    feats, ends, vs, acc, cxy, cp, sums, idx, into, at_here,
    qt, gt, own, delta, flipped, right, dqt, *pairs
):
    a, s_all, dp_all, pd_all = (pairs[i * UNROLL : (i + 1) * UNROLL] for i in range(4))
    labr, labc, q, k, v = labr.at[0], labc.at[0], q.at[0], k.at[0], v.at[0]
    go, ot, lse, dqkv, tg = go.at[0], ot.at[0], lse.at[0], dqkv.at[0], tg.at[0]
    length = k.shape[0]
    width = heads * 64
    tiles = length // 128
    qb = pl.program_id(1)
    first = pl.multiple_of(qb * BQ, BQ)
    block = pl.program_id(0) * pl.num_programs(1) + qb
    begin = pl.multiple_of(spans[0, block] * 128, 128)
    count = spans[1, block]

    @pl.when(qb == 0)
    def _():
        key_features(labc, tab, k, feats, heads)
        sub = iota((256, length), 0)
        ends[0:256, 0:length] = to_bf16(sub == labr[2:3, :])
        ends[256:512, 0:length] = to_bf16(sub == labr[3:4, :])
        ends[512 : 512 + width, 0:length] = k[...].T
        ends[:, length:] = jnp.zeros((512 + width, PAD), bf16)
        for h in range(heads):
            vs[h, 0:length, :] = v[:, h * 64 : h * 64 + 64]
            vs[h, length:, :] = jnp.zeros((PAD, 64), bf16)
        acc[...] = jnp.zeros_like(acc)
        cxy[...] = jnp.zeros_like(cxy)
        cp[...] = jnp.zeros_like(cp)
        sums[...] = jnp.zeros_like(sums)

    near = pl.ds(pl.multiple_of(first, 128), 2 * BQ)
    for par in range(UNROLL):
        query_features(labr, first, a[par])
        pd_all[par][near, BQ : 2 * BQ] = jnp.zeros((2 * BQ, BQ), bf16)
    near_buckets(labr, labc, first, idx)
    here_cols = labc[pl.ds(first + PAD, BQ), :]
    windows = []
    for half in (0, 1):
        lo = jnp.clip(qb * 2 + half - 1, 0, tiles - 3)
        windows.append(pl.multiple_of(lo * 128, 128))
        origin = here_cols[half * 128 : half * 128 + 1, 1:2]
        into[half] = to_bf16(
            iota((REACH, 384), 0) == labr[1:2, pl.ds(windows[half], 384)] - origin + 92
        )
        at_here[half * 128 : half * 128 + 128, :] = to_bf16(
            255 - iota((128, 256), 1) == here_cols[half * 128 : half * 128 + 128, 1:2] - origin
        )

    qt[...] = q[...].T
    gt[...] = go[...].T
    own_scores(own, qt, k[pl.ds(first, BQ), :], tab, heads)
    padded = labr[4:5, pl.ds(first, BQ)] != 1
    delta_all = gt[...].astype(f32) * ot[...]
    zeros = jnp.zeros((BQ, 64), bf16)
    for h in range(heads):
        cols = slice(h * 64, h * 64 + 64)
        delta[h] = jnp.broadcast_to(jnp.sum(delta_all[cols], axis=0, keepdims=True), (8, BQ))
        right[h, 0:BQ] = jnp.concatenate([go[:, cols], zeros], axis=1)
        right[h, BQ : 2 * BQ] = jnp.concatenate([zeros, q[:, cols]], axis=1)
    for kind in (0, 1):
        flipped[kind] = to_bf16(
            255 - iota((BQ, 256), 1) == here_cols[:, 2 + kind : 3 + kind]
        )

    def some_heads(i, n):
        size = n * UNIT
        span = pl.ds(begin, size)
        span_padded = pl.ds(pl.multiple_of(begin + PAD, 128), size)
        turns = [(par, i * UNROLL + par) for par in range(UNROLL)]
        cols_of = lambda h: pl.ds(pl.multiple_of(h * 64, 64), 64)
        for par, h in turns:
            a[par][512:576, :] = qt[cols_of(h), :]
            s_all[par][span_padded, :] = jnp.dot(
                feats[h, span, :], a[par][...], preferred_element_type=f32
            )
            dp_all[par][0:size, :] = jnp.dot(
                vs[h, span, :], gt[cols_of(h), :], preferred_element_type=f32
            )
        for par, h in turns:
            add_near(s_all[par], tab, idx, padded, first, h, own[h, 0:1, :])
        for par, h in turns:
            pd = pd_all[par]
            lse_row = lse[pl.ds(skip + h, 1), :]
            delta_row = delta[h, 0:1, :]
            every = jnp.zeros((8, BQ), f32)
            high = jnp.zeros((8, BQ), f32)
            for row in range(0, size, TR):
                t = spans[0, block] + row // 128
                rows = pl.ds(pl.multiple_of(begin + PAD + row, TR), TR)
                p = jnp.exp(s_all[par][rows, :] - (lse_row - far_constant(far, qb, t, h)))
                ds = p * (dp_all[par][row : row + TR, :] - delta_row)
                pd[rows, 0:BQ] = p.astype(bf16)
                pd[rows, BQ : 2 * BQ] = ds.astype(bf16)
                part = rows_sum(ds)
                every = every + part
                high = high + jnp.where(t >= 2 * qb + 2, part, 0.0)
            for row in range(0, BQ, TR):
                ds = pd[pl.ds(pl.multiple_of(first + PAD + row, TR), TR), BQ : 2 * BQ].astype(f32)
                high = high + rows_sum(
                    jnp.where(iota((TR, BQ), 0) + row > iota((TR, BQ), 1), ds, 0.0)
                )
            sums[h, 0:8, :] += every - high
            sums[h, 8:16, :] += high
        placed = []
        for par, h in turns:
            acc[h, span, :] += jnp.dot(
                pd_all[par][span_padded, :], right[h], preferred_element_type=f32
            )
            dst = pd_all[par][span_padded, BQ : 2 * BQ]
            dqt[cols_of(h), :] = jnp.dot(
                ends[pl.ds(pl.multiple_of(512 + h * 64, 64), 64), span],
                dst,
                preferred_element_type=f32,
            )
            placed.append(
                jnp.dot(ends[0:512, span], dst, preferred_element_type=f32).astype(bf16)
            )
        puts = []
        for par, h in turns:
            puts.append(
                jnp.concatenate(
                    [
                        jnp.dot(
                            into[half],
                            pd_all[par][
                                pl.ds(pl.multiple_of(windows[half] + PAD, 128), 384),
                                BQ + half * 128 : BQ + half * 128 + 128,
                            ],
                            preferred_element_type=f32,
                        ).astype(bf16)
                        for half in (0, 1)
                    ],
                    axis=1,
                )
            )
        for par, h in turns:
            for kind in (0, 1):
                part = slice(kind * 256, kind * 256 + 256)
                cxy[h, part, :] += jnp.dot(
                    placed[par][part], flipped[kind], preferred_element_type=f32
                )
            cp[h] += jnp.dot(puts[par], at_here[...], preferred_element_type=f32)

    def body(n):
        def step(i, _):
            some_heads(i, n)
            return 0

        lax.fori_loop(0, heads // UNROLL, step, 0)

    for_each_size(count, length // UNIT, body)
    dqkv[pl.ds(first, BQ), 0:width] = dqt[...].T.astype(bf16)

    @pl.when(qb == pl.num_programs(1) - 1)
    def _():
        for h in range(0, heads, 2):
            one, two = acc[h, 0:length, :], acc[h + 1, 0:length, :]
            dqkv[:, width + h * 64 : width + h * 64 + 128] = jnp.concatenate(
                [one[:, 64:], two[:, 64:]], axis=1
            ).astype(bf16)
            dqkv[:, 2 * width + h * 64 : 2 * width + h * 64 + 128] = jnp.concatenate(
                [one[:, :64], two[:, :64]], axis=1
            ).astype(bf16)
        lines = []
        for kind in (0, 1, 2):
            for h in range(heads):
                c = cp[h] if kind == 0 else cxy[h, (kind - 1) * 256 : kind * 256, :]
                c = jnp.concatenate([c, jnp.zeros_like(c)], axis=1)
                c = pltpu.roll(c, 0, 1, stride=1, stride_axis=0)
                lines.append(jnp.sum(c, axis=0, keepdims=True))
        rel = jnp.dot(
            jnp.concatenate(lines[:heads], axis=0),
            spread[0],
            preferred_element_type=f32,
            precision=lax.Precision.HIGHEST,
        )
        box = jnp.dot(
            jnp.concatenate(lines[heads:], axis=0),
            spread[1],
            preferred_element_type=f32,
            precision=lax.Precision.HIGHEST,
        )
        lane = iota((heads, 128), 1)
        low_all = jnp.concatenate([jnp.sum(sums[h, 0:8, :]).reshape(1, 1) for h in range(heads)], axis=0)
        high_all = jnp.concatenate([jnp.sum(sums[h, 8:16, :]).reshape(1, 1) for h in range(heads)], axis=0)
        near_low = jnp.sum(jnp.where(lane < 15, rel, 0.0), axis=1, keepdims=True)
        near_high = jnp.sum(jnp.where((lane >= 16) & (lane < 31), rel, 0.0), axis=1, keepdims=True)
        rel = jnp.where(lane == 15, low_all - near_low, rel)
        rel = jnp.where(lane == 31, high_all - near_high, rel)
        tg[...] = jnp.concatenate([rel, box], axis=0)


def spread_tables():
    slot = jnp.arange(512)
    number = jnp.arange(128)
    rel_t = slot - 347
    rel = (bucket_of(rel_t)[:, None] == number[None]) & (jnp.abs(rel_t) < 91)[:, None]
    box = bucket_of(slot - 255)[:, None] == number[None]
    return jnp.stack([rel, box]).astype(f32)


def key_spans(segments):
    starts = segments[:, ::BQ]
    ends = segments[:, BQ - 1 :: BQ]
    lo = jnp.sum(segments[:, None, :] < starts[:, :, None], axis=2) // 128
    hi = jnp.sum(segments[:, None, :] <= ends[:, :, None], axis=2)
    count = (hi - lo * 128 + UNIT - 1) // UNIT
    return jnp.stack([lo.reshape(-1), count.reshape(-1)]).astype(jnp.int32)


def label_arrays(segments, positions, boxes, pad_mask):
    zero = jnp.zeros_like(segments)
    labr = jnp.stack([segments, positions, boxes[0], boxes[1], pad_mask, zero, zero, zero], axis=1)
    return labr, jnp.pad(jnp.swapaxes(labr, 1, 2), ((0, 0), (PAD, PAD), (0, 0)))


def table_rows(tables):
    kinds, _, heads = tables.shape
    rows = jnp.swapaxes(tables, 1, 2).reshape(kinds * heads, NB).astype(f32)
    far = jnp.stack([tables[0, 15], tables[0, 31]]).astype(f32)
    return jnp.pad(rows, ((0, 0), (0, 128 - NB))), far


def cost(flops, nbytes):
    return pl.CostEstimate(flops=flops, bytes_accessed=nbytes, transcendentals=0)


def attention_forward(qkv, spans, labr, labc, tab, far):
    rows, length, wide = qkv.shape
    width = wide // 3
    heads = width // 64
    steps = length // BQ
    smem = pl.BlockSpec(memory_space=pltpu.SMEM)
    return pl.pallas_call(
        functools.partial(fwd_kernel, heads),
        out_shape=(
            jax.ShapeDtypeStruct((rows, length, width), bf16),
            jax.ShapeDtypeStruct((rows, width, length), f32),
            jax.ShapeDtypeStruct((rows, 8, length), f32),
        ),
        grid=(rows, steps),
        in_specs=[
            smem,
            smem,
            pl.BlockSpec((1, 8, length), lambda r, i: (r, 0, 0)),
            pl.BlockSpec((1, length + 2 * PAD, 8), lambda r, i: (r, 0, 0)),
            pl.BlockSpec(tab.shape, lambda r, i: (0, 0)),
            pl.BlockSpec((1, BQ, width), lambda r, i: (r, i, 0)),
            pl.BlockSpec((1, length, width), lambda r, i: (r, 0, 1)),
            pl.BlockSpec((1, length, width), lambda r, i: (r, 0, 2)),
        ],
        out_specs=(
            pl.BlockSpec((1, BQ, width), lambda r, i: (r, i, 0)),
            pl.BlockSpec((1, width, BQ), lambda r, i: (r, 0, i)),
            pl.BlockSpec((1, 8, BQ), lambda r, i: (r, 0, i)),
        ),
        scratch_shapes=[
            pltpu.VMEM((heads, length + PAD, 640), bf16),
            pltpu.VMEM((width, length + PAD), bf16),
            pltpu.VMEM((512, BQ), jnp.int32),
            pltpu.VMEM((width, BQ), bf16),
            pltpu.VMEM((heads, 8, BQ), f32),
            pltpu.VMEM((width, BQ), f32),
            *[pltpu.VMEM((640, BQ), bf16)] * UNROLL,
            *[pltpu.VMEM((length + 2 * PAD, BQ), f32)] * UNROLL,
            *[pltpu.VMEM((length, BQ), bf16)] * UNROLL,
        ],
        compiler_params=pltpu.CompilerParams(vmem_limit_bytes=48 << 20),
        cost_estimate=cost(rows * heads * length * length * 4000, rows * length * wide * 4),
    )(far, spans, labr, labc, tab, qkv, qkv, qkv)


def attention_backward(qkv, spans, labr, labc, tables, go, ot, lse, part, parts):
    rows, length, wide = qkv.shape
    wide = wide // parts
    width = wide // 3
    count = tables.shape[2] // parts
    tab, far = table_rows(tables[:, :, part * count : (part + 1) * count])
    heads = width // 64
    steps = length // BQ
    spread = spread_tables()
    smem = pl.BlockSpec(memory_space=pltpu.SMEM)
    return pl.pallas_call(
        functools.partial(bwd_kernel, heads, part * heads),
        out_shape=(
            jax.ShapeDtypeStruct((rows, length, wide), bf16),
            jax.ShapeDtypeStruct((rows, 3 * heads, 128), f32),
        ),
        grid=(rows, steps),
        in_specs=[
            smem,
            smem,
            pl.BlockSpec((1, 8, length), lambda r, i: (r, 0, 0)),
            pl.BlockSpec((1, length + 2 * PAD, 8), lambda r, i: (r, 0, 0)),
            pl.BlockSpec(tab.shape, lambda r, i: (0, 0)),
            pl.BlockSpec(spread.shape, lambda r, i: (0, 0, 0)),
            pl.BlockSpec((1, BQ, width), lambda r, i: (r, i, part)),
            pl.BlockSpec((1, length, width), lambda r, i: (r, 0, parts + part)),
            pl.BlockSpec((1, length, width), lambda r, i: (r, 0, 2 * parts + part)),
            pl.BlockSpec((1, BQ, width), lambda r, i: (r, i, part)),
            pl.BlockSpec((1, width, BQ), lambda r, i: (r, part, i)),
            pl.BlockSpec((1, 8, BQ), lambda r, i: (r, 0, i)),
        ],
        out_specs=(
            pl.BlockSpec((1, length, wide), lambda r, i: (r, 0, 0)),
            pl.BlockSpec((1, 3 * heads, 128), lambda r, i: (r, 0, 0)),
        ),
        scratch_shapes=[
            pltpu.VMEM((heads, length + PAD, 640), bf16),
            pltpu.VMEM((512 + width, length + PAD), bf16),
            pltpu.VMEM((heads, length + PAD, 64), bf16),
            pltpu.VMEM((heads, length + PAD, 128), f32),
            pltpu.VMEM((heads, 512, 256), f32),
            pltpu.VMEM((heads, REACH, 256), f32),
            pltpu.VMEM((heads, 16, BQ), f32),
            pltpu.VMEM((512, BQ), jnp.int32),
            pltpu.VMEM((2, REACH, 384), bf16),
            pltpu.VMEM((BQ, 256), bf16),
            pltpu.VMEM((width, BQ), bf16),
            pltpu.VMEM((width, BQ), bf16),
            pltpu.VMEM((heads, 8, BQ), f32),
            pltpu.VMEM((heads, 8, BQ), f32),
            pltpu.VMEM((2, BQ, 256), bf16),
            pltpu.VMEM((heads, 2 * BQ, 128), bf16),
            pltpu.VMEM((width, BQ), f32),
            *[pltpu.VMEM((640, BQ), bf16)] * UNROLL,
            *[pltpu.VMEM((length + 2 * PAD, BQ), f32)] * UNROLL,
            *[pltpu.VMEM((length, BQ), f32)] * UNROLL,
            *[pltpu.VMEM((length + 2 * PAD, 2 * BQ), bf16)] * UNROLL,
        ],
        compiler_params=pltpu.CompilerParams(vmem_limit_bytes=59 << 20),
        cost_estimate=cost(rows * heads * length * length * 8500, rows * length * wide * 6),
    )(far, spans, labr, labc, tab, spread, qkv, qkv, qkv, go, ot, lse)


epsilon = 1e-06
gelu_coefficient = 0.7978845608028654
CHUNKS = 2


def dot_nt(one, two):
    return lax.dot_general(one, two, (((1,), (1,)), ((), ())), preferred_element_type=f32)


def dot_nn(one, two):
    return jnp.dot(one, two, preferred_element_type=f32)


def ffn_kernel(slots, n2_own, n2_other, og_own, og_other, *refs):
    weights = refs[:slots]
    down, down_send, n2g, n2g_send, *terms = refs[slots : 2 * slots + 4]
    wt, gate, up, hg, hid, dgate, dup, down_sum, n2g_sum, n2, og, n2t, ogt, sems, stage, out_sems = refs[2 * slots + 4 :]
    slices, kinds, wide, lanes = weights[0].shape
    whole_lanes = lanes % 128 == 0
    slot = pl.program_id(0)

    def fetch(j, c, d):
        return pltpu.make_async_copy(
            weights[j].at[d, c],
            wt.at[j, c, :, pl.ds(d * lanes, lanes)],
            sems.at[j, c, d],
        )

    @pl.when(slot == 0)
    def _():
        for j in range(slots):
            for c in range(kinds):
                for d in range(slices):
                    if whole_lanes:
                        fetch(j, c, d).start()
                    else:
                        wt[j, c, :, d * lanes : (d + 1) * lanes] = weights[j][d, c]
        half = n2_own.shape[0]
        n2[:half, :] = n2_own[...]
        n2[half:, :] = n2_other[...]
        og[:half, :] = og_own[...]
        og[half:, :] = og_other[...]
        n2t[...] = n2[...].T
        ogt[...] = og[...].T

    if whole_lanes:
        for j in range(slots):

            @pl.when(slot == j)
            def _():
                for c in range(kinds):
                    for d in range(slices):
                        fetch(j, c, d).wait()

    gate[...] = dot_nn(wt[slot, 0], n2t[...])
    up[...] = dot_nn(wt[slot, 1], n2t[...])
    hg[...] = dot_nn(wt[slot, 2], ogt[...])

    def chunk(c, _):
        rows = pl.ds(pl.multiple_of(c * 16, 16), 16)
        g, u, back = gate[rows, :], up[rows, :], hg[rows, :]
        square = g * g
        t = jnp.tanh(gelu_coefficient * (g + 0.044715 * square * g))
        mid = 0.5 * (1.0 + t)
        act = g * mid
        slope = mid + 0.5 * g * (1.0 - t * t) * (gelu_coefficient * (1.0 + 0.134145 * square))
        hid[rows, :] = (act * u).astype(bf16)
        dgate[rows, :] = (back * u * slope).astype(bf16)
        dup[rows, :] = (back * act).astype(bf16)
        return 0

    lax.fori_loop(0, wide // 16, chunk, 0, unroll=CHUNKS)
    n2g_all = dot_nn(dgate[...].T, wt[slot, 0]) + dot_nn(dup[...].T, wt[slot, 1])
    down_all = dot_nn(hid[...].T, wt[slot, 2])

    @pl.when(slot == 0)
    def _():
        n2g_sum[...] = n2g_all
        down_sum[...] = down_all

    @pl.when(slot > 0)
    def _():
        n2g_sum[...] += n2g_all
        down_sum[...] += down_all

    for c, (one, two) in enumerate(((dgate, n2), (dup, n2), (hid, og))):
        term = dot_nn(one[...], two[...]).astype(bf16)
        for d in range(slices):
            stage[slot, d, c] = term[:, d * lanes : (d + 1) * lanes]

    def hand_out(j):
        return pltpu.make_async_copy(stage.at[j], terms[j], out_sems.at[j])

    for j in range(slots):

        @pl.when(slot == j)
        def _():
            hand_out(j).start()

    @pl.when(slot == pl.num_programs(0) - 1)
    def _():
        part = n2.shape[0] // 2
        n2g[...] = n2g_sum[:part, :]
        n2g_send[...] = n2g_sum[part:, :].astype(bf16)
        down[...] = down_sum[:part, :]
        down_send[...] = down_sum[part:, :].astype(bf16)
        for j in range(slots):
            hand_out(j).wait()


def ffn(n2_own, n2_other, og_own, og_other, weights):
    tokens, depth = 2 * n2_own.shape[0], n2_own.shape[1]
    slots = len(weights)
    slices, kinds, wide, lanes = weights[0].shape
    terms = jax.ShapeDtypeStruct((slices, kinds, wide, lanes), bf16)
    if lanes % 128 == 0:
        source = pl.BlockSpec(memory_space=pl.ANY)
    else:
        source = pl.BlockSpec(
            weights[0].shape, lambda i: (0, 0, 0, 0), pipeline_mode=pl.Buffered(1)
        )
    whole = lambda shape: pl.BlockSpec(shape, lambda i: (0,) * len(shape))
    own = jax.ShapeDtypeStruct((tokens // 2, depth), f32)
    send = jax.ShapeDtypeStruct((tokens // 2, depth), bf16)
    return pl.pallas_call(
        functools.partial(ffn_kernel, slots),
        out_shape=(own, send, own, send) + (terms,) * slots,
        grid=(slots,),
        in_specs=[whole(n2_own.shape)] * 4 + [source] * slots,
        out_specs=(whole(own.shape),) * 4
        + (pl.BlockSpec(memory_space=pl.ANY),) * slots,
        scratch_shapes=[
            pltpu.VMEM((slots, kinds, wide, depth), bf16),
            *[pltpu.VMEM((wide, tokens), f32)] * 3,
            *[pltpu.VMEM((wide, tokens), bf16)] * 3,
            *[pltpu.VMEM((tokens, depth), f32)] * 2,
            *[pltpu.VMEM((tokens, depth), bf16)] * 2,
            *[pltpu.VMEM((depth, tokens), bf16)] * 2,
            pltpu.SemaphoreType.DMA((slots, kinds, slices)),
            pltpu.VMEM((slots, slices, kinds, wide, lanes), bf16),
            pltpu.SemaphoreType.DMA((slots,)),
        ],
        compiler_params=pltpu.CompilerParams(vmem_limit_bytes=59 << 20),
        cost_estimate=cost(
            20 * slots * tokens * depth * wide, 4 * slots * weights[0].size + 8 * tokens * depth
        ),
    )(n2_own, n2_other, og_own, og_other, *weights)


def whole_blocks(arrays):
    return [pl.BlockSpec(a.shape, lambda i, n=len(a.shape): (0,) * n) for a in arrays]


def project_kernel(count, here, *refs):
    blocks, (w, qkv, kept) = refs[:count], refs[count:]
    for k in range(count):

        @pl.when(pl.program_id(0) == k)
        def _():
            kept[...] = blocks[k][...]
            qkv[...] = dot_nn(blocks[k][...], w[...]).astype(bf16)


def project(here, blocks, w):
    count = len(blocks)
    part, depth = blocks[0].shape
    wide = w.shape[1]
    whole = lambda shape: pl.BlockSpec(shape, lambda k, here: (0, 0))
    placed = lambda width: pl.BlockSpec((part, width), lambda k, here: (here[0] ^ k, 0))
    return pl.pallas_call(
        functools.partial(project_kernel, count),
        out_shape=(
            jax.ShapeDtypeStruct((count * part, wide), bf16),
            jax.ShapeDtypeStruct((count * part, depth), bf16),
        ),
        grid_spec=pltpu.PrefetchScalarGridSpec(
            num_scalar_prefetch=1,
            grid=(count,),
            in_specs=[whole((part, depth))] * count + [whole(w.shape)],
            out_specs=(placed(wide), placed(depth)),
        ),
        compiler_params=pltpu.CompilerParams(vmem_limit_bytes=40 << 20),
        cost_estimate=cost(2 * count * part * depth * wide, 2 * depth * wide + 4 * count * part * depth),
    )(here, *blocks, w)


def join_kernel(count, me, *refs):
    parts, (half, other, x, gain, mixed, middle, n2, w) = refs[:count], refs[count:]
    for k in range(count):
        mixed[:, k * parts[0].shape[1] : (k + 1) * parts[0].shape[1]] = parts[k][...]
    slices, rows, _ = half.shape
    for j in range(slices):
        for low, source in enumerate((half, other)):
            at = me[0] ^ (2 * j + low)
            w[pl.ds(pl.multiple_of(at * rows, rows), rows), :] = source[j]
    total = x[...].astype(f32) + dot_nt(mixed[...], w[...])
    middle[...] = total
    scale = lax.rsqrt(jnp.mean(total * total, axis=1, keepdims=True) + epsilon)
    n2[...] = (total * scale * gain[...]).astype(bf16)


def join(me, parts, half, other, x, gain):
    count = len(parts)
    part, width = parts[0].shape
    depth = x.shape[1]
    outs = (
        jax.ShapeDtypeStruct((part, count * width), bf16),
        jax.ShapeDtypeStruct((part, depth), f32),
        jax.ShapeDtypeStruct((part, depth), bf16),
        jax.ShapeDtypeStruct((depth, count * width), bf16),
    )
    return pl.pallas_call(
        functools.partial(join_kernel, count),
        out_shape=outs,
        grid=(1,),
        in_specs=[pl.BlockSpec(memory_space=pltpu.SMEM)]
        + whole_blocks([*parts, half, other, x, gain]),
        out_specs=tuple(whole_blocks(outs)),
        compiler_params=pltpu.CompilerParams(vmem_limit_bytes=59 << 20),
        cost_estimate=cost(4 * part * half.size, 8 * half.size + 12 * part * depth),
    )(me, *parts, half, other, x, gain)


def store_halves(core, term, keep, send):
    slices, rows, _ = keep.shape
    for j in range(slices):
        low = term[2 * j * rows : (2 * j + 1) * rows]
        high = term[(2 * j + 1) * rows : (2 * j + 2) * rows]
        keep[j] = jnp.where(core == 0, low, high).astype(bf16)
        send[j] = jnp.where(core == 0, high, low).astype(bf16)


def split_kernel(count, core, own, other, middle, og, gain, mixed, w, *refs):
    middle_grad, keep, send = refs[:3]
    outs = refs[3:]
    total = middle[...]
    scale = lax.rsqrt(jnp.mean(total * total, axis=1, keepdims=True) + epsilon)
    a = (own[...] + other[...].astype(f32)) * gain[...]
    grad = (
        og[...].astype(f32)
        + scale * a
        - total * (scale * scale * scale) * jnp.mean(a * total, axis=1, keepdims=True)
    )
    middle_grad[...] = grad
    low = grad.astype(bf16)
    back = dot_nn(low, w[...]).astype(bf16)
    width = outs[0].shape[1]
    for k in range(count):
        outs[k][...] = back[:, k * width : (k + 1) * width]
    store_halves(core[0], dot_nn(low.T, mixed[...]), keep, send)


def split(core, own, other, middle, og, gain, mixed, w, count, dp):
    part, depth = middle.shape
    columns = w.shape[1]
    slices = (dp // 2, depth // dp, columns)
    outs = (
        jax.ShapeDtypeStruct((part, depth), f32),
        jax.ShapeDtypeStruct(slices, bf16),
        jax.ShapeDtypeStruct(slices, bf16),
    ) + (jax.ShapeDtypeStruct((part, columns // count), bf16),) * count
    return pl.pallas_call(
        functools.partial(split_kernel, count),
        out_shape=outs,
        grid=(1,),
        in_specs=[pl.BlockSpec(memory_space=pltpu.SMEM)]
        + whole_blocks([own, other, middle, og, gain, mixed, w]),
        out_specs=tuple(whole_blocks(outs)),
        compiler_params=pltpu.CompilerParams(vmem_limit_bytes=59 << 20),
        cost_estimate=cost(4 * part * w.size, 10 * w.size + 16 * part * depth),
    )(core, own, other, middle, og, gain, mixed, w)


def part_columns(w, part, parts):
    width = w.shape[1] // 3
    size = width // parts
    return [slice(c * width + part * size, c * width + (part + 1) * size) for c in range(3)]


def finish_kernel(count, parts, here, *refs):
    grads, w, outs = refs[:parts], refs[parts], refs[parts + 1 :]
    total = None
    for part in range(parts):
        columns = jnp.concatenate([w[:, at] for at in part_columns(w, part, parts)], axis=1)
        term = dot_nt(grads[part][...], columns)
        total = term if total is None else total + term
    for j, out in enumerate(outs):

        @pl.when(pl.program_id(0) == j)
        def _():
            out[...] = total.astype(out.dtype)


def finish(here, grads, w, count):
    parts = len(grads)
    length, wide = grads[0].shape
    depth = w.shape[0]
    rows = length // count
    whole = lambda shape: pl.BlockSpec(shape, lambda k, here: (0,) * len(shape))
    return pl.pallas_call(
        functools.partial(finish_kernel, count, parts),
        out_shape=(jax.ShapeDtypeStruct((rows, depth), f32),)
        + (jax.ShapeDtypeStruct((rows, depth), bf16),) * (count - 1),
        grid_spec=pltpu.PrefetchScalarGridSpec(
            num_scalar_prefetch=1,
            grid=(count,),
            in_specs=[pl.BlockSpec((rows, wide), lambda k, here: (here[0] ^ k, 0))] * parts
            + [whole(w.shape)],
            out_specs=(whole((rows, depth)),) * count,
        ),
        compiler_params=pltpu.CompilerParams(vmem_limit_bytes=40 << 20),
        cost_estimate=cost(2 * length * w.size, 2 * w.size + 4 * length * depth),
    )(here, *grads, w)


def weight_kernel(parts, core, *refs):
    grads, (kept, tables, keep, send) = refs[:parts], refs[parts:]
    slices, rows, _ = keep.shape
    rows -= 16
    turned = kept[...].T
    for part in range(parts):
        term = dot_nn(turned, grads[part][...])
        size = term.shape[1] // 3
        for c, at in enumerate(part_columns(keep.at[0], part, parts)):
            columns = pl.ds(at.start, size)
            store_halves(
                core[0],
                term[:, c * size : (c + 1) * size],
                keep.at[:, pl.ds(0, rows), columns],
                send.at[:, pl.ds(0, rows), columns],
            )
    count = tables.shape[0]
    number = NB // (2 * slices)
    for j in range(slices):
        low = tables[:, 2 * j * number : (2 * j + 1) * number]
        high = tables[:, (2 * j + 1) * number : (2 * j + 2) * number]
        keep[j, rows:, :] = jnp.zeros((16, keep.shape[2]), bf16)
        send[j, rows:, :] = jnp.zeros((16, keep.shape[2]), bf16)
        keep[j, rows : rows + count, 0:number] = jnp.where(core[0] == 0, low, high).astype(bf16)
        send[j, rows : rows + count, 0:number] = jnp.where(core[0] == 0, high, low).astype(bf16)


def weight_term(core, grads, kept, tables, dp):
    parts = len(grads)
    wide, depth = parts * grads[0].shape[1], kept.shape[1]
    slices = (dp // 2, depth // dp + 16, wide)
    outs = (jax.ShapeDtypeStruct(slices, bf16),) * 2
    return pl.pallas_call(
        functools.partial(weight_kernel, parts),
        out_shape=outs,
        grid=(1,),
        in_specs=[pl.BlockSpec(memory_space=pltpu.SMEM)] + whole_blocks([*grads, kept, tables]),
        out_specs=tuple(whole_blocks(outs)),
        compiler_params=pltpu.CompilerParams(vmem_limit_bytes=40 << 20),
        cost_estimate=cost(2 * kept.size * wide, 8 * depth * wide + 4 * kept.size),
    )(core, *grads, kept, tables)


def bits_of(size):
    return [1 << b for b in reversed(range(size.bit_length() - 1))]


def swap(value, axis, size, distance):
    return lax.ppermute(value, axis, [(j, j ^ distance) for j in range(size)])


def after(value, *others):
    return lax.optimization_barrier((value,) + others)[0]


def scatter_begin(parts, size, bits):
    held = {k: [v] for k, v in parts.items()}
    total = lambda terms: sum(v.astype(f32) for v in terms)
    for b in reversed(bits[1:]):
        arrived = []
        for k in sorted([k for k in held if not k & b], reverse=True):
            send = total(held.pop(k | b)).astype(bf16)
            if k == 0 and arrived:
                send = after(send, *arrived)
            arrived.append(swap(send, ("mq", "mr"), size, b))
            held[k].append(arrived[-1])
    return held[0], held[bits[0]]


def join_pair(own, other, b, axis):
    low = (lax.axis_index("dp") // b) % 2 == 0
    pair = (jnp.where(low, own, other), jnp.where(low, other, own))
    return jnp.concatenate(pair, axis=axis)


def halve(whole, b):
    pairs = whole.reshape((whole.shape[0] // 2, 2) + whole.shape[1:])
    mine = (lax.axis_index("dp") // b) % 2
    kept = lax.dynamic_index_in_dim(pairs, mine, 1, keepdims=False)
    sent = lax.dynamic_index_in_dim(pairs, 1 - mine, 1, keepdims=False)
    return kept, sent.astype(bf16)


def scatter_dp(kept, sent, size, b, ahead=()):
    while True:
        other = swap(sent, "dp", size, b)
        other = after(other, *ahead) if ahead else other
        whole = kept.astype(f32) + other.astype(f32)
        b, ahead = 2 * b, ()
        if b >= size:
            return whole.reshape(whole.shape[1:])
        kept, sent = halve(whole, b)


def on_device(
    dp,
    mp,
    inputs,
    segments,
    positions,
    boxes,
    pad_mask,
    w_qkv,
    w_out,
    w_gate_up,
    w_down,
    bias_tables,
    gains,
    out_grad,
):
    gain_values = gains.astype(f32)
    here = lax.axis_index(("mq", "mr"))
    me = lax.axis_index("dp")
    here_ref = here.astype(jnp.int32).reshape(1)
    me_ref = me.astype(jnp.int32).reshape(1)
    core_ref = (me % 2).astype(jnp.int32).reshape(1)
    rows, part, depth = inputs.shape
    width = w_out.shape[0]
    heads = width // 64
    slice_rows = w_qkv.shape[1]
    wide = w_down.shape[0]
    all_bits = bits_of(mp)
    near_bit = 1
    x = inputs.reshape(part, depth)
    og_own = out_grad.reshape(part, depth)

    def trade(blocks):
        return [blocks[0]] + [swap(blocks[k], ("mq", "mr"), mp, k) for k in range(1, mp)]

    wqkv_own = jnp.concatenate([w_qkv[c] for c in range(3)], axis=1)
    wqkv = lax.all_gather(wqkv_own, "dp", axis=0, tiled=True)
    wide_x = x.astype(f32)
    scale_one = lax.rsqrt(jnp.mean(wide_x * wide_x, axis=1, keepdims=True) + epsilon)
    n1 = {0: (wide_x * scale_one * gain_values[0:1]).astype(bf16)}
    wo_held = {0: w_out.T}
    for b in all_bits:
        for k in list(wo_held):
            wo_held[k ^ b] = swap(wo_held[k], ("mq", "mr"), mp, b)
    wo_half = jnp.concatenate([wo_held[k] for k in range(mp)], axis=1)
    for b in all_bits:
        for k in list(n1):
            send = after(n1[k], wo_half) if k else n1[k]
            n1[k ^ b] = swap(send, ("mq", "mr"), mp, b)
    wo_half = wo_half[None]
    chip_bits = [1 << j for j in range(1, dp.bit_length() - 1)]
    for b in chip_bits[:-1]:
        wo_half = jnp.concatenate([wo_half, swap(wo_half, "dp", dp, b)], axis=0)
    packed = jnp.concatenate([jnp.swapaxes(w_gate_up, 1, 2), w_down[None]], axis=0)
    packs = {0: packed.reshape(3 * wide, slice_rows)}

    labr, labc = label_arrays(segments, positions, boxes, pad_mask)
    tab, far = table_rows(bias_tables)
    spans = key_spans(segments)
    qkv, normed_one = project(
        here_ref, [n1[k] for k in range(mp)], after(wqkv, wo_half)
    )
    qkv = qkv.reshape(rows, mp * part, 3 * width)
    for b in all_bits[:-1]:
        for k in list(packs):
            packs[k ^ b] = swap(after(packs[k], n1[mp - 1]), ("mq", "mr"), mp, b)
    og_other = swap(after(og_own, n1[mp - 1]), ("mq", "mr"), mp, near_bit)
    wo_other = swap(wo_half, "dp", dp, chip_bits[-1])
    mixed, ot, lse = attention_forward(qkv, spans, labr, labc, tab, far)
    mixed_rows = mixed.reshape(mp * part, width)
    mixed_in = trade(
        [lax.dynamic_slice_in_dim(mixed_rows, (here ^ k) * part, part, 0) for k in range(mp)]
    )
    wo_half = jnp.concatenate([wo_half, after(wo_other, *mixed_in[1:])], axis=0)
    wo_other = swap(wo_half, "dp", dp, 1)
    ffn_w = []
    for k, v in packs.items():
        ahead = (mixed,) if k else ()
        v = lax.all_gather(after(v, *ahead) if k else v, "dp", axis=0, tiled=True)
        ffn_w.append(v.reshape(dp, 3, wide, slice_rows))
    mixed_all, middle, normed_two, wo = join(
        me_ref, mixed_in, wo_half, wo_other, x, gain_values[1:2]
    )

    n2_other = swap(normed_two, ("mq", "mr"), mp, near_bit)
    down, down_send, n2g, n2g_send, *ffn_terms = ffn(
        normed_two, n2_other, og_own, og_other, ffn_w
    )
    n2g_other = swap(n2g_send, ("mq", "mr"), mp, near_bit)
    terms = {}
    for k, term in zip(packs, ffn_terms):
        term = term if k else after(term, n2g_other)
        terms[k] = lax.psum_scatter(
            term.reshape(-1, slice_rows), "dp", scatter_dimension=0, tiled=True
        )

    split_out = split(
        core_ref,
        n2g,
        n2g_other,
        middle,
        og_own,
        gain_values[1:2],
        mixed_all,
        wo,
        mp,
        dp,
    )
    middle_grad, out_keep, out_send = split_out[:3]
    out_whole = out_keep.astype(f32) + swap(out_send, "dp", dp, 1).astype(f32)
    out_kept, out_sent = halve(out_whole, 2)
    go_in = trade(list(split_out[3:]))
    go_in = jnp.stack(go_in[:1] + [after(v, out_sent) for v in go_in[1:]])
    go = jnp.concatenate(
        [lax.dynamic_index_in_dim(go_in, here ^ m, 0, keepdims=False) for m in range(mp)], axis=0
    )
    go, down_send, out_sent = lax.optimization_barrier((go, down_send, out_sent))
    down_other = swap(down_send, ("mq", "mr"), mp, near_bit)
    out_other = swap(out_sent, "dp", dp, 2)
    go = go.reshape(rows, mp * part, width)
    halves = 2 if width % 256 == 0 else 1
    back = functools.partial(attention_backward, qkv, spans, labr, labc, bias_tables)
    dqkv, tg = zip(back(go, ot, lse, 0, halves))
    far_sums = {k: v for k, v in terms.items() if k}
    if halves == 2:
        go = after(go, dqkv[0], down_other, out_other, *far_sums.values())
        second = back(go, ot, lse, 1, halves)
        dqkv, tg = dqkv + second[:1], tg + second[1:]
    w_grad = {0: terms[0], **far_sums}
    for b in reversed(all_bits[:-1]):
        for k in [k for k in w_grad if k and not k & b and k | b in w_grad]:
            w_grad[k] = w_grad[k].astype(f32) + swap(
                w_grad.pop(k | b).astype(bf16), ("mq", "mr"), mp, b
            ).astype(f32)
    far_other = [
        swap(v.astype(bf16), ("mq", "mr"), mp, k) for k, v in w_grad.items() if k
    ]
    dqkv = lax.optimization_barrier(tuple(dqkv) + (down_other, out_other) + tuple(far_other))
    far_other = dqkv[halves + 2 :]
    dqkv = [v.reshape(mp * part, -1) for v in dqkv[:halves]]
    parts = finish(here_ref, dqkv, wqkv, mp)
    tg = jnp.sum(jnp.stack(tg), axis=1).reshape(halves, 3, heads // halves, 128)
    tg = jnp.swapaxes(tg, 0, 1).reshape(3 * heads, 128)
    own_terms, last_terms = scatter_begin(dict(enumerate(parts)), mp, all_bits)
    qkv_keep, qkv_send = weight_term(
        core_ref, [after(v, parts[-1]) for v in dqkv], normed_one, tg, dp
    )
    qkv_send, last_terms[-1] = lax.optimization_barrier((qkv_send, last_terms[-1]))
    last_send = sum(v.astype(f32) for v in last_terms).astype(bf16)
    qkv_other = after(swap(qkv_send, "dp", dp, 1), last_send)
    qkv_whole = qkv_keep.astype(f32) + qkv_other.astype(f32)
    out_whole = out_kept.astype(f32) + after(out_other, qkv_whole).astype(f32)
    out_sum = scatter_dp(*halve(out_whole, 4), dp, 4)
    last = swap(last_send, ("mq", "mr"), mp, all_bits[0])
    qkv_kept, qkv_sent = halve(qkv_whole, 2)
    qkv_sum = scatter_dp(qkv_kept, qkv_sent, dp, 2)
    qkv_sum, own_sum = lax.optimization_barrier((qkv_sum, terms[0]))
    table_sum = qkv_sum[slice_rows : slice_rows + 3 * heads, : NB // dp]
    qkv_sum = qkv_sum[:slice_rows]
    out = (middle + down + after(down_other, last_send).astype(f32)).astype(bf16)
    qkv_out = jnp.stack([qkv_sum[:, c * width : (c + 1) * width] for c in range(3)])
    w_grad = own_sum.astype(f32) + sum(v.astype(f32) for v in far_other)
    w_grad = lax.optimization_barrier(w_grad.reshape(3, wide, slice_rows))
    gate_up_out = jnp.swapaxes(w_grad[:2], 1, 2)
    down_out = w_grad[2]
    table_out = jnp.swapaxes(table_sum.reshape(3, heads, NB // dp), 1, 2)

    own_gains = lax.dynamic_slice_in_dim(gain_values, me * slice_rows, slice_rows, 1)
    products = jnp.stack(
        [
            jnp.sum(qkv_sum * wqkv_own.astype(f32), axis=1),
            jnp.sum(gate_up_out * w_gate_up.astype(f32), axis=(0, 2)),
        ]
    )
    products = (products / own_gains).reshape(2, mp, slice_rows // mp)
    products = jnp.stack(
        [lax.dynamic_index_in_dim(products, here ^ k, 1, keepdims=False) for k in range(mp)], axis=1
    )
    products = jnp.pad(products, ((0, 14), (0, 0), (0, width - slice_rows // mp)))
    sums = jnp.concatenate([out_sum, products.reshape(16, mp * width)], axis=0).astype(bf16)
    sums = trade([sums[:, k * width : (k + 1) * width] for k in range(mp)])
    sums = sum(v.astype(f32) for v in sums)
    sums, last = lax.optimization_barrier((sums, last))
    n1g = sum(v.astype(f32) for v in own_terms + [last])
    a = n1g * gain_values[0:1]
    input_grad = (
        middle_grad
        + scale_one * a
        - wide_x
        * (scale_one * scale_one * scale_one)
        * jnp.mean(a * wide_x, axis=1, keepdims=True)
    ).astype(bf16)
    out_out = sums[:slice_rows].T
    gain_out = sums[slice_rows : slice_rows + 2, : slice_rows // mp]
    shape = inputs.shape
    return (
        out.reshape(shape),
        input_grad.reshape(shape),
        qkv_out,
        out_out,
        gate_up_out,
        down_out,
        table_out,
        gain_out,
    )


def solution(mesh):
    dp, mp = mesh.shape["dp"], mesh.shape["mp"]
    split_mesh = jax.sharding.Mesh(mesh.devices.reshape(dp, mp // 2, 2), ("dp", "mq", "mr"))
    both = ("mq", "mr")
    placed = (
        P("dp", both, None),
        P("dp", None),
        P("dp", None),
        P(None, "dp", None),
        P("dp", None),
        P(None, "dp", both),
        P(both, "dp"),
        P(None, "dp", both),
        P(both, "dp"),
        P(None, None, both),
        P(),
        P("dp", both, None),
    )
    return jax.shard_map(
        functools.partial(on_device, dp, mp),
        mesh=split_mesh,
        in_specs=placed,
        out_specs=(
            P("dp", both, None),
            P("dp", both, None),
            P(None, "dp", both),
            P(both, "dp"),
            P(None, "dp", both),
            P(both, "dp"),
            P(None, "dp", both),
            P(None, ("dp", "mq", "mr")),
        ),
        check_vma=False,
    )
```
